32 devices in a mesh: groups: 2 (over x), tm: 16 (over z, y, core).
Axes of the slice: x: 2, y: 2, z: 4, core: 2. Of those that a mesh axis runs over, the one named last changes fastest.
Arguments:
- tokens: bfloat16 [8192, 1024], P(('groups', 'tm')), parts along dimension 0, may hold values from -16 to 16
- log_decay: float32 [8, 8192], P(None, ('groups', 'tm')), parts along dimension 1, may hold values from -1.5 to 0
- mem_index: int32 [64, 8], P(('groups', 'tm')), parts along dimension 0, may hold values from 0 to 29, as said below
- mem_count: int32 [64], P(('groups', 'tm')), parts along dimension 0, may hold values from 0 to 8
- w_rq: bfloat16 [1024, 512], replicated, may hold values from -0.1875 to 0.1875
- w_rk: bfloat16 [1024, 512], replicated, may hold values from -0.1875 to 0.1875
- w_rv: bfloat16 [1024, 1024], replicated, may hold values from -0.1875 to 0.1875
- norm_gain: float32 [1024], replicated, may hold values from 0.5 to 1.5
- w_mq: bfloat16 [1024, 512], replicated, may hold values from -1 to 1
- w_mk: bfloat16 [1024, 512], replicated, may hold values from -1 to 1
- w_mv: bfloat16 [1024, 512], replicated, may hold values from -0.1875 to 0.1875
- w_out: bfloat16 [512, 1024], replicated, may hold values from -0.25 to 0.25
Outputs:
- layer_out: bfloat16 [8192, 1024], P(('groups', 'tm')), parts along dimension 0
The draws below stay inside these ranges and needn't reach their ends.
There are 2 independent parts, one for each index of `groups`. The reference program is written for one: setup_inputs(seed, part) draws one part's arguments, and reference() takes and returns one part's arrays. A program takes and returns all parts, laid end to end along the dimension named above; an argument that names none is the same for every part. Nothing has to cross between parts.
Inputs may be any that keep to these rules, and one draw needn't show every extreme that they name: `mem_index`: entries i < mem_count[f] of frame f's list are distinct frames held by lower indices of tm than frame f's own; all the live entries of the 2 frames of one index of tm name at most one frame of any other index.
All inputs are finite; a program needn't handle non-finite values.
Results may differ from the reference program's by a relative error of at most 0.04.
Values may be sent and summed in bfloat16 or wider, within the bound.
No kernel may reach another device: no remote copies, remote signals or barrier semaphores. Data moves between devices by JAX's collectives and lax.ppermute only.
A program may use at most 128 MiB of HBM per device.

```python
import math
import jax
import jax.numpy as jnp
from jax import lax

D = 1024
H = 8
DK = 64
DV = 128
MH = 4
MD = 128
MC = 512
P_SIZE = 128
BLK = 64
MEM = 8
FR_DEV = 2
FRAMES = 32
TOKENS = 4096


def draw_tokens(key, part):
    first = jax.random.fold_in(key, 0)
    base = jax.random.normal(first, (TOKENS, D), jnp.float32)
    return jnp.clip(base, -6.0, 6.0).astype(jnp.bfloat16)


def draw_log_decay(key, part):
    temporal_carry_handoff = FRAMES * BLK
    keys = jax.random.split(key, 8)
    frame_factor = jnp.exp(jax.random.uniform(keys[0], (H, 2, FRAMES, 1), jnp.float32, math.log(0.35), math.log(2.8)))
    token_factor = jnp.exp(jax.random.uniform(keys[1], (H, 2, FRAMES, BLK), jnp.float32, math.log(0.7), math.log(1.4)))
    weight_tensors = (frame_factor * token_factor).reshape(H, 2, temporal_carry_handoff)
    order = jax.random.permutation(keys[2], H)
    rank = jnp.zeros((H,), jnp.int32).at[order].set(jnp.arange(H, dtype=jnp.int32))
    fast_count = jax.random.randint(keys[3], (), 2, 6)
    fast = rank < fast_count
    target = jax.random.uniform(keys[4], (H, 1, 1), jnp.float32, 0.05, 0.5)
    span = jax.random.uniform(keys[5], (H, 1, 1), jnp.float32, 30.0, 50.0)
    slow_rate = target * weight_tensors / jnp.sum(weight_tensors, axis=-1, keepdims=True)
    fast_rate = weight_tensors / jnp.mean(weight_tensors, axis=-1, keepdims=True) / span
    forgetting_rate = jnp.where(fast[:, None, None], fast_rate, slow_rate)
    image_patch_regions = jax.random.randint(keys[6], (3,), 0, temporal_carry_handoff)
    contiguous_span_extent = jnp.any(jnp.arange(temporal_carry_handoff)[None, :] == image_patch_regions[:, None], axis=0)
    kept_memory_images = jax.random.uniform(keys[7], (H, 1, 1), jnp.float32, 0.5, 0.8)
    overall_total_aggregate = -(forgetting_rate + jnp.where(contiguous_span_extent[None, None, :], -jnp.log(kept_memory_images), 0.0))
    return overall_total_aggregate.reshape(H, 2, FRAMES, BLK).transpose(0, 2, 1, 3).reshape(H, TOKENS)


def memory_tables(key):
    key = jax.random.fold_in(key, 7)
    keys = jax.random.split(key, 5)
    owners = FRAMES // FR_DEV
    frame_ids = jnp.arange(FRAMES, dtype=jnp.int32)
    device_of = frame_ids // FR_DEV
    pick = jax.random.randint(keys[0], (owners, owners), 0, FR_DEV)
    pick = pick.at[owners - 1, owners - 2].set(FR_DEV - 1)
    pick = pick.at[1, 0].set(0)
    offset = jax.random.randint(keys[1], (owners,), 0, 1048576)
    last_offset = (owners - 2 - (FR_DEV - 1) * MEM) % (owners - 1)
    offset = offset.at[owners - 1].set(last_offset)
    slots = jnp.arange(MEM, dtype=jnp.int32)
    position = offset[device_of][:, None] + (frame_ids % FR_DEV)[:, None] * MEM + slots[None, :]
    chosen = position % jnp.maximum(device_of, 1)[:, None]
    busy = jax.random.randint(keys[3], (owners,), MEM - 1, MEM + 1)
    raw = jax.random.randint(keys[4], (FRAMES,), 0, 2)
    counts = jnp.maximum(busy[device_of] - raw, 0)
    counts = jnp.minimum(counts, device_of)
    counts = jnp.where(frame_ids == FRAMES - 1, MEM, counts)
    index = chosen * FR_DEV + pick[device_of[:, None], chosen]
    return (index.astype(jnp.int32), counts.astype(jnp.int32))


def draw_mem_index(key, part):
    index, counts = memory_tables(key)
    return index


def draw_mem_count(key, part):
    index, counts = memory_tables(key)
    return counts


def memory_pair(key):
    key = jax.random.fold_in(key, 11)
    first_key, second_key = jax.random.split(key)
    first = jax.random.normal(first_key, (D, MC), jnp.float32) * D ** (-0.5)
    other = jax.random.normal(second_key, (D, MC), jnp.float32) * D ** (-0.5)
    second = other
    return (first, second)


def draw_w_mq(key, part):
    first, second = memory_pair(key)
    return first.astype(jnp.bfloat16)


def draw_w_mk(key, part):
    first, second = memory_pair(key)
    return second.astype(jnp.bfloat16)


def scatter_about(stream_key, shape, scale, bound, held_as=jnp.bfloat16):
    values = scale * jax.random.normal(stream_key, shape, jnp.float32)
    return jnp.clip(values, min=-bound, max=bound).astype(held_as)


def setup_inputs(seed: int = 0, part: int = 0) -> dict:
    key_of = jax.random.split(jax.random.key(seed), 13)
    part_splits = jax.random.split(jax.random.fold_in(key_of[12], part), 13)
    return {
        "tokens": draw_tokens(jax.random.fold_in(jax.random.fold_in(key_of[12], part), 71), part),
        "log_decay": draw_log_decay(jax.random.fold_in(jax.random.fold_in(key_of[12], part), 71), part),
        "mem_index": draw_mem_index(jax.random.fold_in(jax.random.fold_in(key_of[12], part), 71), part),
        "mem_count": draw_mem_count(jax.random.fold_in(jax.random.fold_in(key_of[12], part), 71), part),
        "w_rq": scatter_about(key_of[4], (D, H * DK), D ** -0.5, 0.1875),
        "w_rk": scatter_about(key_of[5], (D, H * DK), D ** -0.5, 0.1875),
        "w_rv": scatter_about(key_of[6], (D, H * DV), D ** -0.5, 0.1875),
        "norm_gain": jnp.clip(jax.random.uniform(key_of[7], (H * DV,), jnp.float32, 0.5, 1.5), 0.5, 1.5),
        "w_mq": draw_w_mq(jax.random.fold_in(key_of[12], 71), part),
        "w_mk": draw_w_mk(jax.random.fold_in(key_of[12], 71), part),
        "w_mv": scatter_about(key_of[10], (D, MC), D ** -0.5, 0.1875),
        "w_out": scatter_about(key_of[11], (MC, D), MC ** -0.5, 0.25),
    }


HIGHEST = lax.Precision.HIGHEST

def dilation_stride(queries, keys_rec, values_rec, decays, state):
    cumulated = jnp.cumsum(decays, axis=-1)
    length = decays.shape[-1]
    lower = jnp.arange(length)[:, None] >= jnp.arange(length)[None, :]
    gaps = cumulated[..., :, None] - cumulated[..., None, :]
    weight_tensors = jnp.where(lower, jnp.exp(jnp.where(lower, gaps, 0.0)), 0.0)
    scores = jnp.einsum('bhtd,bhsd->bhts', queries, keys_rec, precision=HIGHEST) * weight_tensors
    inner = jnp.einsum('bhts,bhsv->bhtv', scores, values_rec, precision=HIGHEST)
    carried = jnp.exp(cumulated)[..., None] * jnp.einsum('bhtd,bhdv->bhtv', queries, state, precision=HIGHEST)
    tail_decay = jnp.exp(cumulated[..., -1:] - cumulated)
    new_state = jnp.exp(cumulated[..., -1])[..., None, None] * state + jnp.einsum('bhsd,bhsv->bhdv', keys_rec * tail_decay[..., None], values_rec, precision=HIGHEST)
    return (inner + carried, new_state, cumulated)

def reference(tokens, log_decay, mem_index, mem_count, w_rq, w_rk, w_rv, norm_gain, w_mq, w_mk, w_mv, w_out):

    def project(weight):
        return jnp.dot(tokens, weight, preferred_element_type=jnp.float32).astype(jnp.bfloat16)

    def heads(values, width):
        return values.astype(jnp.float32).reshape(FRAMES, 2, BLK, H, width).transpose(0, 1, 3, 2, 4)
    queries = heads(project(w_rq), DK) * DK ** (-0.5)
    keys_rec = heads(project(w_rk), DK)
    values_rec = heads(project(w_rv), DV)
    decays = log_decay.reshape(H, FRAMES, 2, BLK).transpose(1, 2, 0, 3)

    def advance(state, inputs):
        frame_q, frame_k, frame_v, frame_d = inputs
        output, new_state, cumulated = dilation_stride(frame_q, frame_k, frame_v, frame_d, state)
        return (new_state, output)
    start = jnp.zeros((2, H, DK, DV), jnp.float32)
    final_state, outputs = lax.scan(advance, start, (queries, keys_rec, values_rec, decays))
    scale = lax.rsqrt(lax.optimization_barrier(jnp.mean(outputs * outputs, axis=-1, keepdims=True)) + 1e-05)
    normed = (outputs * scale).transpose(0, 1, 3, 2, 4).reshape(TOKENS, H * DV) * norm_gain
    hidden = (tokens.astype(jnp.float32) + normed).astype(jnp.bfloat16)

    def mem_project(weight):
        return jnp.dot(hidden, weight, preferred_element_type=jnp.float32).astype(jnp.bfloat16).reshape(FRAMES, P_SIZE, MC)
    mem_q = mem_project(w_mq)
    mem_k = mem_project(w_mk)
    mem_v = mem_project(w_mv)
    slot_of = jnp.arange((MEM + 1) * P_SIZE, dtype=jnp.int32) // P_SIZE

    def attend(frame):
        chosen = mem_index[frame]
        count = mem_count[frame]
        keys_all = jnp.concatenate([mem_k[frame][None], jnp.take(mem_k, chosen, axis=0)], axis=0)
        keys_all = keys_all.reshape((MEM + 1) * P_SIZE, MH, MD).astype(jnp.float32)
        values_all = jnp.concatenate([mem_v[frame][None], jnp.take(mem_v, chosen, axis=0)], axis=0)
        values_all = values_all.reshape((MEM + 1) * P_SIZE, MH, MD).astype(jnp.float32)
        query_rows = mem_q[frame].reshape(P_SIZE, MH, MD).astype(jnp.float32)
        scores = jnp.einsum('qhd,khd->hqk', query_rows, keys_all, precision=HIGHEST) * MD ** (-0.5)
        live = (slot_of == 0) | (slot_of - 1 < count)
        scores = jnp.where(live[None, None, :], scores, -1e+30)
        peak = lax.optimization_barrier(jnp.max(scores, axis=-1, keepdims=True))
        expo = jnp.exp(scores - peak)
        probs = (expo / lax.optimization_barrier(jnp.sum(expo, axis=-1, keepdims=True))).astype(jnp.bfloat16)
        mixed = jnp.einsum('hqk,khd->qhd', probs.astype(jnp.float32), values_all, precision=HIGHEST)
        return mixed.reshape(P_SIZE, MC).astype(jnp.bfloat16)
    attended = lax.map(attend, jnp.arange(FRAMES, dtype=jnp.int32)).reshape(TOKENS, MC)
    projected = jnp.dot(attended, w_out, preferred_element_type=jnp.float32)
    return (hidden.astype(jnp.float32) + projected).astype(jnp.bfloat16)
```

```python
import functools

import jax
import jax.numpy as jnp
from jax import lax
from jax.experimental import pallas as pl
from jax.experimental.pallas import tpu as pltpu
from jax.sharding import PartitionSpec as P

H = 8
DK = 64
DV = 128
MH = 4
MD = 128
MC = 512
P_SIZE = 128
BLK = 64
LANES = 4
HC = H // LANES
ROWS = HC * 2 * DK
TAIL = 16
PAIRS = HC * 2
NEG = -1e30
F32 = jnp.float32
BF16 = jnp.bfloat16


VMEM = pl.BlockSpec(memory_space=pltpu.VMEM)
SMEM = pl.BlockSpec(memory_space=pltpu.SMEM)
ANY = pl.BlockSpec(memory_space=pl.ANY)


def params(mib=48):
    return pltpu.CompilerParams(vmem_limit_bytes=mib << 20)


def cost(flops, nbytes):
    return pl.CostEstimate(flops=flops, bytes_accessed=nbytes, transcendentals=0)


def chain_of(iota):
    return (iota // BLK) % 2


def nn(a, b, **kw):
    return lax.dot_general(a, b, (((1,), (0,)), ((), ())), preferred_element_type=F32, **kw)


def nt(a, b, **kw):
    return lax.dot_general(a, b, (((1,), (1,)), ((), ())), preferred_element_type=F32, **kw)


def tn(a, b, **kw):
    return lax.dot_general(a, b, (((0,), (0,)), ((), ())), preferred_element_type=F32, **kw)


def by_chain(x):
    rows = x.shape[0]
    chain = chain_of(lax.broadcasted_iota(jnp.int32, (rows, DK), 0))
    zero = jnp.zeros_like(x)
    return jnp.concatenate([jnp.where(chain == 0, x, zero), jnp.where(chain == 1, x, zero)], axis=1)


def split3(x):
    hi = x.astype(BF16)
    rest = x - hi.astype(F32)
    mid = rest.astype(BF16)
    return hi, mid, (rest - mid.astype(F32)).astype(BF16)


def read_message(x):
    state = x[:ROWS].astype(F32)
    tail = x[ROWS:].astype(F32)
    total = tail[0:PAIRS] + tail[PAIRS : 2 * PAIRS] + tail[2 * PAIRS : 3 * PAIRS]
    return state, total


def spread(total):
    return jnp.concatenate(
        [jnp.broadcast_to(total[p : p + 1], (DK, total.shape[1])) for p in range(PAIRS)], axis=0
    )


def write_message(ref, state, total):
    ref[:ROWS, :] = state.astype(BF16)
    hi, mid, lo = split3(total)
    pad = jnp.zeros((TAIL - 3 * PAIRS, total.shape[1]), F32)
    ref[ROWS:, :] = jnp.concatenate(
        [hi.astype(F32), mid.astype(F32), lo.astype(F32), pad], axis=0
    ).astype(BF16)


def local_kernel(x_ref, wk_ref, wv_ref, ld_ref, k_ref, v_ref, *rest):
    outs, chunks = rest[:LANES], rest[LANES]
    step = pl.program_id(0)
    rows = x_ref.shape[0]
    x = x_ref[...]
    k = nn(x, wk_ref[...]).astype(BF16)
    v = nn(x, wv_ref[...]).astype(BF16)
    k_ref[...] = k
    v_ref[...] = v
    ld = ld_ref[0]
    t = lax.broadcasted_iota(jnp.int32, (rows, rows), 0)
    s = lax.broadcasted_iota(jnp.int32, (rows, rows), 1)
    after = ((s > t) & (chain_of(s) == chain_of(t))).astype(F32)
    tail = jnp.exp(nt(after, ld, precision=lax.Precision.HIGHEST))
    states, totals = [], []
    chain = chain_of(lax.broadcasted_iota(jnp.int32, ld.shape, 1))
    sums = [jnp.sum(jnp.where(chain == b, ld, 0.0), axis=1, keepdims=True) for b in (0, 1)]
    for h in range(HC):
        kt = (k[:, h * DK : (h + 1) * DK].astype(F32) * tail[:, h : h + 1]).astype(BF16)
        states.append(tn(by_chain(kt), v[:, h * DV : (h + 1) * DV]))
        totals += [jnp.broadcast_to(sums[b][h : h + 1], (1, DV)) for b in (0, 1)]
    write_message(
        chunks.at[step], jnp.concatenate(states, axis=0), jnp.concatenate(totals, axis=0)
    )

    @pl.when(step == LANES - 1)
    def _():
        lane = lax.rem(lax.axis_index("tm"), LANES)
        for f in range(LANES):
            outs[f][...] = chunks[lane ^ f]


def local(tokens, w_rk, w_rv, ld):
    rows, d = tokens.shape
    whole = lambda q: (0, 0)
    message = jax.ShapeDtypeStruct((ROWS + TAIL, DV), BF16)
    return pl.pallas_call(
        local_kernel,
        grid=(LANES,),
        in_specs=[
            pl.BlockSpec((rows, d), whole),
            pl.BlockSpec((d, HC * DK), lambda q: (0, q)),
            pl.BlockSpec((d, HC * DV), lambda q: (0, q)),
            pl.BlockSpec((1, HC, rows), lambda q: (q, 0, 0)),
        ],
        out_specs=[
            pl.BlockSpec((rows, HC * DK), lambda q: (0, q)),
            pl.BlockSpec((rows, HC * DV), lambda q: (0, q)),
        ]
        + [pl.BlockSpec((ROWS + TAIL, DV), whole)] * LANES,
        out_shape=[
            jax.ShapeDtypeStruct((rows, H * DK), BF16),
            jax.ShapeDtypeStruct((rows, H * DV), BF16),
        ]
        + [message] * LANES,
        scratch_shapes=[pltpu.VMEM((LANES, ROWS + TAIL, DV), BF16)],
        compiler_params=params(),
        name="local",
    )(tokens, w_rk, w_rv, ld.reshape(LANES, HC, rows))


def inner_kernel(x_ref, wq_ref, k_ref, v_ref, ld_ref, inner_ref, qq_ref):
    rows = x_ref.shape[0]
    q = nn(x_ref[...], wq_ref[...]).astype(BF16)
    ld = ld_ref[0]
    t = lax.broadcasted_iota(jnp.int32, (rows, rows), 0)
    s = lax.broadcasted_iota(jnp.int32, (rows, rows), 1)
    upto = (s <= t) & (chain_of(s) == chain_of(t))
    ones = upto.astype(F32)
    column = nt(ones, ld, precision=lax.Precision.HIGHEST)
    row = nt(ld, ones, precision=lax.Precision.HIGHEST)
    for h in range(HC):
        qh = q[:, h * DK : (h + 1) * DK]
        gap = column[:, h : h + 1] - row[h : h + 1, :]
        weight = jnp.exp(jnp.where(upto, gap, NEG)) * DK**-0.5
        scores = nt(qh, k_ref[:, h * DK : (h + 1) * DK]) * weight
        inner_ref[:, h * DV : (h + 1) * DV] = nn(
            scores.astype(BF16), v_ref[:, h * DV : (h + 1) * DV]
        )
        scaled = qh.astype(F32) * (jnp.exp(column[:, h : h + 1]) * DK**-0.5)
        qq_ref[:, h * 2 * DK : (h + 1) * 2 * DK] = by_chain(scaled.astype(BF16))


def inner(tokens, w_rq, k, v, ld):
    rows, d = tokens.shape
    return pl.pallas_call(
        inner_kernel,
        grid=(LANES,),
        in_specs=[
            pl.BlockSpec((rows, d), lambda q: (0, 0)),
            pl.BlockSpec((d, HC * DK), lambda q: (0, q)),
            pl.BlockSpec((rows, HC * DK), lambda q: (0, q)),
            pl.BlockSpec((rows, HC * DV), lambda q: (0, q)),
            pl.BlockSpec((1, HC, rows), lambda q: (q, 0, 0)),
        ],
        out_specs=[
            pl.BlockSpec((rows, HC * DV), lambda q: (0, q)),
            pl.BlockSpec((rows, HC * 2 * DK), lambda q: (0, q)),
        ],
        out_shape=[
            jax.ShapeDtypeStruct((rows, H * DV), F32),
            jax.ShapeDtypeStruct((rows, H * 2 * DK), BF16),
        ],
        compiler_params=params(),
        cost_estimate=cost(2 * rows * d * H * DK, 6 << 20),
        name="inner",
    )(tokens, w_rq, k, v, ld.reshape(LANES, HC, rows))


def plane_kernel(*refs):
    parts, out, ordered = refs[:LANES], refs[LANES], refs[LANES + 1]
    lane = lax.rem(lax.axis_index("tm"), LANES)
    for f in range(LANES):
        ordered[lane ^ f] = parts[f][...]
    state, total = read_message(ordered[0])
    for i in range(1, LANES):
        mine, decay = read_message(ordered[i])
        state = spread(jnp.exp(decay)) * state + mine
        total = total + decay
    write_message(out, state, total)


def plane_total(parts):
    return pl.pallas_call(
        plane_kernel,
        in_specs=[VMEM] * LANES,
        out_specs=VMEM,
        out_shape=jax.ShapeDtypeStruct((ROWS + TAIL, DV), BF16),
        scratch_shapes=[pltpu.VMEM((LANES, ROWS + TAIL, DV), BF16)],
        compiler_params=params(),
        name="plane",
    )(*parts)


def prefix_kernel(count, *refs):
    parts, earlier = refs[:LANES], refs[LANES : LANES + count]
    outs = refs[LANES + count : 2 * LANES + count]
    ordered, results = refs[2 * LANES + count :]
    lane = lax.rem(lax.axis_index("tm"), LANES)
    for f in range(LANES):
        ordered[lane ^ f] = parts[f][...]
    state = jnp.zeros((ROWS, DV), F32)
    for ref in reversed(earlier):
        mine, decay = read_message(ref[...])
        state = spread(jnp.exp(decay)) * state + mine
    for i in range(LANES):
        results[i] = state.astype(BF16)
        if i + 1 < LANES:
            mine, decay = read_message(ordered[i])
            state = spread(jnp.exp(decay)) * state + mine
    for f in range(LANES):
        outs[f][...] = results[lane ^ f]


def prefix(parts, earlier):
    return pl.pallas_call(
        functools.partial(prefix_kernel, len(earlier)),
        in_specs=[VMEM] * (LANES + len(earlier)),
        out_specs=[VMEM] * LANES,
        out_shape=[jax.ShapeDtypeStruct((ROWS, DV), BF16)] * LANES,
        scratch_shapes=[
            pltpu.VMEM((LANES, ROWS + TAIL, DV), BF16),
            pltpu.VMEM((LANES, ROWS, DV), BF16),
        ],
        compiler_params=params(),
        name="prefix",
    )(*parts, *earlier)


def hidden_kernel(frames, *refs):
    inner_ref, qq_ref = refs[:2]
    states = refs[2 : 2 + LANES]
    x_ref, gain_ref, wq, wk, wv = refs[2 + LANES : 7 + LANES]
    hid_ref, q_ref = refs[7 + LANES : 9 + LANES]
    kv_refs = refs[9 + LANES : 9 + LANES + frames]
    ordered, bq, bk, bv, sems = refs[9 + LANES + frames :]
    copies = [
        pltpu.make_async_copy(src, dst, sems.at[i])
        for i, (src, dst) in enumerate(((wq, bq), (wk, bk), (wv, bv)))
    ]
    for copy in copies:
        copy.start()
    lane = lax.rem(lax.axis_index("tm"), LANES)
    for f in range(LANES):
        ordered[lane ^ f] = states[f][...]
    for h in range(H):
        cols = slice(h * DV, (h + 1) * DV)
        state = ordered[h // HC, (h % HC) * 2 * DK : (h % HC + 1) * 2 * DK, :]
        o = inner_ref[:, cols] + nn(qq_ref[:, h * 2 * DK : (h + 1) * 2 * DK], state)
        scale = lax.rsqrt(jnp.mean(o * o, axis=1, keepdims=True) + 1e-05)
        y = o * scale * gain_ref[:, cols]
        hid_ref[:, cols] = (x_ref[:, cols].astype(F32) + y).astype(BF16)
    hid = hid_ref[...]
    copies[0].wait()
    q_ref[...] = nn(hid, bq[...]).astype(BF16)
    for i, buf in ((1, bk), (2, bv)):
        copies[i].wait()
        part = nn(hid, buf[...]).astype(BF16)
        for f in range(frames):
            kv_refs[f][:, (i - 1) * MC : i * MC] = part[f * P_SIZE : (f + 1) * P_SIZE]


def hidden_of(inner_out, qq, states, tokens, gain, w_mq, w_mk, w_mv):
    rows, d = tokens.shape
    frames = rows // P_SIZE
    return pl.pallas_call(
        functools.partial(hidden_kernel, frames),
        in_specs=[VMEM] * (LANES + 4) + [ANY] * 3,
        out_specs=[VMEM] * (2 + frames),
        out_shape=[
            jax.ShapeDtypeStruct((rows, d), BF16),
            jax.ShapeDtypeStruct((rows, MC), BF16),
        ]
        + [jax.ShapeDtypeStruct((P_SIZE, 2 * MC), BF16)] * frames,
        scratch_shapes=[pltpu.VMEM((LANES, ROWS, DV), BF16)]
        + [pltpu.VMEM((d, MC), BF16)] * 3
        + [pltpu.SemaphoreType.DMA((3,))],
        compiler_params=params(),
        name="hidden",
    )(inner_out, qq, *states, tokens, gain.reshape(1, d), w_mq, w_mk, w_mv)


def attend_kernel(frames, blocks, *refs):
    idx_ref, cnt_ref, pidx_ref, pcnt_ref, q_ref, pq_ref = refs[:6]
    kv_refs = refs[6 : 6 + blocks]
    o_ref, po_ref, lse_ref, plse_ref = refs[6 + blocks : 10 + blocks]
    kv, scores, peak, total, acc, lse, table, counts, need, sems = refs[10 + blocks :]
    slots = idx_ref.shape[1]
    me = lax.axis_index("tm")
    lane = lax.rem(me, LANES)
    plane = me // LANES

    def clear(b, _):
        need[b] = (b < frames).astype(jnp.int32)
        return 0

    lse[...] = jnp.zeros_like(lse)
    lax.fori_loop(0, blocks, clear, 0)
    for g, (index, live) in enumerate(((idx_ref, cnt_ref), (pidx_ref, pcnt_ref))):
        for f in range(frames):
            row = g * frames + f
            if g == 0:
                table[row, 0] = f

            def visit(i, n, index=index, f=f, row=row):
                frame = index[f, i]
                owner = frame // frames
                its = lax.rem(owner, LANES)
                here = (its // 2) == (lane // 2)
                block = ((plane - owner // LANES) * 2 + ((its ^ lane) & 1)) * frames
                block = block + lax.rem(frame, frames)

                @pl.when(here)
                def _():
                    table[row, n] = block
                    need[block] = 1

                return n + here.astype(jnp.int32)

            counts[row] = lax.fori_loop(
                0, jnp.minimum(live[f], slots), visit, jnp.int32(1 if g == 0 else 0)
            )
    for b in range(blocks):

        @pl.when(need[b] == 1)
        def _(b=b):
            pltpu.make_async_copy(kv_refs[b], kv.at[b], sems.at[b]).start()

    for b in range(blocks):

        @pl.when(need[b] == 1)
        def _(b=b):
            pltpu.make_async_copy(kv_refs[b], kv.at[b], sems.at[b]).wait()

    for row in range(2 * frames):
        queries, out, stats = (q_ref, o_ref, lse_ref) if row < frames else (pq_ref, po_ref, plse_ref)
        f = row % frames
        span = slice(f * P_SIZE, (f + 1) * P_SIZE)
        n = counts[row]
        peak[...] = jnp.full_like(peak, NEG)
        total[...] = jnp.zeros_like(total)
        acc[...] = jnp.zeros_like(acc)

        def score(i, _, queries=queries, span=span, row=row):
            b = table[row, i]
            for e in range(MH):
                cols = slice(e * MD, (e + 1) * MD)
                s = nt(queries[span, cols], kv[b, :, cols]) * MD**-0.5
                scores[i, e] = s
                peak[e] = jnp.maximum(peak[e], s)
            return 0

        lax.fori_loop(0, n, score, 0)
        tops = [jnp.max(peak[e], axis=1, keepdims=True) for e in range(MH)]
        for e in range(MH):
            peak[e] = jnp.broadcast_to(tops[e], (P_SIZE, P_SIZE))

        def weigh(i, _, row=row):
            b = table[row, i]
            for e in range(MH):
                p = jnp.exp(scores[i, e] - peak[e])
                total[e] += p
                acc[e] += nn(p.astype(BF16), kv[b, :, MC + e * MD : MC + (e + 1) * MD])
            return 0

        lax.fori_loop(0, n, weigh, 0)
        for e in range(MH):
            l = jnp.maximum(jnp.sum(total[e], axis=1, keepdims=True), 1e-30)
            out[span, e * MD : (e + 1) * MD] = (acc[e] / l).astype(out.dtype)
            lse[:, e : e + 1] = tops[e] + jnp.log(l)
        stats[:, span] = jnp.transpose(lse[...])[:8]


def attend(index, live, pindex, plive, q, pq, kvs, frames):
    rows = q.shape[0]
    blocks = len(kvs)
    slots = index.shape[1]
    return pl.pallas_call(
        functools.partial(attend_kernel, frames, blocks),
        in_specs=[SMEM] * 4 + [VMEM] * 2 + [ANY] * blocks,
        out_specs=[VMEM] * 4,
        out_shape=[
            jax.ShapeDtypeStruct((rows, MC), F32),
            jax.ShapeDtypeStruct((rows, MC), BF16),
            jax.ShapeDtypeStruct((8, rows), F32),
            jax.ShapeDtypeStruct((8, rows), F32),
        ],
        scratch_shapes=[
            pltpu.VMEM((blocks, P_SIZE, 2 * MC), BF16),
            pltpu.VMEM((slots + 1, MH, P_SIZE, P_SIZE), F32),
            pltpu.VMEM((MH, P_SIZE, P_SIZE), F32),
            pltpu.VMEM((MH, P_SIZE, P_SIZE), F32),
            pltpu.VMEM((MH, P_SIZE, MD), F32),
            pltpu.VMEM((P_SIZE, 128), F32),
            pltpu.SMEM((2 * frames, slots + 1), jnp.int32),
            pltpu.SMEM((2 * frames,), jnp.int32),
            pltpu.SMEM((blocks,), jnp.int32),
            pltpu.SemaphoreType.DMA((blocks,)),
        ],
        compiler_params=params(),
        name="attend",
    )(index, live, pindex, plive, q, pq, *kvs)


def output_kernel(o_ref, lse_ref, po_ref, plse_ref, hid_ref, w_ref, out_ref, mixed):
    rows = o_ref.shape[0]
    mine, other = lse_ref[...], plse_ref[...]
    top = jnp.maximum(mine, other)
    a, b = jnp.exp(mine - top), jnp.exp(other - top)
    inv = 1.0 / (a + b)
    both = jnp.concatenate([a * inv, b * inv, jnp.zeros((128 - 16, rows), F32)], axis=0)
    weights = jnp.transpose(both)
    for e in range(MH):
        cols = slice(e * MD, (e + 1) * MD)
        value = o_ref[:, cols] * weights[:, e : e + 1]
        value = value + po_ref[:, cols].astype(F32) * weights[:, 8 + e : 9 + e]
        mixed[:, cols] = value.astype(BF16)
    out_ref[...] = (hid_ref[...].astype(F32) + nn(mixed[...], w_ref[...])).astype(BF16)


def output(o, lse, po, plse, hid, w_out):
    rows, d = hid.shape
    return pl.pallas_call(
        output_kernel,
        in_specs=[VMEM] * 6,
        out_specs=VMEM,
        out_shape=jax.ShapeDtypeStruct((rows, d), BF16),
        scratch_shapes=[pltpu.VMEM((rows, MC), BF16)],
        compiler_params=params(),
        name="output",
    )(o, lse, po, plse, hid, w_out)


def on_device(
    tokens, log_decay, mem_index, mem_count, w_rq, w_rk, w_rv, norm_gain, w_mq, w_mk, w_mv, w_out
):
    size = lax.axis_size("tm")
    planes = size // LANES
    frames = tokens.shape[0] // P_SIZE

    def flip(x, bits):
        return lax.ppermute(x, "tm", [(i, i ^ bits) for i in range(size)])

    def up(x, distance):
        step = distance * LANES
        return lax.ppermute(x, "tm", [(i, i + step) for i in range(size - step)])

    partner_index, partner_count = flip(mem_index, 2), flip(mem_count, 2)
    k, v, *chunks = local(tokens, w_rk, w_rv, log_decay)
    parts = [chunks[0]] + [flip(chunks[f], f) for f in range(1, LANES)]
    inner_out, qq = inner(tokens, w_rq, k, v, log_decay)
    total = plane_total(parts)
    earlier = [up(total, distance) for distance in range(1, planes)]
    mine = prefix(parts, earlier)
    states = [mine[0]] + [flip(mine[f], f) for f in range(1, LANES)]
    hid, q, *kv = hidden_of(inner_out, qq, states, tokens, norm_gain, w_mq, w_mk, w_mv)
    partner_q = flip(q, 2)
    held = []
    for distance in range(planes):
        if distance:
            kv = [up(x, 1) for x in kv]
        held += kv + [flip(x, 1) for x in kv]
    o, po, lse, plse = attend(
        mem_index, mem_count, partner_index, partner_count, q, partner_q, held, frames
    )
    return output(o, lse, flip(po, 2), flip(plse, 2), hid, w_out)


def solution(mesh):
    placed = (
        P(("groups", "tm"), None),
        P(None, ("groups", "tm")),
        P(("groups", "tm"), None),
        P(("groups", "tm")),
        P(),
        P(),
        P(),
        P(),
        P(),
        P(),
        P(),
        P(),
    )
    return jax.shard_map(
        on_device, mesh=mesh, in_specs=placed, out_specs=P(("groups", "tm"), None), check_vma=False
    )
```

```python
import functools

import jax
import jax.numpy as jnp
from jax import lax
from jax.experimental import pallas as pl
from jax.experimental.pallas import tpu as pltpu
from jax.sharding import PartitionSpec as P


H = 8
DK = 64
DV = 128
MH = 4
MD = 128
MC = 512
P_SIZE = 128
BLK = 64
LANES = 4
HC = H // LANES
ROWS = HC * 2 * DK
TAIL = 16
PAIRS = HC * 2
NEG = -1e30
F32 = jnp.float32
BF16 = jnp.bfloat16


VMEM = pl.BlockSpec(memory_space=pltpu.VMEM)
SMEM = pl.BlockSpec(memory_space=pltpu.SMEM)
HBM = pl.BlockSpec(memory_space=pltpu.HBM)


def params(mib=48):
    return pltpu.CompilerParams(vmem_limit_bytes=mib << 20)


def cost(flops, nbytes):
    return pl.CostEstimate(flops=flops, bytes_accessed=nbytes, transcendentals=0)


def chain_of(iota):
    return (iota // BLK) % 2


def nn(a, b, **kw):
    return lax.dot_general(a, b, (((1,), (0,)), ((), ())), preferred_element_type=F32, **kw)


def nt(a, b, **kw):
    return lax.dot_general(a, b, (((1,), (1,)), ((), ())), preferred_element_type=F32, **kw)


def tn(a, b, **kw):
    return lax.dot_general(a, b, (((0,), (0,)), ((), ())), preferred_element_type=F32, **kw)


def by_chain(x):
    rows = x.shape[0]
    chain = chain_of(lax.broadcasted_iota(jnp.int32, (rows, DK), 0))
    zero = jnp.zeros_like(x)
    return jnp.concatenate([jnp.where(chain == 0, x, zero), jnp.where(chain == 1, x, zero)], axis=1)


def split3(x):
    hi = x.astype(BF16)
    rest = x - hi.astype(F32)
    mid = rest.astype(BF16)
    return hi, mid, (rest - mid.astype(F32)).astype(BF16)


def read_message(x):
    state = x[:ROWS].astype(F32)
    tail = x[ROWS:].astype(F32)
    total = tail[0:PAIRS] + tail[PAIRS : 2 * PAIRS] + tail[2 * PAIRS : 3 * PAIRS]
    return state, total


def spread(total):
    return jnp.concatenate(
        [jnp.broadcast_to(total[p : p + 1], (DK, total.shape[1])) for p in range(PAIRS)], axis=0
    )


def write_message(ref, state, total):
    ref[:ROWS, :] = state.astype(BF16)
    hi, mid, lo = split3(total)
    pad = jnp.zeros((TAIL - 3 * PAIRS, total.shape[1]), F32)
    ref[ROWS:, :] = jnp.concatenate(
        [hi.astype(F32), mid.astype(F32), lo.astype(F32), pad], axis=0
    ).astype(BF16)


def local_kernel(x_in, ld_in, wk_ref, wv_ref, k_ref, v_ref, *rest):
    outs, (chunks, x_ref, ld_ref, bk, bv, sems, own) = rest[:LANES], rest[LANES:]
    rows = x_ref.shape[0]
    first = [
        pltpu.make_async_copy(ld_in, ld_ref, own.at[0]),
        pltpu.make_async_copy(x_in, x_ref, own.at[1]),
    ]
    for copy in first:
        copy.start()
    copies = []
    for q in range(LANES):
        kc, vc = slice(q * HC * DK, (q + 1) * HC * DK), slice(q * HC * DV, (q + 1) * HC * DV)
        copies.append(
            (
                pltpu.make_async_copy(wk_ref.at[:, kc], bk.at[:, kc], sems.at[0, q]),
                pltpu.make_async_copy(wv_ref.at[:, vc], bv.at[:, vc], sems.at[1, q]),
            )
        )
    for pair in copies:
        for copy in pair:
            copy.start()
    first[0].wait()
    ld = ld_ref[...]
    t = lax.broadcasted_iota(jnp.int32, (rows, rows), 0)
    s = lax.broadcasted_iota(jnp.int32, (rows, rows), 1)
    after = ((s > t) & (chain_of(s) == chain_of(t))).astype(F32)
    tail = jnp.exp(nt(after, ld, precision=lax.Precision.HIGHEST))
    chain = chain_of(lax.broadcasted_iota(jnp.int32, ld.shape, 1))
    sums = [jnp.sum(jnp.where(chain == b, ld, 0.0), axis=1, keepdims=True) for b in (0, 1)]
    first[1].wait()
    x = x_ref[...]
    for q in range(LANES):
        for copy in copies[q]:
            copy.wait()
        kc, vc = slice(q * HC * DK, (q + 1) * HC * DK), slice(q * HC * DV, (q + 1) * HC * DV)
        k = nn(x, bk[:, kc]).astype(BF16)
        v = nn(x, bv[:, vc]).astype(BF16)
        k_ref[:, kc] = k
        v_ref[:, vc] = v
        states, totals = [], []
        for i in range(HC):
            h = q * HC + i
            kt = (k[:, i * DK : (i + 1) * DK].astype(F32) * tail[:, h : h + 1]).astype(BF16)
            states.append(tn(by_chain(kt), v[:, i * DV : (i + 1) * DV]))
            totals += [jnp.broadcast_to(sums[b][h : h + 1], (1, DV)) for b in (0, 1)]
        write_message(
            chunks.at[q], jnp.concatenate(states, axis=0), jnp.concatenate(totals, axis=0)
        )
    lane = lax.rem(lax.axis_index("tm"), LANES)
    for f in range(LANES):
        outs[f][...] = chunks[lane ^ f]


def local(tokens, w_rk, w_rv, ld):
    rows, d = tokens.shape
    message = jax.ShapeDtypeStruct((ROWS + TAIL, DV), BF16)
    return pl.pallas_call(
        local_kernel,
        in_specs=[HBM] * 4,
        out_specs=[VMEM] * (2 + LANES),
        out_shape=[
            jax.ShapeDtypeStruct((rows, H * DK), BF16),
            jax.ShapeDtypeStruct((rows, H * DV), BF16),
        ]
        + [message] * LANES,
        scratch_shapes=[
            pltpu.VMEM((LANES, ROWS + TAIL, DV), BF16),
            pltpu.VMEM((rows, d), BF16),
            pltpu.VMEM((H, rows), F32),
            pltpu.VMEM((d, H * DK), BF16),
            pltpu.VMEM((d, H * DV), BF16),
            pltpu.SemaphoreType.DMA((2, LANES)),
            pltpu.SemaphoreType.DMA((2,)),
        ],
        compiler_params=params(62),
        name="local",
    )(tokens, ld, w_rk, w_rv)


def list_live(frames, distances, tables, groups):
    me = lax.axis_index("tm")
    lane = lax.rem(me, LANES)
    plane = me // LANES
    spans = len(distances)
    for part in range(spans):
        table, counts, need = tables[3 * part : 3 * part + 3]

        def clear(b, _, need=need, part=part):
            need[b] = (b < frames).astype(jnp.int32) if part == 0 else jnp.int32(0)
            return 0

        lax.fori_loop(0, need.shape[0], clear, 0)
        for g in range(2):
            for f in range(frames):
                counts[g * frames + f] = jnp.int32(1 if part == 0 and g == 0 else 0)
                if part == 0 and g == 0:
                    table[f, 0] = jnp.int32(f)
    for g, (index, live) in enumerate(groups):
        slots = index.shape[1]
        for f in range(frames):
            row = g * frames + f

            def visit(i, carry, index=index, f=f, row=row):
                frame = index[f, i]
                owner = frame // frames
                its = lax.rem(owner, LANES)
                here = (its // 2) == (lane // 2)
                distance = plane - owner // LANES
                for part, (low, high) in enumerate(distances):
                    table, counts, need = tables[3 * part : 3 * part + 3]

                    @pl.when(here & (distance >= low) & (distance < high))
                    def _(table=table, counts=counts, need=need, low=low):
                        block = ((distance - low) * 2 + ((its ^ lane) & 1)) * frames
                        block = block + lax.rem(frame, frames)
                        n = counts[row]
                        table[row, n] = block
                        need[block] = 1
                        counts[row] = n + 1

                return carry

            lax.fori_loop(0, jnp.minimum(live[f], slots), visit, 0)


def inner_kernel(frames, distances, *refs):
    x_ref, ld_ref, k_ref, v_ref, idx, cnt, pidx, pcnt, wq_ref = refs[:9]
    inner_ref, qq_ref = refs[9:11]
    tables, (bq, sem) = refs[11:-2], refs[-2:]
    copy = pltpu.make_async_copy(wq_ref, bq, sem)
    copy.start()
    list_live(frames, distances, tables, ((idx, cnt), (pidx, pcnt)))
    rows = x_ref.shape[0]
    ld = ld_ref[...]
    t = lax.broadcasted_iota(jnp.int32, (rows, rows), 0)
    s = lax.broadcasted_iota(jnp.int32, (rows, rows), 1)
    upto = (s <= t) & (chain_of(s) == chain_of(t))
    ones = upto.astype(F32)
    column = nt(ones, ld, precision=lax.Precision.HIGHEST)
    row = nt(ld, ones, precision=lax.Precision.HIGHEST)
    grown = jnp.exp(column) * DK**-0.5
    copy.wait()
    q = nn(x_ref[...], bq[...]).astype(BF16)
    for h in range(H):
        qh = q[:, h * DK : (h + 1) * DK]
        gap = column[:, h : h + 1] - row[h : h + 1, :]
        weight = jnp.exp(jnp.where(upto, gap, NEG)) * DK**-0.5
        scores = nt(qh, k_ref[:, h * DK : (h + 1) * DK]) * weight
        inner_ref[:, h * DV : (h + 1) * DV] = nn(
            scores.astype(BF16), v_ref[:, h * DV : (h + 1) * DV]
        )
        scaled = qh.astype(F32) * grown[:, h : h + 1]
        qq_ref[:, h * 2 * DK : (h + 1) * 2 * DK] = by_chain(scaled.astype(BF16))


def inner(tokens, w_rq, k, v, ld, index, live, pindex, plive, distances):
    rows, d = tokens.shape
    frames = rows // P_SIZE
    slots = index.shape[1]
    table_shapes = []
    for low, high in distances:
        table_shapes += [
            jax.ShapeDtypeStruct((2 * frames, slots + 1), jnp.int32),
            jax.ShapeDtypeStruct((2 * frames,), jnp.int32),
            jax.ShapeDtypeStruct(((high - low) * 2 * frames,), jnp.int32),
        ]
    out = pl.pallas_call(
        functools.partial(inner_kernel, frames, distances),
        in_specs=[VMEM] * 4 + [SMEM] * 4 + [HBM],
        out_specs=[VMEM] * 2 + [SMEM] * len(table_shapes),
        out_shape=[
            jax.ShapeDtypeStruct((rows, H * DV), F32),
            jax.ShapeDtypeStruct((rows, H * 2 * DK), BF16),
        ]
        + table_shapes,
        scratch_shapes=[pltpu.VMEM((d, H * DK), BF16), pltpu.SemaphoreType.DMA(())],
        compiler_params=params(),
        cost_estimate=cost(2 * rows * d * H * DK, 8 << 20),
        name="inner",
    )(tokens, ld, k, v, index, live, pindex, plive, w_rq)
    return out[0], out[1], [out[2 + 3 * i : 5 + 3 * i] for i in range(len(distances))]


def plane_kernel(*refs):
    parts, out, ordered = refs[:LANES], refs[LANES], refs[LANES + 1]
    lane = lax.rem(lax.axis_index("tm"), LANES)
    for f in range(LANES):
        ordered[lane ^ f] = parts[f][...]
    state, total = read_message(ordered[0])
    for i in range(1, LANES):
        mine, decay = read_message(ordered[i])
        state = spread(jnp.exp(decay)) * state + mine
        total = total + decay
    write_message(out, state, total)


def plane_total(parts):
    return pl.pallas_call(
        plane_kernel,
        in_specs=[VMEM] * LANES,
        out_specs=VMEM,
        out_shape=jax.ShapeDtypeStruct((ROWS + TAIL, DV), BF16),
        scratch_shapes=[pltpu.VMEM((LANES, ROWS + TAIL, DV), BF16)],
        compiler_params=params(),
        name="plane",
    )(*parts)


def prefix_kernel(count, *refs):
    parts, earlier = refs[:LANES], refs[LANES : LANES + count]
    outs = refs[LANES + count : 2 * LANES + count]
    ordered, results = refs[2 * LANES + count :]
    lane = lax.rem(lax.axis_index("tm"), LANES)
    for f in range(LANES):
        ordered[lane ^ f] = parts[f][...]
    state = jnp.zeros((ROWS, DV), F32)
    for ref in reversed(earlier):
        mine, decay = read_message(ref[...])
        state = spread(jnp.exp(decay)) * state + mine
    for i in range(LANES):
        results[i] = state.astype(BF16)
        if i + 1 < LANES:
            mine, decay = read_message(ordered[i])
            state = spread(jnp.exp(decay)) * state + mine
    for f in range(LANES):
        outs[f][...] = results[lane ^ f]


def prefix(parts, earlier):
    return pl.pallas_call(
        functools.partial(prefix_kernel, len(earlier)),
        in_specs=[VMEM] * (LANES + len(earlier)),
        out_specs=[VMEM] * LANES,
        out_shape=[jax.ShapeDtypeStruct((ROWS, DV), BF16)] * LANES,
        scratch_shapes=[
            pltpu.VMEM((LANES, ROWS + TAIL, DV), BF16),
            pltpu.VMEM((LANES, ROWS, DV), BF16),
        ],
        compiler_params=params(),
        name="prefix",
    )(*parts, *earlier)


def hidden_kernel(frames, *refs):
    inner_ref, qq_ref = refs[:2]
    states = refs[2 : 2 + LANES]
    x_ref, gain_ref, wq, wk, wv = refs[2 + LANES : 7 + LANES]
    hid_ref, q_ref = refs[7 + LANES : 9 + LANES]
    kv_refs = refs[9 + LANES : 9 + LANES + frames]
    ordered, bq, bk, bv, sems = refs[9 + LANES + frames :]
    copies = [
        pltpu.make_async_copy(src, dst, sems.at[i])
        for i, (src, dst) in enumerate(((wq, bq), (wk, bk), (wv, bv)))
    ]
    for copy in copies:
        copy.start()
    lane = lax.rem(lax.axis_index("tm"), LANES)
    for f in range(LANES):
        ordered[lane ^ f] = states[f][...]
    for h in range(H):
        cols = slice(h * DV, (h + 1) * DV)
        state = ordered[h // HC, (h % HC) * 2 * DK : (h % HC + 1) * 2 * DK, :]
        o = inner_ref[:, cols] + nn(qq_ref[:, h * 2 * DK : (h + 1) * 2 * DK], state)
        scale = lax.rsqrt(jnp.mean(o * o, axis=1, keepdims=True) + 1e-05)
        y = o * scale * gain_ref[:, cols]
        hid_ref[:, cols] = (x_ref[:, cols].astype(F32) + y).astype(BF16)
    hid = hid_ref[...]
    copies[0].wait()
    q_ref[...] = nn(hid, bq[...]).astype(BF16)
    for i, buf in ((1, bk), (2, bv)):
        copies[i].wait()
        part = nn(hid, buf[...]).astype(BF16)
        for f in range(frames):
            kv_refs[f][:, (i - 1) * MC : i * MC] = part[f * P_SIZE : (f + 1) * P_SIZE]


def hidden_of(inner_out, qq, states, tokens, gain, w_mq, w_mk, w_mv):
    rows, d = tokens.shape
    frames = rows // P_SIZE
    return pl.pallas_call(
        functools.partial(hidden_kernel, frames),
        in_specs=[VMEM] * (LANES + 4) + [HBM] * 3,
        out_specs=[VMEM] * (2 + frames),
        out_shape=[
            jax.ShapeDtypeStruct((rows, d), BF16),
            jax.ShapeDtypeStruct((rows, MC), BF16),
        ]
        + [jax.ShapeDtypeStruct((P_SIZE, 2 * MC), BF16)] * frames,
        scratch_shapes=[pltpu.VMEM((LANES, ROWS, DV), BF16)]
        + [pltpu.VMEM((d, MC), BF16)] * 3
        + [pltpu.SemaphoreType.DMA((3,))],
        compiler_params=params(),
        name="hidden",
    )(inner_out, qq, *states, tokens, gain.reshape(1, d), w_mq, w_mk, w_mv)


def attend_kernel(frames, blocks, first, last, *refs):
    table, counts, need, q_ref, pq_ref = refs[:5]
    refs = refs[5:]
    if not first:
        acc_in, stat_in = refs[:2]
        refs = refs[2:]
    kv_refs = refs[:blocks]
    refs = refs[blocks:]
    if last:
        o_ref, po_ref, lse_ref, plse_ref = refs[:4]
        refs = refs[4:]
    else:
        acc_out, stat_out = refs[:2]
        refs = refs[2:]
    kv, scores, peak, total, acc, stat, sems = refs
    copies = [pltpu.make_async_copy(kv_refs[b], kv.at[b], sems.at[b]) for b in range(blocks)]
    for b in range(blocks):

        @pl.when(need[b] == 1)
        def _(b=b):
            copies[b].start()

    for b in range(blocks):

        @pl.when(need[b] == 1)
        def _(b=b):
            copies[b].wait()

    scale = MD**-0.5
    for row in range(2 * frames):
        queries = q_ref if row < frames else pq_ref
        f = row % frames
        span = slice(f * P_SIZE, (f + 1) * P_SIZE)
        held = slice(row * P_SIZE, (row + 1) * P_SIZE)
        n = counts[row]
        if first:
            stat[...] = jnp.zeros_like(stat)
            acc[...] = jnp.zeros_like(acc)
            peak[...] = jnp.full_like(peak, NEG)
        else:
            stat[...] = stat_in[held, :]
            for e in range(MH):
                acc[e] = acc_in[held, e * MD : (e + 1) * MD]

        @pl.when(n > 0)
        def _(row=row, queries=queries, span=span, n=n):
            if not first:
                for e in range(MH):
                    peak[e] = jnp.broadcast_to(stat[:, e : e + 1], (P_SIZE, P_SIZE))
            total[...] = jnp.zeros_like(total)
            half = (n + 1) // 2

            def score(i, _):
                b0 = table[row, 2 * i]
                more = 2 * i + 1 < n
                b1 = jnp.where(more, table[row, jnp.minimum(2 * i + 1, n - 1)], b0)
                for e in range(MH):
                    cols = slice(e * MD, (e + 1) * MD)
                    s0 = nt(queries[span, cols], kv[b0, :, cols])
                    s1 = nt(queries[span, cols], kv[b1, :, cols])
                    s1 = jnp.where(more, s1, NEG)
                    scores[2 * i, e] = s0
                    scores[2 * i + 1, e] = s1
                    peak[e] = jnp.maximum(peak[e], jnp.maximum(s0, s1))
                return 0

            lax.fori_loop(0, half, score, 0)
            for e in range(MH):
                top = jnp.max(peak[e], axis=1, keepdims=True)
                peak[e] = jnp.broadcast_to(top, (P_SIZE, P_SIZE))
                if not first:
                    fade = jnp.exp((stat[:, e : e + 1] - top) * scale)
                    acc[e] = acc[e] * fade
                    stat[:, MH + e : MH + e + 1] = stat[:, MH + e : MH + e + 1] * fade
                stat[:, e : e + 1] = top

            def weigh(i, _):
                b0 = table[row, 2 * i]
                b1 = table[row, jnp.minimum(2 * i + 1, n - 1)]
                for e in range(MH):
                    cols = slice(MC + e * MD, MC + (e + 1) * MD)
                    p0 = jnp.exp((scores[2 * i, e] - peak[e]) * scale)
                    p1 = jnp.exp((scores[2 * i + 1, e] - peak[e]) * scale)
                    total[e] += p0 + p1
                    acc[e] += nn(p0.astype(BF16), kv[b0, :, cols]) + nn(
                        p1.astype(BF16), kv[b1, :, cols]
                    )
                return 0

            lax.fori_loop(0, half, weigh, 0)
            for e in range(MH):
                stat[:, MH + e : MH + e + 1] += jnp.sum(total[e], axis=1, keepdims=True)

        if first:

            @pl.when(n == 0)
            def _():
                for e in range(MH):
                    stat[:, e : e + 1] = jnp.full((P_SIZE, 1), NEG, F32)

        if last:
            out, stats = (o_ref, lse_ref) if row < frames else (po_ref, plse_ref)
            for e in range(MH):
                l = jnp.maximum(stat[:, MH + e : MH + e + 1], 1e-30)
                out[span, e * MD : (e + 1) * MD] = (acc[e] / l).astype(out.dtype)
            flat = jnp.transpose(stat[...])
            low = jnp.log(jnp.maximum(flat[MH : 2 * MH], 1e-30))
            stats[:, span] = jnp.concatenate([flat[:MH] * scale + low, low], axis=0)
        else:
            stat_out[held, :] = stat[...]
            for e in range(MH):
                acc_out[held, e * MD : (e + 1) * MD] = acc[e]


def attend(tables, q, pq, kvs, state, last):
    rows = q.shape[0]
    frames = rows // P_SIZE
    blocks = len(kvs)
    slots = tables[0].shape[1]
    first = state is None
    state = [] if first else list(state)
    if last:
        out_shape = [
            jax.ShapeDtypeStruct((rows, MC), F32),
            jax.ShapeDtypeStruct((rows, MC), BF16),
            jax.ShapeDtypeStruct((2 * MH, rows), F32),
            jax.ShapeDtypeStruct((2 * MH, rows), F32),
        ]
    else:
        out_shape = [
            jax.ShapeDtypeStruct((2 * rows, MC), F32),
            jax.ShapeDtypeStruct((2 * rows, 128), F32),
        ]
    return pl.pallas_call(
        functools.partial(attend_kernel, frames, blocks, first, last),
        in_specs=[SMEM] * 3 + [VMEM] * (2 + len(state)) + [HBM] * blocks,
        out_specs=[VMEM] * len(out_shape),
        out_shape=out_shape,
        scratch_shapes=[
            pltpu.VMEM((blocks, P_SIZE, 2 * MC), BF16),
            pltpu.VMEM((slots + 2, MH, P_SIZE, P_SIZE), F32),
            pltpu.VMEM((MH, P_SIZE, P_SIZE), F32),
            pltpu.VMEM((MH, P_SIZE, P_SIZE), F32),
            pltpu.VMEM((MH, P_SIZE, MD), F32),
            pltpu.VMEM((P_SIZE, 128), F32),
            pltpu.SemaphoreType.DMA((blocks,)),
        ],
        compiler_params=params(),
        cost_estimate=cost(4 * 8 * frames * P_SIZE * P_SIZE * MC, blocks * P_SIZE * MC * 4),
        name="attend_last" if last else "attend",
    )(*tables, q, pq, *state, *kvs)


def output_kernel(o_ref, lse_ref, po_ref, plse_ref, hid_ref, w_ref, out_ref, mixed):
    rows = o_ref.shape[0]
    mine, other = lse_ref[...], plse_ref[...]
    top = jnp.maximum(mine, other)
    a, b = jnp.exp(mine - top), jnp.exp(other - top)
    inv = 1.0 / (a + b)
    both = jnp.concatenate([a * inv, b * inv, jnp.zeros((128 - 16, rows), F32)], axis=0)
    weights = jnp.transpose(both)
    for e in range(MH):
        cols = slice(e * MD, (e + 1) * MD)
        value = o_ref[:, cols] * weights[:, e : e + 1]
        value = value + po_ref[:, cols].astype(F32) * weights[:, 8 + e : 9 + e]
        mixed[:, cols] = value.astype(BF16)
    out_ref[...] = (hid_ref[...].astype(F32) + nn(mixed[...], w_ref[...])).astype(BF16)


def output(o, lse, po, plse, hid, w_out):
    rows, d = hid.shape
    return pl.pallas_call(
        output_kernel,
        in_specs=[VMEM] * 6,
        out_specs=VMEM,
        out_shape=jax.ShapeDtypeStruct((rows, d), BF16),
        scratch_shapes=[pltpu.VMEM((rows, MC), BF16)],
        compiler_params=params(),
        name="output",
    )(o, lse, po, plse, hid, w_out)


def on_device(
    tokens, log_decay, mem_index, mem_count, w_rq, w_rk, w_rv, norm_gain, w_mq, w_mk, w_mv, w_out
):
    size = lax.axis_size("tm")
    planes = size // LANES

    def flip(x, bits):
        return lax.ppermute(x, "tm", [(i, i ^ bits) for i in range(size)])

    def up(x, distance):
        step = distance * LANES
        return lax.ppermute(x, "tm", [(i, i + step) for i in range(size - step)])

    spans = ((0, planes - 1), (planes - 1, planes)) if planes > 1 else ((0, planes),)
    partner_index, partner_count = flip(mem_index, 2), flip(mem_count, 2)
    k, v, *chunks = local(tokens, w_rk, w_rv, log_decay)
    parts = [chunks[0]] + [flip(chunks[f], f) for f in range(1, LANES)]
    inner_out, qq, tables = inner(
        tokens, w_rq, k, v, log_decay, mem_index, mem_count, partner_index, partner_count, spans
    )
    total = plane_total(parts)
    earlier = [up(total, distance) for distance in range(1, planes)]
    mine = prefix(parts, earlier)
    states = [mine[0]] + [flip(mine[f], f) for f in range(1, LANES)]
    hid, q, *kv = hidden_of(inner_out, qq, states, tokens, norm_gain, w_mq, w_mk, w_mv)
    partner_q = flip(q, 2)
    held = []
    for distance in range(planes):
        if distance:
            moved = []
            for x in kv:
                moved.append(up(x, 1))
            kv = moved
        near = []
        for x in kv:
            near.append(flip(x, 1))
        held.append(kv + near)
    state = None
    for (low, high), table in zip(spans, tables):
        blocks = [x for group in held[low:high] for x in group]
        state = attend(table, q, partner_q, blocks, state, high == planes)
    o, po, lse, plse = state
    return output(o, lse, flip(po, 2), flip(plse, 2), hid, w_out)


def solution(mesh):
    placed = (
        P(("groups", "tm"), None),
        P(None, ("groups", "tm")),
        P(("groups", "tm"), None),
        P(("groups", "tm")),
        P(),
        P(),
        P(),
        P(),
        P(),
        P(),
        P(),
        P(),
    )

    return jax.shard_map(
        on_device, mesh=mesh, in_specs=placed, out_specs=P(("groups", "tm"), None), check_vma=False
    )
```

```python
import functools

import jax
import jax.numpy as jnp
from jax import lax
from jax.experimental import pallas as pl
from jax.experimental.pallas import tpu as pltpu
from jax.sharding import PartitionSpec as P


H = 8
DK = 64
DV = 128
MH = 4
MD = 128
MC = 512
P_SIZE = 128
BLK = 64
LANES = 4
HC = H // LANES
ROWS = HC * 2 * DK
TAIL = 16
PAIRS = HC * 2
NEG = -1e30
F32 = jnp.float32
BF16 = jnp.bfloat16


VMEM = pl.BlockSpec(memory_space=pltpu.VMEM)
SMEM = pl.BlockSpec(memory_space=pltpu.SMEM)
HBM = pl.BlockSpec(memory_space=pltpu.HBM)


def params(mib=48):
    return pltpu.CompilerParams(vmem_limit_bytes=mib << 20)


def cost(flops, nbytes):
    return pl.CostEstimate(flops=flops, bytes_accessed=nbytes, transcendentals=0)


def chain_of(iota):
    return (iota // BLK) % 2


def nn(a, b, **kw):
    return lax.dot_general(a, b, (((1,), (0,)), ((), ())), preferred_element_type=F32, **kw)


def nt(a, b, **kw):
    return lax.dot_general(a, b, (((1,), (1,)), ((), ())), preferred_element_type=F32, **kw)


def tn(a, b, **kw):
    return lax.dot_general(a, b, (((0,), (0,)), ((), ())), preferred_element_type=F32, **kw)


def by_chain(x):
    rows = x.shape[0]
    chain = chain_of(lax.broadcasted_iota(jnp.int32, (rows, DK), 0))
    zero = jnp.zeros_like(x)
    return jnp.concatenate([jnp.where(chain == 0, x, zero), jnp.where(chain == 1, x, zero)], axis=1)


def split3(x):
    hi = x.astype(BF16)
    rest = x - hi.astype(F32)
    mid = rest.astype(BF16)
    return hi, mid, (rest - mid.astype(F32)).astype(BF16)


def read_message(x):
    state = x[:ROWS].astype(F32)
    tail = x[ROWS:].astype(F32)
    total = tail[0:PAIRS] + tail[PAIRS : 2 * PAIRS] + tail[2 * PAIRS : 3 * PAIRS]
    return state, total


def spread(total):
    return jnp.concatenate(
        [jnp.broadcast_to(total[p : p + 1], (DK, total.shape[1])) for p in range(PAIRS)], axis=0
    )


def write_message(ref, state, total):
    ref[:ROWS, :] = state.astype(BF16)
    hi, mid, lo = split3(total)
    pad = jnp.zeros((TAIL - 3 * PAIRS, total.shape[1]), F32)
    ref[ROWS:, :] = jnp.concatenate(
        [hi.astype(F32), mid.astype(F32), lo.astype(F32), pad], axis=0
    ).astype(BF16)


def decay_terms(ld):
    return jnp.concatenate([t.astype(F32) for t in split3(ld)], axis=0).astype(BF16)


def column_sums(mask, ld):
    x = nt(mask.astype(BF16), decay_terms(ld))
    return x[:, :H] + x[:, H : 2 * H] + x[:, 2 * H : 3 * H]


def row_sums(mask, ld):
    x = nt(decay_terms(ld), mask.astype(BF16))
    return x[:H] + x[H : 2 * H] + x[2 * H : 3 * H]


def position():
    lane = lax.rem(lax.axis_index("tm"), LANES)
    return lane // 2, lane & 1


def local_kernel(x_in, ld_in, wk_in, wv_in, idx, cnt, k_ref, v_ref, keep, give, pack, *rest):
    chunks, x_ref, ld_ref, bk, bv, sems = rest
    rows = x_ref.shape[0]
    copies = [
        pltpu.make_async_copy(src, dst, sems.at[i])
        for i, (src, dst) in enumerate(
            ((ld_in, ld_ref), (x_in, x_ref), (wk_in, bk), (wv_in, bv))
        )
    ]
    for copy in copies:
        copy.start()
    frames, slots = idx.shape
    for f in range(frames):
        for i in range(slots):
            pack[f, i] = idx[f, i]
        pack[f, slots] = cnt[f]
    t = lax.broadcasted_iota(jnp.int32, (rows, rows), 0)
    s = lax.broadcasted_iota(jnp.int32, (rows, rows), 1)
    after = ((s > t) & (chain_of(s) == chain_of(t))).astype(F32)
    copies[0].wait()
    ld = ld_ref[...]
    tail = jnp.exp(column_sums(after, ld))
    chain = chain_of(lax.broadcasted_iota(jnp.int32, ld.shape, 1))
    sums = [jnp.sum(jnp.where(chain == b, ld, 0.0), axis=1, keepdims=True) for b in (0, 1)]
    for copy in copies[1:]:
        copy.wait()
    x = x_ref[...]
    k = nn(x, bk[...]).astype(BF16)
    k_ref[...] = k
    for q in range(LANES):
        vc = slice(q * HC * DV, (q + 1) * HC * DV)
        v = nn(x, bv[:, vc]).astype(BF16)
        v_ref[:, vc] = v
        states, totals = [], []
        for i in range(HC):
            h = q * HC + i
            kt = (k[:, h * DK : (h + 1) * DK].astype(F32) * tail[:, h : h + 1]).astype(BF16)
            states.append(tn(by_chain(kt), v[:, i * DV : (i + 1) * DV]))
            totals += [jnp.broadcast_to(sums[b][h : h + 1], (1, DV)) for b in (0, 1)]
        write_message(
            chunks.at[q], jnp.concatenate(states, axis=0), jnp.concatenate(totals, axis=0)
        )
    _, core = position()
    for y in range(2):
        keep[y] = chunks[2 * y + core]
        give[y] = chunks[2 * y + 1 - core]


def local(tokens, w_rk, w_rv, ld, index, live):
    rows, d = tokens.shape
    message = jax.ShapeDtypeStruct((2, ROWS + TAIL, DV), BF16)
    frames, slots = index.shape
    return pl.pallas_call(
        local_kernel,
        in_specs=[HBM] * 4 + [SMEM] * 2,
        out_specs=[VMEM] * 4 + [SMEM],
        out_shape=[
            jax.ShapeDtypeStruct((rows, H * DK), BF16),
            jax.ShapeDtypeStruct((rows, H * DV), BF16),
            message,
            message,
            jax.ShapeDtypeStruct((frames, slots + 1), jnp.int32),
        ],
        scratch_shapes=[
            pltpu.VMEM((LANES, ROWS + TAIL, DV), BF16),
            pltpu.VMEM((rows, d), BF16),
            pltpu.VMEM((H, rows), F32),
            pltpu.VMEM((d, H * DK), BF16),
            pltpu.VMEM((d, H * DV), BF16),
            pltpu.SemaphoreType.DMA((4,)),
        ],
        compiler_params=params(62),
        name="local",
    )(tokens, ld, w_rk, w_rv, index, live)


def list_live(frames, distances, tables, groups):
    me = lax.axis_index("tm")
    lane = lax.rem(me, LANES)
    plane = me // LANES
    spans = len(distances)
    for part in range(spans):
        table, counts, need = tables[3 * part : 3 * part + 3]

        def clear(b, _, need=need, part=part):
            need[b] = (b < frames).astype(jnp.int32) if part == 0 else jnp.int32(0)
            return 0

        lax.fori_loop(0, need.shape[0], clear, 0)
        for g in range(2):
            for f in range(frames):
                counts[g * frames + f] = jnp.int32(1 if part == 0 and g == 0 else 0)
                if part == 0 and g == 0:
                    table[f, 0] = jnp.int32(f)
    for g, index in enumerate(groups):
        slots = index.shape[1] - 1
        for f in range(frames):
            row = g * frames + f

            def visit(i, carry, index=index, f=f, row=row):
                frame = index[f, i]
                owner = frame // frames
                its = lax.rem(owner, LANES)
                here = (its // 2) == (lane // 2)
                distance = plane - owner // LANES
                for part, (low, high) in enumerate(distances):
                    table, counts, need = tables[3 * part : 3 * part + 3]

                    @pl.when(here & (distance >= low) & (distance < high))
                    def _(table=table, counts=counts, need=need, low=low):
                        block = ((distance - low) * 2 + ((its ^ lane) & 1)) * frames
                        block = block + lax.rem(frame, frames)
                        n = counts[row]
                        table[row, n] = block
                        need[block] = 1
                        counts[row] = n + 1

                return carry

            lax.fori_loop(0, jnp.minimum(index[f, slots], slots), visit, 0)


def inner_kernel(frames, distances, *refs):
    x_in, ld_ref, k_in, v_in, pack, other, wq_in = refs[:7]
    inner_ref, qq_ref = refs[7:9]
    tables, (x_ref, k_ref, v_ref, bq, sems) = refs[9:-5], refs[-5:]
    copies = [
        pltpu.make_async_copy(src, dst, sems.at[i])
        for i, (src, dst) in enumerate(
            ((x_in, x_ref), (wq_in, bq), (k_in, k_ref), (v_in, v_ref))
        )
    ]
    for copy in copies:
        copy.start()
    list_live(frames, distances, tables, (pack, other))
    rows = x_in.shape[0]
    ld = ld_ref[...]
    t = lax.broadcasted_iota(jnp.int32, (rows, rows), 0)
    s = lax.broadcasted_iota(jnp.int32, (rows, rows), 1)
    upto = (s <= t) & (chain_of(s) == chain_of(t))
    ones = upto.astype(F32)
    column = column_sums(ones, ld)
    row = row_sums(ones, ld)
    grown = jnp.exp(column) * DK**-0.5
    for copy in copies:
        copy.wait()
    q = nn(x_ref[...], bq[...]).astype(BF16)
    for h in range(H):
        qh = q[:, h * DK : (h + 1) * DK]
        gap = column[:, h : h + 1] - row[h : h + 1, :]
        weight = jnp.exp(jnp.where(upto, gap, NEG)) * DK**-0.5
        scores = nt(qh, k_ref[:, h * DK : (h + 1) * DK]) * weight
        inner_ref[:, h * DV : (h + 1) * DV] = nn(
            scores.astype(BF16), v_ref[:, h * DV : (h + 1) * DV]
        )
        scaled = qh.astype(F32) * grown[:, h : h + 1]
        qq_ref[:, h * 2 * DK : (h + 1) * 2 * DK] = by_chain(scaled.astype(BF16))


def inner(tokens, w_rq, k, v, ld, pack, other, distances):
    rows, d = tokens.shape
    frames = rows // P_SIZE
    slots = pack.shape[1] - 1
    table_shapes = []
    for low, high in distances:
        table_shapes += [
            jax.ShapeDtypeStruct((2 * frames, slots + 1), jnp.int32),
            jax.ShapeDtypeStruct((2 * frames,), jnp.int32),
            jax.ShapeDtypeStruct(((high - low) * 2 * frames,), jnp.int32),
        ]
    out = pl.pallas_call(
        functools.partial(inner_kernel, frames, distances),
        in_specs=[HBM, VMEM, HBM, HBM, SMEM, SMEM, HBM],
        out_specs=[VMEM] * 2 + [SMEM] * len(table_shapes),
        out_shape=[
            jax.ShapeDtypeStruct((rows, H * DV), F32),
            jax.ShapeDtypeStruct((rows, H * 2 * DK), BF16),
        ]
        + table_shapes,
        scratch_shapes=[
            pltpu.VMEM((rows, d), BF16),
            pltpu.VMEM((rows, H * DK), BF16),
            pltpu.VMEM((rows, H * DV), BF16),
            pltpu.VMEM((d, H * DK), BF16),
            pltpu.SemaphoreType.DMA((4,)),
        ],
        compiler_params=params(48),
        cost_estimate=cost(2 * rows * d * H * DK, 8 << 20),
        name="inner",
    )(tokens, ld, k, v, pack, other, w_rq)
    return out[0], out[1], [out[2 + 3 * i : 5 + 3 * i] for i in range(len(distances))]


def join(first, second):
    return spread(jnp.exp(second[1])) * first[0] + second[0], first[1] + second[1]


def chip_kernel(keep, got, stay, send, ordered, results):
    y, core = position()
    ordered[core] = keep[...]
    ordered[1 - core] = got[...]
    for q in range(2):
        write_message(
            results.at[q], *join(read_message(ordered[0, q]), read_message(ordered[1, q]))
        )
    stay[...] = results[y]
    send[...] = results[1 - y]


def plane_kernel(stay, got, out, ordered):
    y, _ = position()
    ordered[y] = stay[...]
    ordered[1 - y] = got[...]
    write_message(out, *join(read_message(ordered[0]), read_message(ordered[1])))


def prefix_kernel(count, *refs):
    (stay, got), earlier = refs[:2], refs[2 : 2 + count]
    mine, send, ordered, results = refs[2 + count :]
    y, _ = position()
    plane = lax.axis_index("tm") // LANES
    ordered[y] = stay[...]
    ordered[1 - y] = got[...]
    state = jnp.zeros((ROWS, DV), F32)
    for distance in range(count, 0, -1):
        step, _ = join((state, 0.0), read_message(earlier[distance - 1][...]))
        state = jnp.where(plane >= distance, step, 0.0)
    results[0] = state.astype(BF16)
    results[1] = join((state, 0.0), read_message(ordered[0]))[0].astype(BF16)
    mine[...] = results[y]
    send[...] = results[1 - y]


def split_kernel(keep, local_got, mine, got, kept, give, ordered, both, results):
    y, core = position()
    ordered[core] = keep[...]
    ordered[1 - core] = local_got[...]
    both[y] = mine[...]
    both[1 - y] = got[...]
    for q in range(2):
        state = both[q]
        results[0, q] = state
        results[1, q] = join((state.astype(F32), 0.0), read_message(ordered[0, q]))[0].astype(BF16)
    kept[...] = results[core]
    give[...] = results[1 - core]


def small(kernel, outs, scratch, *args):
    return pl.pallas_call(
        kernel,
        in_specs=[VMEM] * len(args),
        out_specs=[VMEM] * len(outs),
        out_shape=[jax.ShapeDtypeStruct(shape, BF16) for shape in outs],
        scratch_shapes=[pltpu.VMEM(shape, BF16) for shape in scratch],
        compiler_params=params(8),
    )(*args)


def hidden_kernel(frames, *refs):
    inner_ref, qq_ref = refs[:2]
    kept, got = refs[2:4]
    x_ref, gain_ref, wq, wk, wv = refs[4:9]
    hid_ref, q_ref = refs[9:11]
    kv_refs = refs[11 : 11 + frames]
    ordered, bq, bk, bv, sems = refs[11 + frames :]
    copies = [
        pltpu.make_async_copy(src, dst, sems.at[i])
        for i, (src, dst) in enumerate(((wq, bq), (wk, bk), (wv, bv)))
    ]
    for copy in copies:
        copy.start()
    _, core = position()
    for y in range(2):
        ordered[2 * y + core] = kept[y]
        ordered[2 * y + 1 - core] = got[y]
    for h in range(H):
        cols = slice(h * DV, (h + 1) * DV)
        state = ordered[h // HC, (h % HC) * 2 * DK : (h % HC + 1) * 2 * DK, :]
        o = inner_ref[:, cols] + nn(qq_ref[:, h * 2 * DK : (h + 1) * 2 * DK], state)
        scale = lax.rsqrt(jnp.mean(o * o, axis=1, keepdims=True) + 1e-05)
        y = o * scale * gain_ref[:, cols]
        hid_ref[:, cols] = (x_ref[:, cols].astype(F32) + y).astype(BF16)
    hid = hid_ref[...]
    copies[0].wait()
    q_ref[...] = nn(hid, bq[...]).astype(BF16)
    for i, buf in ((1, bk), (2, bv)):
        copies[i].wait()
        part = nn(hid, buf[...]).astype(BF16)
        for f in range(frames):
            kv_refs[f][:, (i - 1) * MC : i * MC] = part[f * P_SIZE : (f + 1) * P_SIZE]


def hidden_of(inner_out, qq, states, tokens, gain, w_mq, w_mk, w_mv):
    rows, d = tokens.shape
    frames = rows // P_SIZE
    return pl.pallas_call(
        functools.partial(hidden_kernel, frames),
        in_specs=[VMEM] * 6 + [HBM] * 3,
        out_specs=[VMEM] * (2 + frames),
        out_shape=[
            jax.ShapeDtypeStruct((rows, d), BF16),
            jax.ShapeDtypeStruct((rows, MC), BF16),
        ]
        + [jax.ShapeDtypeStruct((P_SIZE, 2 * MC), BF16)] * frames,
        scratch_shapes=[pltpu.VMEM((LANES, ROWS, DV), BF16)]
        + [pltpu.VMEM((d, MC), BF16)] * 3
        + [pltpu.SemaphoreType.DMA((3,))],
        compiler_params=params(),
        name="hidden",
    )(inner_out, qq, *states, tokens, gain.reshape(1, d), w_mq, w_mk, w_mv)


def attend_kernel(frames, blocks, first, last, *refs):
    table, counts, need, q_ref, pq_ref = refs[:5]
    refs = refs[5:]
    if not first:
        acc_in, stat_in = refs[:2]
        refs = refs[2:]
    kv_refs = refs[:blocks]
    refs = refs[blocks:]
    if last:
        o_ref, po_ref, lse_ref, plse_ref = refs[:4]
        refs = refs[4:]
    else:
        acc_out, stat_out = refs[:2]
        refs = refs[2:]
    kv, scores, peak, total, acc, stat, sems = refs
    copies = [pltpu.make_async_copy(kv_refs[b], kv.at[b], sems.at[b]) for b in range(blocks)]
    for b in range(blocks):

        @pl.when(need[b] == 1)
        def _(b=b):
            copies[b].start()

    for b in range(blocks):

        @pl.when(need[b] == 1)
        def _(b=b):
            copies[b].wait()

    scale = MD**-0.5
    for row in range(2 * frames):
        queries = q_ref if row < frames else pq_ref
        f = row % frames
        span = slice(f * P_SIZE, (f + 1) * P_SIZE)
        held = slice(row * P_SIZE, (row + 1) * P_SIZE)
        n = counts[row]
        if first:
            stat[...] = jnp.zeros_like(stat)
            acc[...] = jnp.zeros_like(acc)
            peak[...] = jnp.full_like(peak, NEG)
        else:
            stat[...] = stat_in[held, :]
            for e in range(MH):
                acc[e] = acc_in[held, e * MD : (e + 1) * MD]

        @pl.when(n > 0)
        def _(row=row, queries=queries, span=span, n=n):
            if not first:
                for e in range(MH):
                    peak[e] = jnp.broadcast_to(stat[:, e : e + 1], (P_SIZE, P_SIZE))
            total[...] = jnp.zeros_like(total)
            half = (n + 1) // 2

            def score(i, _):
                b0 = table[row, 2 * i]
                more = 2 * i + 1 < n
                b1 = jnp.where(more, table[row, jnp.minimum(2 * i + 1, n - 1)], b0)
                for e in range(MH):
                    cols = slice(e * MD, (e + 1) * MD)
                    s0 = nt(queries[span, cols], kv[b0, :, cols])
                    s1 = nt(queries[span, cols], kv[b1, :, cols])
                    s1 = jnp.where(more, s1, NEG)
                    scores[2 * i, e] = s0
                    scores[2 * i + 1, e] = s1
                    peak[e] = jnp.maximum(peak[e], jnp.maximum(s0, s1))
                return 0

            lax.fori_loop(0, half, score, 0)
            for e in range(MH):
                top = jnp.max(peak[e], axis=1, keepdims=True)
                peak[e] = jnp.broadcast_to(top, (P_SIZE, P_SIZE))
                if not first:
                    fade = jnp.exp((stat[:, e : e + 1] - top) * scale)
                    acc[e] = acc[e] * fade
                    stat[:, MH + e : MH + e + 1] = stat[:, MH + e : MH + e + 1] * fade
                stat[:, e : e + 1] = top

            def weigh(i, _):
                b0 = table[row, 2 * i]
                b1 = table[row, jnp.minimum(2 * i + 1, n - 1)]
                for e in range(MH):
                    cols = slice(MC + e * MD, MC + (e + 1) * MD)
                    p0 = jnp.exp((scores[2 * i, e] - peak[e]) * scale)
                    p1 = jnp.exp((scores[2 * i + 1, e] - peak[e]) * scale)
                    total[e] += p0 + p1
                    acc[e] += nn(p0.astype(BF16), kv[b0, :, cols]) + nn(
                        p1.astype(BF16), kv[b1, :, cols]
                    )
                return 0

            lax.fori_loop(0, half, weigh, 0)
            for e in range(MH):
                stat[:, MH + e : MH + e + 1] += jnp.sum(total[e], axis=1, keepdims=True)

        if first:

            @pl.when(n == 0)
            def _():
                for e in range(MH):
                    stat[:, e : e + 1] = jnp.full((P_SIZE, 1), NEG, F32)

        if last:
            out, stats = (o_ref, lse_ref) if row < frames else (po_ref, plse_ref)
            for e in range(MH):
                l = jnp.maximum(stat[:, MH + e : MH + e + 1], 1e-30)
                out[span, e * MD : (e + 1) * MD] = (acc[e] / l).astype(out.dtype)
            flat = jnp.transpose(stat[...])
            low = jnp.log(jnp.maximum(flat[MH : 2 * MH], 1e-30))
            stats[:, span] = jnp.concatenate([flat[:MH] * scale + low, low], axis=0)
        else:
            stat_out[held, :] = stat[...]
            for e in range(MH):
                acc_out[held, e * MD : (e + 1) * MD] = acc[e]


def attend(tables, q, pq, kvs, state, last):
    rows = q.shape[0]
    frames = rows // P_SIZE
    blocks = len(kvs)
    slots = tables[0].shape[1]
    first = state is None
    state = [] if first else list(state)
    if last:
        out_shape = [
            jax.ShapeDtypeStruct((rows, MC), F32),
            jax.ShapeDtypeStruct((rows, MC), BF16),
            jax.ShapeDtypeStruct((2 * MH, rows), F32),
            jax.ShapeDtypeStruct((2 * MH, rows), F32),
        ]
    else:
        out_shape = [
            jax.ShapeDtypeStruct((2 * rows, MC), F32),
            jax.ShapeDtypeStruct((2 * rows, 128), F32),
        ]
    return pl.pallas_call(
        functools.partial(attend_kernel, frames, blocks, first, last),
        in_specs=[SMEM] * 3 + [VMEM] * (2 + len(state)) + [HBM] * blocks,
        out_specs=[VMEM] * len(out_shape),
        out_shape=out_shape,
        scratch_shapes=[
            pltpu.VMEM((blocks, P_SIZE, 2 * MC), BF16),
            pltpu.VMEM((slots + 2, MH, P_SIZE, P_SIZE), F32),
            pltpu.VMEM((MH, P_SIZE, P_SIZE), F32),
            pltpu.VMEM((MH, P_SIZE, P_SIZE), F32),
            pltpu.VMEM((MH, P_SIZE, MD), F32),
            pltpu.VMEM((P_SIZE, 128), F32),
            pltpu.SemaphoreType.DMA((blocks,)),
        ],
        compiler_params=params(),
        cost_estimate=cost(4 * 8 * frames * P_SIZE * P_SIZE * MC, blocks * P_SIZE * MC * 4),
        name="attend_last" if last else "attend",
    )(*tables, q, pq, *state, *kvs)


def output_kernel(o_ref, lse_ref, po_ref, plse_ref, hid_ref, w_ref, out_ref, mixed):
    rows = o_ref.shape[0]
    mine, other = lse_ref[...], plse_ref[...]
    top = jnp.maximum(mine, other)
    a, b = jnp.exp(mine - top), jnp.exp(other - top)
    inv = 1.0 / (a + b)
    both = jnp.concatenate([a * inv, b * inv, jnp.zeros((128 - 16, rows), F32)], axis=0)
    weights = jnp.transpose(both)
    for e in range(MH):
        cols = slice(e * MD, (e + 1) * MD)
        value = o_ref[:, cols] * weights[:, e : e + 1]
        value = value + po_ref[:, cols].astype(F32) * weights[:, 8 + e : 9 + e]
        mixed[:, cols] = value.astype(BF16)
    out_ref[...] = (hid_ref[...].astype(F32) + nn(mixed[...], w_ref[...])).astype(BF16)


def output(o, lse, po, plse, hid, w_out):
    rows, d = hid.shape
    return pl.pallas_call(
        output_kernel,
        in_specs=[VMEM] * 6,
        out_specs=VMEM,
        out_shape=jax.ShapeDtypeStruct((rows, d), BF16),
        scratch_shapes=[pltpu.VMEM((rows, MC), BF16)],
        compiler_params=params(),
        name="output",
    )(o, lse, po, plse, hid, w_out)


def on_device(
    tokens, log_decay, mem_index, mem_count, w_rq, w_rk, w_rv, norm_gain, w_mq, w_mk, w_mv, w_out
):
    size = lax.axis_size("tm")
    planes = size // LANES

    def flip(x, bits):
        return lax.ppermute(x, "tm", [(i, i ^ bits) for i in range(size)])

    def up(x, distance):
        step = distance * LANES
        return lax.ppermute(x, "tm", [(i, (i + step) % size) for i in range(size)])

    message, chunk = (ROWS + TAIL, DV), (ROWS, DV)
    spans = ((0, planes - 1), (planes - 1, planes)) if planes > 1 else ((0, planes),)
    k, v, keep, give, pack = local(tokens, w_rk, w_rv, log_decay, mem_index, mem_count)
    core_got = flip(give, 1)
    other = flip(pack, 2)
    stay, send = small(
        chip_kernel, [message] * 2, [(2, 2) + message, (2,) + message], keep, core_got
    )
    column_got = flip(send, 2)
    (total,) = small(plane_kernel, [message], [(2,) + message], stay, column_got)
    earlier = [up(total, d) for d in range(1, planes)]
    inner_out, qq, tables = inner(tokens, w_rq, k, v, log_decay, pack, other, spans)
    mine, send = small(
        functools.partial(prefix_kernel, len(earlier)),
        [chunk] * 2,
        [(2,) + message, (2,) + chunk],
        stay,
        column_got,
        *earlier,
    )
    column_back = flip(send, 2)
    kept, give = small(
        split_kernel,
        [(2,) + chunk] * 2,
        [(2, 2) + message, (2,) + chunk, (2, 2) + chunk],
        keep,
        core_got,
        mine,
        column_back,
    )
    states = (kept, flip(give, 1))
    hid, q, *kv = hidden_of(inner_out, qq, states, tokens, norm_gain, w_mq, w_mk, w_mv)
    partner_q = flip(q, 2)
    held = []
    for distance in range(planes):
        if distance:
            moved = []
            for x in kv:
                moved.append(up(x, 1))
            kv = moved
        near = []
        for x in kv:
            near.append(flip(x, 1))
        held.append(kv + near)
    state = None
    for (low, high), table in zip(spans, tables):
        blocks = [x for group in held[low:high] for x in group]
        state = attend(table, q, partner_q, blocks, state, high == planes)
    o, po, lse, plse = state
    return output(o, lse, flip(po, 2), flip(plse, 2), hid, w_out)


def solution(mesh):
    placed = (
        P(("groups", "tm"), None),
        P(None, ("groups", "tm")),
        P(("groups", "tm"), None),
        P(("groups", "tm")),
        P(),
        P(),
        P(),
        P(),
        P(),
        P(),
        P(),
        P(),
    )

    return jax.shard_map(
        on_device, mesh=mesh, in_specs=placed, out_specs=P(("groups", "tm"), None), check_vma=False
    )
```

```python
import functools

import jax
import jax.numpy as jnp
from jax import lax
from jax.experimental import pallas as pl
from jax.experimental.pallas import tpu as pltpu
from jax.sharding import PartitionSpec as P


H = 8
DK = 64
DV = 128
MH = 4
MD = 128
MC = 512
P_SIZE = 128
BLK = 64
LANES = 4
HC = H // LANES
ROWS = HC * 2 * DK
TAIL = 16
PAIRS = HC * 2
NEG = -1e30
F32 = jnp.float32
BF16 = jnp.bfloat16


VMEM = pl.BlockSpec(memory_space=pltpu.VMEM)
SMEM = pl.BlockSpec(memory_space=pltpu.SMEM)
HBM = pl.BlockSpec(memory_space=pltpu.HBM)


def params(mib=48):
    return pltpu.CompilerParams(vmem_limit_bytes=mib << 20)


def cost(flops, nbytes):
    return pl.CostEstimate(flops=flops, bytes_accessed=nbytes, transcendentals=0)


def chain_of(iota):
    return (iota // BLK) % 2


def nn(a, b, **kw):
    return lax.dot_general(a, b, (((1,), (0,)), ((), ())), preferred_element_type=F32, **kw)


def nt(a, b, **kw):
    return lax.dot_general(a, b, (((1,), (1,)), ((), ())), preferred_element_type=F32, **kw)


def by_chain(x):
    rows = x.shape[0]
    chain = chain_of(lax.broadcasted_iota(jnp.int32, (rows, DK), 0))
    zero = jnp.zeros_like(x)
    return jnp.concatenate([jnp.where(chain == 0, x, zero), jnp.where(chain == 1, x, zero)], axis=1)


def split3(x):
    hi = x.astype(BF16)
    rest = x - hi.astype(F32)
    mid = rest.astype(BF16)
    return hi, mid, (rest - mid.astype(F32)).astype(BF16)


def read_message(x):
    state = x[:ROWS].astype(F32)
    tail = x[ROWS:].astype(F32)
    total = tail[0:PAIRS] + tail[PAIRS : 2 * PAIRS] + tail[2 * PAIRS : 3 * PAIRS]
    return state, total


def spread(total):
    return jnp.concatenate(
        [jnp.broadcast_to(total[p : p + 1], (DK, total.shape[1])) for p in range(PAIRS)], axis=0
    )


def write_message(ref, state, total):
    ref[:ROWS, :] = state.astype(BF16)
    hi, mid, lo = split3(total)
    pad = jnp.zeros((TAIL - 3 * PAIRS, total.shape[1]), F32)
    ref[ROWS:, :] = jnp.concatenate(
        [hi.astype(F32), mid.astype(F32), lo.astype(F32), pad], axis=0
    ).astype(BF16)


def decay_terms(ld):
    return jnp.concatenate([t.astype(F32) for t in split3(ld)], axis=0).astype(BF16)


def column_sums(mask, ld):
    x = nt(mask.astype(BF16), decay_terms(ld))
    return x[:, :H] + x[:, H : 2 * H] + x[:, 2 * H : 3 * H]


def row_sums(mask, ld):
    x = nt(decay_terms(ld), mask.astype(BF16))
    return x[:H] + x[H : 2 * H] + x[2 * H : 3 * H]


def position():
    lane = lax.rem(lax.axis_index("tm"), LANES)
    return lane // 2, lane & 1


def local_kernel(x_in, ld_in, wk_in, wv_in, idx_in, cnt_in, k_ref, v_ref, keep, give, pack, *rest):
    chunks, x_ref, ld_ref, bk, bv, idx, cnt, sems = rest
    rows = x_ref.shape[0]
    copies = [
        pltpu.make_async_copy(src, dst, sems.at[i])
        for i, (src, dst) in enumerate(
            (
                (ld_in, ld_ref),
                (x_in, x_ref),
                (wk_in, bk),
                (wv_in, bv),
                (idx_in, idx),
                (cnt_in, cnt),
            )
        )
    ]
    for copy in copies:
        copy.start()
    t = lax.broadcasted_iota(jnp.int32, (rows, rows), 0)
    s = lax.broadcasted_iota(jnp.int32, (rows, rows), 1)
    after = ((s > t) & (chain_of(s) == chain_of(t))).astype(F32)
    copies[0].wait()
    ld = ld_ref[...]
    tail = jnp.exp(row_sums(after, ld))
    chain = chain_of(lax.broadcasted_iota(jnp.int32, ld.shape, 1))
    sums = [jnp.sum(jnp.where(chain == b, ld, 0.0), axis=1, keepdims=True) for b in (0, 1)]
    tails = [jnp.where(chain == b, tail, 0.0) for b in (0, 1)]
    copies[1].wait()
    copies[2].wait()
    x = x_ref[...]
    k = nn(x, bk[...]).astype(BF16)
    k_ref[...] = k
    turned = [
        jnp.transpose(k[:, q * HC * DK : (q + 1) * HC * DK].astype(F32)) for q in range(LANES)
    ]
    for copy in copies[3:]:
        copy.wait()
    v = nn(x, bv[...]).astype(BF16)
    v_ref[...] = v
    for q in range(LANES):
        states, totals = [], []
        for i in range(HC):
            h = q * HC + i
            kt = turned[q][i * DK : (i + 1) * DK]
            both = jnp.concatenate([(kt * tails[b][h : h + 1]).astype(BF16) for b in (0, 1)], axis=0)
            states.append(nn(both, v[:, h * DV : (h + 1) * DV]))
            totals += [jnp.broadcast_to(sums[b][h : h + 1], (1, DV)) for b in (0, 1)]
        write_message(
            chunks.at[q], jnp.concatenate(states, axis=0), jnp.concatenate(totals, axis=0)
        )
    _, core = position()
    for y in range(2):
        keep[y] = chunks[2 * y + core]
        give[y] = chunks[2 * y + 1 - core]
    frames, slots = idx.shape
    for f in range(frames):
        for i in range(slots):
            pack[f, i] = idx[f, i]
        pack[f, slots] = cnt[f]


def local(tokens, w_rk, w_rv, ld, index, live):
    rows, d = tokens.shape
    message = jax.ShapeDtypeStruct((2, ROWS + TAIL, DV), BF16)
    frames, slots = index.shape
    return pl.pallas_call(
        local_kernel,
        in_specs=[HBM] * 6,
        out_specs=[VMEM] * 4 + [SMEM],
        out_shape=[
            jax.ShapeDtypeStruct((rows, H * DK), BF16),
            jax.ShapeDtypeStruct((rows, H * DV), BF16),
            message,
            message,
            jax.ShapeDtypeStruct((frames, slots + 1), jnp.int32),
        ],
        scratch_shapes=[
            pltpu.VMEM((LANES, ROWS + TAIL, DV), BF16),
            pltpu.VMEM((rows, d), BF16),
            pltpu.VMEM((H, rows), F32),
            pltpu.VMEM((d, H * DK), BF16),
            pltpu.VMEM((d, H * DV), BF16),
            pltpu.SMEM((frames, slots), jnp.int32),
            pltpu.SMEM((frames,), jnp.int32),
            pltpu.SemaphoreType.DMA((6,)),
        ],
        compiler_params=params(62),
        name="local",
    )(tokens, ld, w_rk, w_rv, index, live)


def list_live(frames, distances, tables, groups):
    me = lax.axis_index("tm")
    lane = lax.rem(me, LANES)
    plane = me // LANES
    spans = len(distances)
    for part in range(spans):
        table, counts, need = tables[3 * part : 3 * part + 3]

        def clear(b, _, need=need, part=part):
            need[b] = (b < frames).astype(jnp.int32) if part == 0 else jnp.int32(0)
            return 0

        lax.fori_loop(0, need.shape[0], clear, 0)
        for g in range(2):
            for f in range(frames):
                counts[g * frames + f] = jnp.int32(1 if part == 0 and g == 0 else 0)
                if part == 0 and g == 0:
                    table[f, 0] = jnp.int32(f)
    for g, index in enumerate(groups):
        slots = index.shape[1] - 1
        for f in range(frames):
            row = g * frames + f

            def visit(i, carry, index=index, f=f, row=row):
                frame = index[f, i]
                owner = frame // frames
                its = lax.rem(owner, LANES)
                here = (its // 2) == (lane // 2)
                distance = plane - owner // LANES
                for part, (low, high) in enumerate(distances):
                    table, counts, need = tables[3 * part : 3 * part + 3]

                    @pl.when(here & (distance >= low) & (distance < high))
                    def _(table=table, counts=counts, need=need, low=low):
                        block = ((distance - low) * 2 + ((its ^ lane) & 1)) * frames
                        block = block + lax.rem(frame, frames)
                        n = counts[row]
                        table[row, n] = block
                        need[block] = 1
                        counts[row] = n + 1

                return carry

            lax.fori_loop(0, jnp.minimum(index[f, slots], slots), visit, 0)


def inner_kernel(frames, distances, *refs):
    x_in, ld_ref, k_in, v_in, pack, other, wq_in = refs[:7]
    inner_ref, qq_ref = refs[7:9]
    tables, (x_ref, k_ref, v_ref, bq, sems) = refs[9:-5], refs[-5:]
    copies = [
        pltpu.make_async_copy(src, dst, sems.at[i])
        for i, (src, dst) in enumerate(
            ((x_in, x_ref), (wq_in, bq), (k_in, k_ref), (v_in, v_ref))
        )
    ]
    for copy in copies:
        copy.start()
    list_live(frames, distances, tables, (pack, other))
    rows = x_in.shape[0]
    ld = ld_ref[...]
    t = lax.broadcasted_iota(jnp.int32, (rows, rows), 0)
    s = lax.broadcasted_iota(jnp.int32, (rows, rows), 1)
    upto = (s <= t) & (chain_of(s) == chain_of(t))
    ones = upto.astype(F32)
    column = column_sums(ones, ld)
    row = row_sums(ones, ld)
    grown = jnp.exp(column) * DK**-0.5
    for copy in copies:
        copy.wait()
    q = nn(x_ref[...], bq[...]).astype(BF16)
    for h in range(H):
        qh = q[:, h * DK : (h + 1) * DK]
        gap = column[:, h : h + 1] - row[h : h + 1, :]
        weight = jnp.exp(jnp.where(upto, gap, NEG)) * DK**-0.5
        scores = nt(qh, k_ref[:, h * DK : (h + 1) * DK]) * weight
        inner_ref[:, h * DV : (h + 1) * DV] = nn(
            scores.astype(BF16), v_ref[:, h * DV : (h + 1) * DV]
        )
        scaled = qh.astype(F32) * grown[:, h : h + 1]
        qq_ref[:, h * 2 * DK : (h + 1) * 2 * DK] = by_chain(scaled.astype(BF16))


def inner(tokens, w_rq, k, v, ld, pack, other, distances):
    rows, d = tokens.shape
    frames = rows // P_SIZE
    slots = pack.shape[1] - 1
    table_shapes = []
    for low, high in distances:
        table_shapes += [
            jax.ShapeDtypeStruct((2 * frames, slots + 1), jnp.int32),
            jax.ShapeDtypeStruct((2 * frames,), jnp.int32),
            jax.ShapeDtypeStruct(((high - low) * 2 * frames,), jnp.int32),
        ]
    out = pl.pallas_call(
        functools.partial(inner_kernel, frames, distances),
        in_specs=[HBM, VMEM, HBM, HBM, SMEM, SMEM, HBM],
        out_specs=[VMEM] * 2 + [SMEM] * len(table_shapes),
        out_shape=[
            jax.ShapeDtypeStruct((rows, H * DV), F32),
            jax.ShapeDtypeStruct((rows, H * 2 * DK), BF16),
        ]
        + table_shapes,
        scratch_shapes=[
            pltpu.VMEM((rows, d), BF16),
            pltpu.VMEM((rows, H * DK), BF16),
            pltpu.VMEM((rows, H * DV), BF16),
            pltpu.VMEM((d, H * DK), BF16),
            pltpu.SemaphoreType.DMA((4,)),
        ],
        compiler_params=params(48),
        cost_estimate=cost(2 * rows * d * H * DK, 8 << 20),
        name="inner",
    )(tokens, ld, k, v, pack, other, w_rq)
    return out[0], out[1], [out[2 + 3 * i : 5 + 3 * i] for i in range(len(distances))]


def join(first, second):
    return spread(jnp.exp(second[1])) * first[0] + second[0], first[1] + second[1]


def chip_kernel(keep, got, stay, send, ordered, results):
    y, core = position()
    ordered[core] = keep[...]
    ordered[1 - core] = got[...]
    for q in range(2):
        write_message(
            results.at[q], *join(read_message(ordered[0, q]), read_message(ordered[1, q]))
        )
    stay[...] = results[y]
    send[...] = results[1 - y]


def plane_kernel(stay, got, out, ordered):
    y, _ = position()
    ordered[y] = stay[...]
    ordered[1 - y] = got[...]
    write_message(out, *join(read_message(ordered[0]), read_message(ordered[1])))


def prefix_kernel(count, *refs):
    (stay, got), earlier = refs[:2], refs[2 : 2 + count]
    mine, send, ordered, results = refs[2 + count :]
    y, _ = position()
    plane = lax.axis_index("tm") // LANES
    ordered[y] = stay[...]
    ordered[1 - y] = got[...]
    state = jnp.zeros((ROWS, DV), F32)
    for distance in range(count, 0, -1):
        step, _ = join((state, 0.0), read_message(earlier[distance - 1][...]))
        state = jnp.where(plane >= distance, step, 0.0)
    results[0] = state.astype(BF16)
    results[1] = join((state, 0.0), read_message(ordered[0]))[0].astype(BF16)
    mine[...] = results[y]
    send[...] = results[1 - y]


def split_kernel(keep, local_got, mine, got, kept, give, ordered, both, results):
    y, core = position()
    ordered[core] = keep[...]
    ordered[1 - core] = local_got[...]
    both[y] = mine[...]
    both[1 - y] = got[...]
    for q in range(2):
        state = both[q]
        results[0, q] = state
        results[1, q] = join((state.astype(F32), 0.0), read_message(ordered[0, q]))[0].astype(BF16)
    kept[...] = results[core]
    give[...] = results[1 - core]


def small(kernel, outs, scratch, *args):
    return pl.pallas_call(
        kernel,
        in_specs=[VMEM] * len(args),
        out_specs=[VMEM] * len(outs),
        out_shape=[jax.ShapeDtypeStruct(shape, BF16) for shape in outs],
        scratch_shapes=[pltpu.VMEM(shape, BF16) for shape in scratch],
        compiler_params=params(8),
    )(*args)


def hidden_kernel(frames, *refs):
    inner_ref, qq_ref = refs[:2]
    kept, got = refs[2:4]
    x_ref, gain_ref, wq, wk, wv = refs[4:9]
    hid_ref, q_ref = refs[9:11]
    kv_refs = refs[11 : 11 + frames]
    ordered, bq, bk, bv, sems = refs[11 + frames :]
    copies = [
        pltpu.make_async_copy(src, dst, sems.at[i])
        for i, (src, dst) in enumerate(((wq, bq), (wk, bk), (wv, bv)))
    ]
    for copy in copies:
        copy.start()
    _, core = position()
    for y in range(2):
        ordered[2 * y + core] = kept[y]
        ordered[2 * y + 1 - core] = got[y]
    for h in range(H):
        cols = slice(h * DV, (h + 1) * DV)
        state = ordered[h // HC, (h % HC) * 2 * DK : (h % HC + 1) * 2 * DK, :]
        o = inner_ref[:, cols] + nn(qq_ref[:, h * 2 * DK : (h + 1) * 2 * DK], state)
        scale = lax.rsqrt(jnp.mean(o * o, axis=1, keepdims=True) + 1e-05)
        y = o * scale * gain_ref[:, cols]
        hid_ref[:, cols] = (x_ref[:, cols].astype(F32) + y).astype(BF16)
    hid = hid_ref[...]
    copies[0].wait()
    q_ref[...] = nn(hid, bq[...]).astype(BF16)
    for i, buf in ((1, bk), (2, bv)):
        copies[i].wait()
        part = nn(hid, buf[...]).astype(BF16)
        for f in range(frames):
            kv_refs[f][:, (i - 1) * MC : i * MC] = part[f * P_SIZE : (f + 1) * P_SIZE]


def hidden_of(inner_out, qq, states, tokens, gain, w_mq, w_mk, w_mv):
    rows, d = tokens.shape
    frames = rows // P_SIZE
    return pl.pallas_call(
        functools.partial(hidden_kernel, frames),
        in_specs=[VMEM] * 6 + [HBM] * 3,
        out_specs=[VMEM] * (2 + frames),
        out_shape=[
            jax.ShapeDtypeStruct((rows, d), BF16),
            jax.ShapeDtypeStruct((rows, MC), BF16),
        ]
        + [jax.ShapeDtypeStruct((P_SIZE, 2 * MC), BF16)] * frames,
        scratch_shapes=[pltpu.VMEM((LANES, ROWS, DV), BF16)]
        + [pltpu.VMEM((d, MC), BF16)] * 3
        + [pltpu.SemaphoreType.DMA((3,))],
        compiler_params=params(),
        name="hidden",
    )(inner_out, qq, *states, tokens, gain.reshape(1, d), w_mq, w_mk, w_mv)


def attend_kernel(frames, blocks, first, last, *refs):
    table, counts, need, q_ref, pq_ref = refs[:5]
    refs = refs[5:]
    if not first:
        acc_in, stat_in = refs[:2]
        refs = refs[2:]
    kv_refs = refs[:blocks]
    refs = refs[blocks:]
    if last:
        o_ref, po_ref, lse_ref, plse_ref = refs[:4]
        refs = refs[4:]
    else:
        acc_out, stat_out = refs[:2]
        refs = refs[2:]
    kv, scores, peak, total, acc, stat, sems = refs
    copies = [pltpu.make_async_copy(kv_refs[b], kv.at[b], sems.at[b]) for b in range(blocks)]
    for b in range(blocks):

        @pl.when(need[b] == 1)
        def _(b=b):
            copies[b].start()

    for b in range(blocks):

        @pl.when(need[b] == 1)
        def _(b=b):
            copies[b].wait()

    scale = MD**-0.5
    for row in range(2 * frames):
        queries = q_ref if row < frames else pq_ref
        f = row % frames
        span = slice(f * P_SIZE, (f + 1) * P_SIZE)
        held = slice(row * P_SIZE, (row + 1) * P_SIZE)
        n = counts[row]
        if first:
            stat[...] = jnp.zeros_like(stat)
            acc[...] = jnp.zeros_like(acc)
            peak[...] = jnp.full_like(peak, NEG)
        else:
            stat[...] = stat_in[held, :]
            for e in range(MH):
                acc[e] = acc_in[held, e * MD : (e + 1) * MD]

        @pl.when(n > 0)
        def _(row=row, queries=queries, span=span, n=n):
            if not first:
                for e in range(MH):
                    peak[e] = jnp.broadcast_to(stat[:, e : e + 1], (P_SIZE, P_SIZE))
            total[...] = jnp.zeros_like(total)
            half = (n + 1) // 2

            def score(i, _):
                b0 = table[row, 2 * i]
                more = 2 * i + 1 < n
                b1 = jnp.where(more, table[row, jnp.minimum(2 * i + 1, n - 1)], b0)
                for e in range(MH):
                    cols = slice(e * MD, (e + 1) * MD)
                    s0 = nt(queries[span, cols], kv[b0, :, cols])
                    s1 = nt(queries[span, cols], kv[b1, :, cols])
                    s1 = jnp.where(more, s1, NEG)
                    scores[2 * i, e] = s0
                    scores[2 * i + 1, e] = s1
                    peak[e] = jnp.maximum(peak[e], jnp.maximum(s0, s1))
                return 0

            lax.fori_loop(0, half, score, 0)
            for e in range(MH):
                top = jnp.max(peak[e], axis=1, keepdims=True)
                peak[e] = jnp.broadcast_to(top, (P_SIZE, P_SIZE))
                if not first:
                    fade = jnp.exp((stat[:, e : e + 1] - top) * scale)
                    acc[e] = acc[e] * fade
                    stat[:, MH + e : MH + e + 1] = stat[:, MH + e : MH + e + 1] * fade
                stat[:, e : e + 1] = top

            def weigh(i, _):
                b0 = table[row, 2 * i]
                b1 = table[row, jnp.minimum(2 * i + 1, n - 1)]
                for e in range(MH):
                    cols = slice(MC + e * MD, MC + (e + 1) * MD)
                    p0 = jnp.exp((scores[2 * i, e] - peak[e]) * scale)
                    p1 = jnp.exp((scores[2 * i + 1, e] - peak[e]) * scale)
                    total[e] += p0 + p1
                    acc[e] += nn(p0.astype(BF16), kv[b0, :, cols]) + nn(
                        p1.astype(BF16), kv[b1, :, cols]
                    )
                return 0

            lax.fori_loop(0, half, weigh, 0)
            for e in range(MH):
                stat[:, MH + e : MH + e + 1] += jnp.sum(total[e], axis=1, keepdims=True)

        if first:

            @pl.when(n == 0)
            def _():
                for e in range(MH):
                    stat[:, e : e + 1] = jnp.full((P_SIZE, 1), NEG, F32)

        if last:
            out, stats = (o_ref, lse_ref) if row < frames else (po_ref, plse_ref)
            for e in range(MH):
                l = jnp.maximum(stat[:, MH + e : MH + e + 1], 1e-30)
                out[span, e * MD : (e + 1) * MD] = (acc[e] / l).astype(out.dtype)
            flat = jnp.transpose(stat[...])
            low = jnp.log(jnp.maximum(flat[MH : 2 * MH], 1e-30))
            stats[:, span] = jnp.concatenate([flat[:MH] * scale + low, low], axis=0)
        else:
            stat_out[held, :] = stat[...]
            for e in range(MH):
                acc_out[held, e * MD : (e + 1) * MD] = acc[e]


def attend(tables, q, pq, kvs, state, last):
    rows = q.shape[0]
    frames = rows // P_SIZE
    blocks = len(kvs)
    slots = tables[0].shape[1]
    first = state is None
    state = [] if first else list(state)
    if last:
        out_shape = [
            jax.ShapeDtypeStruct((rows, MC), F32),
            jax.ShapeDtypeStruct((rows, MC), BF16),
            jax.ShapeDtypeStruct((2 * MH, rows), F32),
            jax.ShapeDtypeStruct((2 * MH, rows), F32),
        ]
    else:
        out_shape = [
            jax.ShapeDtypeStruct((2 * rows, MC), F32),
            jax.ShapeDtypeStruct((2 * rows, 128), F32),
        ]
    return pl.pallas_call(
        functools.partial(attend_kernel, frames, blocks, first, last),
        in_specs=[SMEM] * 3 + [VMEM] * (2 + len(state)) + [HBM] * blocks,
        out_specs=[VMEM] * len(out_shape),
        out_shape=out_shape,
        scratch_shapes=[
            pltpu.VMEM((blocks, P_SIZE, 2 * MC), BF16),
            pltpu.VMEM((slots + 2, MH, P_SIZE, P_SIZE), F32),
            pltpu.VMEM((MH, P_SIZE, P_SIZE), F32),
            pltpu.VMEM((MH, P_SIZE, P_SIZE), F32),
            pltpu.VMEM((MH, P_SIZE, MD), F32),
            pltpu.VMEM((P_SIZE, 128), F32),
            pltpu.SemaphoreType.DMA((blocks,)),
        ],
        compiler_params=params(),
        cost_estimate=cost(4 * 8 * frames * P_SIZE * P_SIZE * MC, blocks * P_SIZE * MC * 4),
        name="attend_last" if last else "attend",
    )(*tables, q, pq, *state, *kvs)


def output_kernel(o_ref, lse_ref, po_ref, plse_ref, hid_ref, w_ref, out_ref, mixed):
    rows = o_ref.shape[0]
    mine, other = lse_ref[...], plse_ref[...]
    top = jnp.maximum(mine, other)
    a, b = jnp.exp(mine - top), jnp.exp(other - top)
    inv = 1.0 / (a + b)
    both = jnp.concatenate([a * inv, b * inv, jnp.zeros((128 - 16, rows), F32)], axis=0)
    weights = jnp.transpose(both)
    for e in range(MH):
        cols = slice(e * MD, (e + 1) * MD)
        value = o_ref[:, cols] * weights[:, e : e + 1]
        value = value + po_ref[:, cols].astype(F32) * weights[:, 8 + e : 9 + e]
        mixed[:, cols] = value.astype(BF16)
    out_ref[...] = (hid_ref[...].astype(F32) + nn(mixed[...], w_ref[...])).astype(BF16)


def output(o, lse, po, plse, hid, w_out):
    rows, d = hid.shape
    return pl.pallas_call(
        output_kernel,
        in_specs=[VMEM] * 6,
        out_specs=VMEM,
        out_shape=jax.ShapeDtypeStruct((rows, d), BF16),
        scratch_shapes=[pltpu.VMEM((rows, MC), BF16)],
        compiler_params=params(),
        name="output",
    )(o, lse, po, plse, hid, w_out)


def on_device(
    tokens, log_decay, mem_index, mem_count, w_rq, w_rk, w_rv, norm_gain, w_mq, w_mk, w_mv, w_out
):
    size = lax.axis_size("tm")
    planes = size // LANES

    def flip(x, bits):
        return lax.ppermute(x, "tm", [(i, i ^ bits) for i in range(size)])

    def up(x, distance):
        step = distance * LANES
        return lax.ppermute(x, "tm", [(i, (i + step) % size) for i in range(size)])

    message, chunk = (ROWS + TAIL, DV), (ROWS, DV)
    spans = ((0, planes - 1), (planes - 1, planes)) if planes > 1 else ((0, planes),)
    k, v, keep, give, pack = local(tokens, w_rk, w_rv, log_decay, mem_index, mem_count)
    core_got = flip(give, 1)
    other = flip(pack, 2)
    stay, send = small(
        chip_kernel, [message] * 2, [(2, 2) + message, (2,) + message], keep, core_got
    )
    column_got = flip(send, 2)
    (total,) = small(plane_kernel, [message], [(2,) + message], stay, column_got)
    earlier = [up(total, d) for d in range(1, planes)]
    inner_out, qq, tables = inner(tokens, w_rq, k, v, log_decay, pack, other, spans)
    mine, send = small(
        functools.partial(prefix_kernel, len(earlier)),
        [chunk] * 2,
        [(2,) + message, (2,) + chunk],
        stay,
        column_got,
        *earlier,
    )
    column_back = flip(send, 2)
    kept, give = small(
        split_kernel,
        [(2,) + chunk] * 2,
        [(2, 2) + message, (2,) + chunk, (2, 2) + chunk],
        keep,
        core_got,
        mine,
        column_back,
    )
    states = (kept, flip(give, 1))
    hid, q, *kv = hidden_of(inner_out, qq, states, tokens, norm_gain, w_mq, w_mk, w_mv)
    partner_q = flip(q, 2)
    held = []
    for distance in range(planes):
        if distance:
            moved = []
            for x in kv:
                moved.append(up(x, 1))
            kv = moved
        near = []
        for x in kv:
            near.append(flip(x, 1))
        held.append(kv + near)
    state = None
    for (low, high), table in zip(spans, tables):
        blocks = [x for group in held[low:high] for x in group]
        state = attend(table, q, partner_q, blocks, state, high == planes)
    o, po, lse, plse = state
    return output(o, lse, flip(po, 2), flip(plse, 2), hid, w_out)


def solution(mesh):
    placed = (
        P(("groups", "tm"), None),
        P(None, ("groups", "tm")),
        P(("groups", "tm"), None),
        P(("groups", "tm")),
        P(),
        P(),
        P(),
        P(),
        P(),
        P(),
        P(),
        P(),
    )

    return jax.shard_map(
        on_device, mesh=mesh, in_specs=placed, out_specs=P(("groups", "tm"), None), check_vma=False
    )
```

```python
import functools

import jax
import jax.numpy as jnp
from jax import lax
from jax.experimental import pallas as pl
from jax.experimental.pallas import tpu as pltpu
from jax.sharding import PartitionSpec as P


H = 8
DK = 64
DV = 128
MH = 4
MD = 128
MC = 512
P_SIZE = 128
BLK = 64
LANES = 4
HC = H // LANES
ROWS = HC * 2 * DK
TAIL = 16
PAIRS = HC * 2
NEG = -1e30
F32 = jnp.float32
BF16 = jnp.bfloat16


VMEM = pl.BlockSpec(memory_space=pltpu.VMEM)
SMEM = pl.BlockSpec(memory_space=pltpu.SMEM)
HBM = pl.BlockSpec(memory_space=pltpu.HBM)


def params(mib=48):
    return pltpu.CompilerParams(vmem_limit_bytes=mib << 20)


def cost(flops, nbytes):
    return pl.CostEstimate(flops=flops, bytes_accessed=nbytes, transcendentals=0)


def chain_of(iota):
    return (iota // BLK) % 2


def nn(a, b, **kw):
    return lax.dot_general(a, b, (((1,), (0,)), ((), ())), preferred_element_type=F32, **kw)


def nt(a, b, **kw):
    return lax.dot_general(a, b, (((1,), (1,)), ((), ())), preferred_element_type=F32, **kw)


def by_chain(x):
    rows = x.shape[0]
    chain = chain_of(lax.broadcasted_iota(jnp.int32, (rows, DK), 0))
    zero = jnp.zeros_like(x)
    return jnp.concatenate([jnp.where(chain == 0, x, zero), jnp.where(chain == 1, x, zero)], axis=1)


def split3(x):
    hi = x.astype(BF16)
    rest = x - hi.astype(F32)
    mid = rest.astype(BF16)
    return hi, mid, (rest - mid.astype(F32)).astype(BF16)


def read_message(x):
    state = x[:ROWS].astype(F32)
    tail = x[ROWS:].astype(F32)
    total = tail[0:PAIRS] + tail[PAIRS : 2 * PAIRS] + tail[2 * PAIRS : 3 * PAIRS]
    return state, total


def spread(total):
    return jnp.concatenate(
        [jnp.broadcast_to(total[p : p + 1], (DK, total.shape[1])) for p in range(PAIRS)], axis=0
    )


def write_message(ref, state, total):
    ref[:ROWS, :] = state.astype(BF16)
    hi, mid, lo = split3(total)
    pad = jnp.zeros((TAIL - 3 * PAIRS, total.shape[1]), F32)
    ref[ROWS:, :] = jnp.concatenate(
        [hi.astype(F32), mid.astype(F32), lo.astype(F32), pad], axis=0
    ).astype(BF16)


def decay_terms(ld):
    return jnp.concatenate([t.astype(F32) for t in split3(ld)], axis=0).astype(BF16)


def column_sums(mask, ld):
    x = nt(mask.astype(BF16), decay_terms(ld))
    return x[:, :H] + x[:, H : 2 * H] + x[:, 2 * H : 3 * H]


def row_sums(mask, ld):
    x = nt(decay_terms(ld), mask.astype(BF16))
    return x[:H] + x[H : 2 * H] + x[2 * H : 3 * H]


def position():
    lane = lax.rem(lax.axis_index("tm"), LANES)
    return lane // 2, lane & 1


def local_kernel(x_in, ld_in, wk_in, wv_in, idx_in, cnt_in, k_ref, v_ref, keep, give, pack, *rest):
    chunks, x_ref, ld_ref, bk, bv, idx, cnt, sems = rest
    rows = x_ref.shape[0]
    copies = [
        pltpu.make_async_copy(src, dst, sems.at[i])
        for i, (src, dst) in enumerate(
            (
                (ld_in, ld_ref),
                (x_in, x_ref),
                (wk_in, bk),
                (wv_in, bv),
                (idx_in, idx),
                (cnt_in, cnt),
            )
        )
    ]
    for copy in copies:
        copy.start()
    t = lax.broadcasted_iota(jnp.int32, (rows, rows), 0)
    s = lax.broadcasted_iota(jnp.int32, (rows, rows), 1)
    after = ((s > t) & (chain_of(s) == chain_of(t))).astype(F32)
    copies[0].wait()
    ld = ld_ref[...]
    tail = jnp.exp(row_sums(after, ld))
    chain = chain_of(lax.broadcasted_iota(jnp.int32, ld.shape, 1))
    sums = [jnp.sum(jnp.where(chain == b, ld, 0.0), axis=1, keepdims=True) for b in (0, 1)]
    tails = [jnp.where(chain == b, tail, 0.0) for b in (0, 1)]
    copies[1].wait()
    copies[2].wait()
    x = x_ref[...]
    k = nn(x, bk[...]).astype(BF16)
    k_ref[...] = k
    turned = [
        jnp.transpose(k[:, q * HC * DK : (q + 1) * HC * DK].astype(F32)) for q in range(LANES)
    ]
    for copy in copies[3:]:
        copy.wait()
    v = nn(x, bv[...]).astype(BF16)
    v_ref[...] = v
    for q in range(LANES):
        states, totals = [], []
        for i in range(HC):
            h = q * HC + i
            kt = turned[q][i * DK : (i + 1) * DK]
            both = jnp.concatenate([(kt * tails[b][h : h + 1]).astype(BF16) for b in (0, 1)], axis=0)
            states.append(nn(both, v[:, h * DV : (h + 1) * DV]))
            totals += [jnp.broadcast_to(sums[b][h : h + 1], (1, DV)) for b in (0, 1)]
        write_message(
            chunks.at[q], jnp.concatenate(states, axis=0), jnp.concatenate(totals, axis=0)
        )
    _, core = position()
    for y in range(2):
        keep[y] = chunks[2 * y + core]
        give[y] = chunks[2 * y + 1 - core]
    frames, slots = idx.shape
    for f in range(frames):
        for i in range(slots):
            pack[f, i] = idx[f, i]
        pack[f, slots] = cnt[f]


def local(tokens, w_rk, w_rv, ld, index, live):
    rows, d = tokens.shape
    message = jax.ShapeDtypeStruct((2, ROWS + TAIL, DV), BF16)
    frames, slots = index.shape
    return pl.pallas_call(
        local_kernel,
        in_specs=[HBM] * 6,
        out_specs=[VMEM] * 4 + [SMEM],
        out_shape=[
            jax.ShapeDtypeStruct((rows, H * DK), BF16),
            jax.ShapeDtypeStruct((rows, H * DV), BF16),
            message,
            message,
            jax.ShapeDtypeStruct((frames, slots + 1), jnp.int32),
        ],
        scratch_shapes=[
            pltpu.VMEM((LANES, ROWS + TAIL, DV), BF16),
            pltpu.VMEM((rows, d), BF16),
            pltpu.VMEM((H, rows), F32),
            pltpu.VMEM((d, H * DK), BF16),
            pltpu.VMEM((d, H * DV), BF16),
            pltpu.SMEM((frames, slots), jnp.int32),
            pltpu.SMEM((frames,), jnp.int32),
            pltpu.SemaphoreType.DMA((6,)),
        ],
        compiler_params=params(62),
        name="local",
    )(tokens, ld, w_rk, w_rv, index, live)


def list_live(frames, distances, tables, groups):
    me = lax.axis_index("tm")
    lane = lax.rem(me, LANES)
    plane = me // LANES
    spans = len(distances)
    for part in range(spans):
        table, counts, need = tables[3 * part : 3 * part + 3]

        def clear(b, _, need=need, part=part):
            need[b] = (b < frames).astype(jnp.int32) if part == 0 else jnp.int32(0)
            return 0

        lax.fori_loop(0, need.shape[0], clear, 0)
        for g in range(2):
            for f in range(frames):
                counts[g * frames + f] = jnp.int32(1 if part == 0 and g == 0 else 0)
                if part == 0 and g == 0:
                    table[f, 0] = jnp.int32(f)
    for g, index in enumerate(groups):
        slots = index.shape[1] - 1
        for f in range(frames):
            row = g * frames + f

            def visit(i, carry, index=index, f=f, row=row):
                frame = index[f, i]
                owner = frame // frames
                its = lax.rem(owner, LANES)
                here = (its // 2) == (lane // 2)
                distance = plane - owner // LANES
                for part, (low, high) in enumerate(distances):
                    table, counts, need = tables[3 * part : 3 * part + 3]

                    @pl.when(here & (distance >= low) & (distance < high))
                    def _(table=table, counts=counts, need=need, low=low):
                        block = ((distance - low) * 2 + ((its ^ lane) & 1)) * frames
                        block = block + lax.rem(frame, frames)
                        n = counts[row]
                        table[row, n] = block
                        need[block] = 1
                        counts[row] = n + 1

                return carry

            lax.fori_loop(0, jnp.minimum(index[f, slots], slots), visit, 0)


def inner_kernel(frames, distances, *refs):
    x_in, ld_ref, k_in, v_in, pack, other, wq_in = refs[:7]
    inner_ref, qq_ref = refs[7:9]
    tables, (x_ref, k_ref, v_ref, bq, sems) = refs[9:-5], refs[-5:]
    copies = [
        pltpu.make_async_copy(src, dst, sems.at[i])
        for i, (src, dst) in enumerate(
            ((x_in, x_ref), (wq_in, bq), (k_in, k_ref), (v_in, v_ref))
        )
    ]
    for copy in copies:
        copy.start()
    list_live(frames, distances, tables, (pack, other))
    rows = x_in.shape[0]
    ld = ld_ref[...]
    t = lax.broadcasted_iota(jnp.int32, (rows, rows), 0)
    s = lax.broadcasted_iota(jnp.int32, (rows, rows), 1)
    upto = (s <= t) & (chain_of(s) == chain_of(t))
    ones = upto.astype(F32)
    column = column_sums(ones, ld)
    row = row_sums(ones, ld)
    grown = jnp.exp(column) * DK**-0.5
    for copy in copies:
        copy.wait()
    q = nn(x_ref[...], bq[...]).astype(BF16)
    for h in range(H):
        qh = q[:, h * DK : (h + 1) * DK]
        gap = column[:, h : h + 1] - row[h : h + 1, :]
        weight = jnp.exp(jnp.where(upto, gap, NEG)) * DK**-0.5
        scores = nt(qh, k_ref[:, h * DK : (h + 1) * DK]) * weight
        inner_ref[:, h * DV : (h + 1) * DV] = nn(
            scores.astype(BF16), v_ref[:, h * DV : (h + 1) * DV]
        )
        scaled = qh.astype(F32) * grown[:, h : h + 1]
        qq_ref[:, h * 2 * DK : (h + 1) * 2 * DK] = by_chain(scaled.astype(BF16))


def inner(tokens, w_rq, k, v, ld, pack, other, distances):
    rows, d = tokens.shape
    frames = rows // P_SIZE
    slots = pack.shape[1] - 1
    table_shapes = []
    for low, high in distances:
        table_shapes += [
            jax.ShapeDtypeStruct((2 * frames, slots + 1), jnp.int32),
            jax.ShapeDtypeStruct((2 * frames,), jnp.int32),
            jax.ShapeDtypeStruct(((high - low) * 2 * frames,), jnp.int32),
        ]
    out = pl.pallas_call(
        functools.partial(inner_kernel, frames, distances),
        in_specs=[HBM, VMEM, HBM, HBM, SMEM, SMEM, HBM],
        out_specs=[VMEM] * 2 + [SMEM] * len(table_shapes),
        out_shape=[
            jax.ShapeDtypeStruct((rows, H * DV), F32),
            jax.ShapeDtypeStruct((rows, H * 2 * DK), BF16),
        ]
        + table_shapes,
        scratch_shapes=[
            pltpu.VMEM((rows, d), BF16),
            pltpu.VMEM((rows, H * DK), BF16),
            pltpu.VMEM((rows, H * DV), BF16),
            pltpu.VMEM((d, H * DK), BF16),
            pltpu.SemaphoreType.DMA((4,)),
        ],
        compiler_params=params(48),
        cost_estimate=cost(2 * rows * d * H * DK, 8 << 20),
        name="inner",
    )(tokens, ld, k, v, pack, other, w_rq)
    return out[0], out[1], [out[2 + 3 * i : 5 + 3 * i] for i in range(len(distances))]


def join(first, second):
    return spread(jnp.exp(second[1])) * first[0] + second[0], first[1] + second[1]


def chip_kernel(keep, got, stay, send, ordered, results):
    y, core = position()
    ordered[core] = keep[...]
    ordered[1 - core] = got[...]
    for q in range(2):
        write_message(
            results.at[q], *join(read_message(ordered[0, q]), read_message(ordered[1, q]))
        )
    stay[...] = results[y]
    send[...] = results[1 - y]


def plane_kernel(stay, got, out, ordered):
    y, _ = position()
    ordered[y] = stay[...]
    ordered[1 - y] = got[...]
    write_message(out, *join(read_message(ordered[0]), read_message(ordered[1])))


def prefix_kernel(count, *refs):
    (stay, got), earlier = refs[:2], refs[2 : 2 + count]
    mine, send, ordered, results = refs[2 + count :]
    y, _ = position()
    plane = lax.axis_index("tm") // LANES
    ordered[y] = stay[...]
    ordered[1 - y] = got[...]
    state = jnp.zeros((ROWS, DV), F32)
    for distance in range(count, 0, -1):
        step, _ = join((state, 0.0), read_message(earlier[distance - 1][...]))
        state = jnp.where(plane >= distance, step, 0.0)
    results[0] = state.astype(BF16)
    results[1] = join((state, 0.0), read_message(ordered[0]))[0].astype(BF16)
    mine[...] = results[y]
    send[...] = results[1 - y]


def split_kernel(keep, local_got, mine, got, kept, give, ordered, both, results):
    y, core = position()
    ordered[core] = keep[...]
    ordered[1 - core] = local_got[...]
    both[y] = mine[...]
    both[1 - y] = got[...]
    for q in range(2):
        state = both[q]
        results[0, q] = state
        results[1, q] = join((state.astype(F32), 0.0), read_message(ordered[0, q]))[0].astype(BF16)
    kept[...] = results[core]
    give[...] = results[1 - core]


def small(kernel, outs, scratch, *args):
    return pl.pallas_call(
        kernel,
        in_specs=[VMEM] * len(args),
        out_specs=[VMEM] * len(outs),
        out_shape=[jax.ShapeDtypeStruct(shape, BF16) for shape in outs],
        scratch_shapes=[pltpu.VMEM(shape, BF16) for shape in scratch],
        compiler_params=params(8),
    )(*args)


def hidden_kernel(frames, *refs):
    inner_ref, qq_ref = refs[:2]
    kept, got = refs[2:4]
    x_ref, gain_ref, wq, wk, wv = refs[4:9]
    hid_ref, q_ref = refs[9:11]
    kv_refs = refs[11 : 11 + frames]
    ordered, bq, bk, bv, sems = refs[11 + frames :]
    copies = [
        pltpu.make_async_copy(src, dst, sems.at[i])
        for i, (src, dst) in enumerate(((wq, bq), (wk, bk), (wv, bv)))
    ]
    for copy in copies:
        copy.start()
    _, core = position()
    for y in range(2):
        ordered[2 * y + core] = kept[y]
        ordered[2 * y + 1 - core] = got[y]
    for h in range(H):
        cols = slice(h * DV, (h + 1) * DV)
        state = ordered[h // HC, (h % HC) * 2 * DK : (h % HC + 1) * 2 * DK, :]
        o = inner_ref[:, cols] + nn(qq_ref[:, h * 2 * DK : (h + 1) * 2 * DK], state)
        scale = lax.rsqrt(jnp.mean(o * o, axis=1, keepdims=True) + 1e-05)
        y = o * scale * gain_ref[:, cols]
        hid_ref[:, cols] = (x_ref[:, cols].astype(F32) + y).astype(BF16)
    hid = hid_ref[...]
    copies[0].wait()
    q_ref[...] = nn(hid, bq[...]).astype(BF16)
    for i, buf in ((1, bk), (2, bv)):
        copies[i].wait()
        part = nn(hid, buf[...]).astype(BF16)
        for f in range(frames):
            kv_refs[f][:, (i - 1) * MC : i * MC] = part[f * P_SIZE : (f + 1) * P_SIZE]


def hidden_of(inner_out, qq, states, tokens, gain, w_mq, w_mk, w_mv):
    rows, d = tokens.shape
    frames = rows // P_SIZE
    return pl.pallas_call(
        functools.partial(hidden_kernel, frames),
        in_specs=[VMEM] * 6 + [HBM] * 3,
        out_specs=[VMEM] * (2 + frames),
        out_shape=[
            jax.ShapeDtypeStruct((rows, d), BF16),
            jax.ShapeDtypeStruct((rows, MC), BF16),
        ]
        + [jax.ShapeDtypeStruct((P_SIZE, 2 * MC), BF16)] * frames,
        scratch_shapes=[pltpu.VMEM((LANES, ROWS, DV), BF16)]
        + [pltpu.VMEM((d, MC), BF16)] * 3
        + [pltpu.SemaphoreType.DMA((3,))],
        compiler_params=params(),
        name="hidden",
    )(inner_out, qq, *states, tokens, gain.reshape(1, d), w_mq, w_mk, w_mv)


def list_assist(frames, reach, steps, planes, pack, table, counts, need):
    me = lax.axis_index("tm")
    lane = lax.rem(me, LANES)
    plane = me // LANES
    slots = pack.shape[1] - 1

    def clear(b, _):
        need[b] = jnp.int32(0)
        return 0

    lax.fori_loop(0, need.shape[0], clear, 0)
    for f in range(frames):
        counts[f] = jnp.int32(0)

        def visit(i, carry, f=f):
            frame = pack[f, i]
            owner = frame // frames
            distance = plane - owner // LANES

            @pl.when((distance >= 1) & (distance <= reach) & (plane + steps < planes))
            def _():
                block = ((distance - 1) * LANES + (lax.rem(owner, LANES) ^ lane)) * frames
                block = block + lax.rem(frame, frames)
                n = counts[f]
                table[f, n] = block
                need[block] = 1
                counts[f] = n + 1

            return carry

        lax.fori_loop(0, jnp.minimum(pack[f, slots], slots), visit, 0)


def attend_kernel(frames, blocks, groups, first, last, assist, *refs):
    if assist is None:
        table, counts, need = refs[:3]
        refs = refs[3:]
    else:
        pack, refs = refs[0], refs[1:]
        table, counts, need = refs[-3:]
        refs = refs[:-3]
        list_assist(frames, *assist, pack, table, counts, need)
    asked, refs = refs[:groups], refs[groups:]
    if not first:
        acc_in, stat_in = refs[:2]
        refs = refs[2:]
    kv_refs, refs = refs[:blocks], refs[blocks:]
    if last:
        outs, refs = refs[: 2 * groups], refs[2 * groups :]
    else:
        acc_out, stat_out = refs[:2]
        refs = refs[2:]
    kv, scores, peak, total, acc, stat, sems = refs
    copies = [pltpu.make_async_copy(kv_refs[b], kv.at[b], sems.at[b]) for b in range(blocks)]
    for b in range(blocks):

        @pl.when(need[b] == 1)
        def _(b=b):
            copies[b].start()

    for b in range(blocks):

        @pl.when(need[b] == 1)
        def _(b=b):
            copies[b].wait()

    scale = MD**-0.5
    for row in range(groups * frames):
        queries = asked[row // frames]
        f = row % frames
        span = slice(f * P_SIZE, (f + 1) * P_SIZE)
        held = slice(row * P_SIZE, (row + 1) * P_SIZE)
        n = counts[row]
        if first:
            stat[...] = jnp.zeros_like(stat)
            acc[...] = jnp.zeros_like(acc)
            peak[...] = jnp.full_like(peak, NEG)
        else:
            stat[...] = stat_in[held, :]
            for e in range(MH):
                acc[e] = acc_in[held, e * MD : (e + 1) * MD]

        @pl.when(n > 0)
        def _(row=row, queries=queries, span=span, n=n):
            if not first:
                for e in range(MH):
                    peak[e] = jnp.broadcast_to(stat[:, e : e + 1], (P_SIZE, P_SIZE))
            total[...] = jnp.zeros_like(total)
            half = (n + 1) // 2

            def score(i, _):
                b0 = table[row, 2 * i]
                more = 2 * i + 1 < n
                b1 = jnp.where(more, table[row, jnp.minimum(2 * i + 1, n - 1)], b0)
                for e in range(MH):
                    cols = slice(e * MD, (e + 1) * MD)
                    s0 = nt(queries[span, cols], kv[b0, :, cols])
                    s1 = nt(queries[span, cols], kv[b1, :, cols])
                    s1 = jnp.where(more, s1, NEG)
                    scores[2 * i, e] = s0
                    scores[2 * i + 1, e] = s1
                    peak[e] = jnp.maximum(peak[e], jnp.maximum(s0, s1))
                return 0

            lax.fori_loop(0, half, score, 0)
            for e in range(MH):
                top = jnp.max(peak[e], axis=1, keepdims=True)
                peak[e] = jnp.broadcast_to(top, (P_SIZE, P_SIZE))
                if not first:
                    fade = jnp.exp((stat[:, e : e + 1] - top) * scale)
                    acc[e] = acc[e] * fade
                    stat[:, MH + e : MH + e + 1] = stat[:, MH + e : MH + e + 1] * fade
                stat[:, e : e + 1] = top

            def weigh(i, _):
                b0 = table[row, 2 * i]
                b1 = table[row, jnp.minimum(2 * i + 1, n - 1)]
                for e in range(MH):
                    cols = slice(MC + e * MD, MC + (e + 1) * MD)
                    p0 = jnp.exp((scores[2 * i, e] - peak[e]) * scale)
                    p1 = jnp.exp((scores[2 * i + 1, e] - peak[e]) * scale)
                    total[e] += p0 + p1
                    acc[e] += nn(p0.astype(BF16), kv[b0, :, cols]) + nn(
                        p1.astype(BF16), kv[b1, :, cols]
                    )
                return 0

            lax.fori_loop(0, half, weigh, 0)
            for e in range(MH):
                stat[:, MH + e : MH + e + 1] += jnp.sum(total[e], axis=1, keepdims=True)

        if first:

            @pl.when(n == 0)
            def _():
                for e in range(MH):
                    stat[:, e : e + 1] = jnp.full((P_SIZE, 1), NEG, F32)

        if last:
            out, stats = outs[2 * (row // frames) : 2 * (row // frames) + 2]
            for e in range(MH):
                l = jnp.maximum(stat[:, MH + e : MH + e + 1], 1e-30)
                out[span, e * MD : (e + 1) * MD] = (acc[e] / l).astype(out.dtype)
            flat = jnp.transpose(stat[...])
            low = jnp.log(jnp.maximum(flat[MH : 2 * MH], 1e-30))
            stats[:, span] = jnp.concatenate([flat[:MH] * scale + low, low], axis=0)
        else:
            stat_out[held, :] = stat[...]
            for e in range(MH):
                acc_out[held, e * MD : (e + 1) * MD] = acc[e]


def attend(lists, asked, kvs, state, last, assist=None):
    rows = asked[0].shape[0]
    frames = rows // P_SIZE
    blocks = len(kvs)
    groups = len(asked)
    slots = lists[0].shape[1] - 1
    first = state is None
    state = [] if first else list(state)
    out_shape = []
    if last:
        for g in range(groups):
            stays = g == 0 and assist is None
            out_shape += [
                jax.ShapeDtypeStruct((rows, MC), F32 if stays else BF16),
                jax.ShapeDtypeStruct((2 * MH, rows), F32),
            ]
    else:
        out_shape = [
            jax.ShapeDtypeStruct((groups * rows, MC), F32),
            jax.ShapeDtypeStruct((groups * rows, 128), F32),
        ]
    scratch = [
        pltpu.VMEM((blocks, P_SIZE, 2 * MC), BF16),
        pltpu.VMEM((slots + 3, MH, P_SIZE, P_SIZE), F32),
        pltpu.VMEM((MH, P_SIZE, P_SIZE), F32),
        pltpu.VMEM((MH, P_SIZE, P_SIZE), F32),
        pltpu.VMEM((MH, P_SIZE, MD), F32),
        pltpu.VMEM((P_SIZE, 128), F32),
        pltpu.SemaphoreType.DMA((blocks,)),
    ]
    if assist is not None:
        scratch += [
            pltpu.SMEM((frames, slots + 1), jnp.int32),
            pltpu.SMEM((frames,), jnp.int32),
            pltpu.SMEM((blocks,), jnp.int32),
        ]
    return pl.pallas_call(
        functools.partial(attend_kernel, frames, blocks, groups, first, last, assist),
        in_specs=[SMEM] * len(lists) + [VMEM] * (groups + len(state)) + [HBM] * blocks,
        out_specs=[VMEM] * len(out_shape),
        out_shape=out_shape,
        scratch_shapes=scratch,
        compiler_params=params(),
        cost_estimate=cost(4 * 8 * frames * P_SIZE * P_SIZE * MC, blocks * P_SIZE * MC * 4),
        name="assist" if assist is not None else "attend_last" if last else "attend",
    )(*lists, *asked, *state, *kvs)


def output_kernel(parts, *refs):
    values, stats = refs[0 : 2 * parts : 2], refs[1 : 2 * parts : 2]
    hid_ref, w_ref, out_ref, mixed = refs[2 * parts :]
    rows = hid_ref.shape[0]
    logs = [ref[...] for ref in stats]
    top = functools.reduce(jnp.maximum, logs)
    shares = [jnp.exp(x - top) for x in logs]
    inv = 1.0 / functools.reduce(jnp.add, shares)
    pad = jnp.zeros((128 - parts * 2 * MH, rows), F32)
    weights = jnp.transpose(jnp.concatenate([x * inv for x in shares] + [pad], axis=0))
    for e in range(MH):
        cols = slice(e * MD, (e + 1) * MD)
        value = 0.0
        for i, ref in enumerate(values):
            at = i * 2 * MH + e
            value = value + ref[:, cols].astype(F32) * weights[:, at : at + 1]
        mixed[:, cols] = value.astype(BF16)
    out_ref[...] = (hid_ref[...].astype(F32) + nn(mixed[...], w_ref[...])).astype(BF16)


def output(parts, hid, w_out):
    rows, d = hid.shape
    flat = [x for part in parts for x in part]
    return pl.pallas_call(
        functools.partial(output_kernel, len(parts)),
        in_specs=[VMEM] * (len(flat) + 2),
        out_specs=VMEM,
        out_shape=jax.ShapeDtypeStruct((rows, d), BF16),
        scratch_shapes=[pltpu.VMEM((rows, MC), BF16)],
        compiler_params=params(),
        name="output",
    )(*flat, hid, w_out)


def on_device(
    tokens, log_decay, mem_index, mem_count, w_rq, w_rk, w_rv, norm_gain, w_mq, w_mk, w_mv, w_out
):
    size = lax.axis_size("tm")
    planes = size // LANES

    def flip(x, bits):
        return lax.ppermute(x, "tm", [(i, i ^ bits) for i in range(size)])

    def up(x, distance):
        step = distance * LANES
        return lax.ppermute(x, "tm", [(i, (i + step) % size) for i in range(size)])

    message, chunk = (ROWS + TAIL, DV), (ROWS, DV)
    steps, reach = reaches(planes)
    spans = ((0, steps), (steps, steps + 1)) if steps else ((0, 1),)
    k, v, keep, give, pack = local(tokens, w_rk, w_rv, log_decay, mem_index, mem_count)
    core_got = flip(give, 1)
    other = flip(pack, 2)
    stay, send = small(
        chip_kernel, [message] * 2, [(2, 2) + message, (2,) + message], keep, core_got
    )
    column_got = flip(send, 2)
    (total,) = small(plane_kernel, [message], [(2,) + message], stay, column_got)
    earlier = [up(total, d) for d in range(1, planes)]
    inner_out, qq, tables = inner(tokens, w_rq, k, v, log_decay, pack, other, spans)
    mine, send = small(
        functools.partial(prefix_kernel, len(earlier)),
        [chunk] * 2,
        [(2,) + message, (2,) + chunk],
        stay,
        column_got,
        *earlier,
    )
    column_back = flip(send, 2)
    kept, give = small(
        split_kernel,
        [(2,) + chunk] * 2,
        [(2, 2) + message, (2,) + chunk, (2, 2) + chunk],
        keep,
        core_got,
        mine,
        column_back,
    )
    states = (kept, flip(give, 1))
    hid, q, *kv = hidden_of(inner_out, qq, states, tokens, norm_gain, w_mq, w_mk, w_mv)

    def between(x, pairs):
        return lax.ppermute(
            x, "tm", [(a * LANES + i, b * LANES + i) for a, b in pairs for i in range(LANES)]
        )

    def onward(x, distance):
        pairs = [(p, p + 1) for p in range(distance - 1, planes - 1)]
        return between(x, pairs + [(p, p) for p in range(distance - 1)] + [(planes - 1, distance - 1)])

    partner_q = flip(q, 2)
    held, across = [], []
    for distance in range(steps + 1):
        if distance:
            kv = [onward(x, distance) for x in kv]
        near = [flip(x, 1) for x in kv]
        held.append(kv + near)
        if 1 <= distance <= reach:
            column = [flip(x, 2) for x in kv]
            both = [flip(x, 1) for x in column]
            across += kv + near + column + both
    parts = []
    if reach:
        helped = [(p, p + steps) for p in range(1, planes - steps)]
        down = [(b, a) for a, b in helped]
        rest = [(p, p) for p in range(planes) if all(p not in pair for pair in helped)]
        far_q = between(q, down)
        far_pack = between(pack, down)
        far = attend([far_pack], [far_q], across, None, True, (reach, steps, planes))
        whole = helped + down + rest
        parts = [[between(x, whole) for x in far]]
    state = None
    for (low, high), table in zip(spans, tables):
        blocks = [x for group in held[low:high] for x in group]
        state = attend(table, [q, partner_q], blocks, state, high == steps + 1)
    o, lse, po, plse = state
    back = [flip(po, 2), flip(plse, 2)]
    return output([[o, lse], back] + parts, hid, w_out)


def reaches(planes):
    steps = planes // 2
    return steps, planes - 1 - steps


def solution(mesh):
    placed = (
        P(("groups", "tm"), None),
        P(None, ("groups", "tm")),
        P(("groups", "tm"), None),
        P(("groups", "tm")),
        P(),
        P(),
        P(),
        P(),
        P(),
        P(),
        P(),
        P(),
    )

    return jax.shard_map(
        on_device, mesh=mesh, in_specs=placed, out_specs=P(("groups", "tm"), None), check_vma=False
    )
```

```python
import functools

import jax
import jax.numpy as jnp
from jax import lax
from jax.experimental import pallas as pl
from jax.experimental.pallas import tpu as pltpu
from jax.sharding import PartitionSpec as P


H = 8
DK = 64
DV = 128
MH = 4
MD = 128
MC = 512
P_SIZE = 128
BLK = 64
LANES = 4
HC = H // LANES
ROWS = HC * 2 * DK
TAIL = 16
PAIRS = HC * 2
NEG = -1e30
F32 = jnp.float32
BF16 = jnp.bfloat16


VMEM = pl.BlockSpec(memory_space=pltpu.VMEM)
SMEM = pl.BlockSpec(memory_space=pltpu.SMEM)
HBM = pl.BlockSpec(memory_space=pltpu.HBM)


def params(mib=48):
    return pltpu.CompilerParams(vmem_limit_bytes=mib << 20)


def cost(flops, nbytes):
    return pl.CostEstimate(flops=flops, bytes_accessed=nbytes, transcendentals=0)


def chain_of(iota):
    return (iota // BLK) % 2


def nn(a, b, **kw):
    return lax.dot_general(a, b, (((1,), (0,)), ((), ())), preferred_element_type=F32, **kw)


def nt(a, b, **kw):
    return lax.dot_general(a, b, (((1,), (1,)), ((), ())), preferred_element_type=F32, **kw)


def by_chain(x):
    rows = x.shape[0]
    chain = chain_of(lax.broadcasted_iota(jnp.int32, (rows, DK), 0))
    zero = jnp.zeros_like(x)
    return jnp.concatenate([jnp.where(chain == 0, x, zero), jnp.where(chain == 1, x, zero)], axis=1)


def split3(x):
    hi = x.astype(BF16)
    rest = x - hi.astype(F32)
    mid = rest.astype(BF16)
    return hi, mid, (rest - mid.astype(F32)).astype(BF16)


def read_message(x):
    state = x[:ROWS].astype(F32)
    tail = x[ROWS:].astype(F32)
    total = tail[0:PAIRS] + tail[PAIRS : 2 * PAIRS] + tail[2 * PAIRS : 3 * PAIRS]
    return state, total


def spread(total):
    return jnp.concatenate(
        [jnp.broadcast_to(total[p : p + 1], (DK, total.shape[1])) for p in range(PAIRS)], axis=0
    )


def write_message(ref, state, total):
    ref[:ROWS, :] = state.astype(BF16)
    hi, mid, lo = split3(total)
    pad = jnp.zeros((TAIL - 3 * PAIRS, total.shape[1]), F32)
    ref[ROWS:, :] = jnp.concatenate(
        [hi.astype(F32), mid.astype(F32), lo.astype(F32), pad], axis=0
    ).astype(BF16)


def decay_terms(ld):
    return jnp.concatenate([t.astype(F32) for t in split3(ld)], axis=0).astype(BF16)


def column_sums(mask, ld):
    x = nt(mask.astype(BF16), decay_terms(ld))
    return x[:, :H] + x[:, H : 2 * H] + x[:, 2 * H : 3 * H]


def row_sums(mask, ld):
    x = nt(decay_terms(ld), mask.astype(BF16))
    return x[:H] + x[H : 2 * H] + x[2 * H : 3 * H]


def position():
    lane = lax.rem(lax.axis_index("tm"), LANES)
    return lane // 2, lane & 1


def local_kernel(x_in, ld_in, wk_in, wv_in, idx_in, cnt_in, k_ref, v_ref, keep, give, pack, *rest):
    chunks, x_ref, ld_ref, bk, bv, idx, cnt, sems = rest
    rows = x_ref.shape[0]
    copies = [
        pltpu.make_async_copy(src, dst, sems.at[i])
        for i, (src, dst) in enumerate(
            (
                (ld_in, ld_ref),
                (x_in, x_ref),
                (wk_in, bk),
                (wv_in, bv),
                (idx_in, idx),
                (cnt_in, cnt),
            )
        )
    ]
    for copy in copies:
        copy.start()
    t = lax.broadcasted_iota(jnp.int32, (rows, rows), 0)
    s = lax.broadcasted_iota(jnp.int32, (rows, rows), 1)
    after = ((s > t) & (chain_of(s) == chain_of(t))).astype(F32)
    copies[0].wait()
    ld = ld_ref[...]
    tail = jnp.exp(row_sums(after, ld))
    chain = chain_of(lax.broadcasted_iota(jnp.int32, ld.shape, 1))
    sums = [jnp.sum(jnp.where(chain == b, ld, 0.0), axis=1, keepdims=True) for b in (0, 1)]
    tails = [jnp.where(chain == b, tail, 0.0) for b in (0, 1)]
    copies[1].wait()
    copies[2].wait()
    x = x_ref[...]
    k = nn(x, bk[...]).astype(BF16)
    k_ref[...] = k
    turned = [
        jnp.transpose(k[:, q * HC * DK : (q + 1) * HC * DK].astype(F32)) for q in range(LANES)
    ]
    for copy in copies[3:]:
        copy.wait()
    v = nn(x, bv[...]).astype(BF16)
    v_ref[...] = v
    for q in range(LANES):
        states, totals = [], []
        for i in range(HC):
            h = q * HC + i
            kt = turned[q][i * DK : (i + 1) * DK]
            both = jnp.concatenate([(kt * tails[b][h : h + 1]).astype(BF16) for b in (0, 1)], axis=0)
            states.append(nn(both, v[:, h * DV : (h + 1) * DV]))
            totals += [jnp.broadcast_to(sums[b][h : h + 1], (1, DV)) for b in (0, 1)]
        write_message(
            chunks.at[q], jnp.concatenate(states, axis=0), jnp.concatenate(totals, axis=0)
        )
    _, core = position()
    for y in range(2):
        keep[y] = chunks[2 * y + core]
        give[y] = chunks[2 * y + 1 - core]
    frames, slots = idx.shape
    for f in range(frames):
        for i in range(slots):
            pack[f, i] = idx[f, i]
        pack[f, slots] = cnt[f]


def local(tokens, w_rk, w_rv, ld, index, live):
    rows, d = tokens.shape
    message = jax.ShapeDtypeStruct((2, ROWS + TAIL, DV), BF16)
    frames, slots = index.shape
    return pl.pallas_call(
        local_kernel,
        in_specs=[HBM] * 6,
        out_specs=[VMEM] * 4 + [SMEM],
        out_shape=[
            jax.ShapeDtypeStruct((rows, H * DK), BF16),
            jax.ShapeDtypeStruct((rows, H * DV), BF16),
            message,
            message,
            jax.ShapeDtypeStruct((frames, slots + 1), jnp.int32),
        ],
        scratch_shapes=[
            pltpu.VMEM((LANES, ROWS + TAIL, DV), BF16),
            pltpu.VMEM((rows, d), BF16),
            pltpu.VMEM((H, rows), F32),
            pltpu.VMEM((d, H * DK), BF16),
            pltpu.VMEM((d, H * DV), BF16),
            pltpu.SMEM((frames, slots), jnp.int32),
            pltpu.SMEM((frames,), jnp.int32),
            pltpu.SemaphoreType.DMA((6,)),
        ],
        compiler_params=params(62),
        name="local",
    )(tokens, ld, w_rk, w_rv, index, live)


def clear(flags):
    rows, blocks = flags.shape

    def one(i, _):
        flags[i // blocks, lax.rem(i, blocks)] = jnp.int32(0)
        return 0

    lax.fori_loop(0, rows * blocks, one, 0)


def each_live(frames, f, index, act):
    me = lax.axis_index("tm")
    slots = index.shape[1] - 1

    def visit(i, carry):
        frame = index[f, i]
        owner = frame // frames
        act(me // LANES - owner // LANES, lax.rem(owner, LANES), lax.rem(frame, frames))
        return carry

    lax.fori_loop(0, jnp.minimum(index[f, slots], slots), visit, 0)


def list_live(frames, distances, tables, groups):
    lane = lax.rem(lax.axis_index("tm"), LANES)
    for flags in tables:
        clear(flags)
    for g, index in enumerate(groups):
        for f in range(frames):
            row = g * frames + f
            if g == 0:
                tables[0][row, f] = jnp.int32(1)

            def act(distance, its, place, row=row):
                here = (its // 2) == (lane // 2)
                for flags, (low, high) in zip(tables, distances):

                    @pl.when(here & (distance >= low) & (distance < high))
                    def _(flags=flags, low=low):
                        block = ((distance - low) * 2 + ((its ^ lane) & 1)) * frames + place
                        flags[row, block] = jnp.int32(1)

            each_live(frames, f, index, act)


def inner_kernel(frames, distances, *refs):
    x_in, ld_ref, k_in, v_in, pack, other, wq_in = refs[:7]
    inner_ref, qq_ref = refs[7:9]
    tables, (x_ref, k_ref, v_ref, bq, sems) = refs[9:-5], refs[-5:]
    copies = [
        pltpu.make_async_copy(src, dst, sems.at[i])
        for i, (src, dst) in enumerate(
            ((x_in, x_ref), (wq_in, bq), (k_in, k_ref), (v_in, v_ref))
        )
    ]
    for copy in copies:
        copy.start()
    list_live(frames, distances, tables, (pack, other))
    rows = x_in.shape[0]
    ld = ld_ref[...]
    t = lax.broadcasted_iota(jnp.int32, (rows, rows), 0)
    s = lax.broadcasted_iota(jnp.int32, (rows, rows), 1)
    upto = (s <= t) & (chain_of(s) == chain_of(t))
    ones = upto.astype(F32)
    column = column_sums(ones, ld)
    row = row_sums(ones, ld)
    grown = jnp.exp(column) * DK**-0.5
    for copy in copies:
        copy.wait()
    q = nn(x_ref[...], bq[...]).astype(BF16)
    for h in range(H):
        qh = q[:, h * DK : (h + 1) * DK]
        gap = column[:, h : h + 1] - row[h : h + 1, :]
        weight = jnp.exp(jnp.where(upto, gap, NEG)) * DK**-0.5
        scores = nt(qh, k_ref[:, h * DK : (h + 1) * DK]) * weight
        inner_ref[:, h * DV : (h + 1) * DV] = nn(
            scores.astype(BF16), v_ref[:, h * DV : (h + 1) * DV]
        )
        scaled = qh.astype(F32) * grown[:, h : h + 1]
        qq_ref[:, h * 2 * DK : (h + 1) * 2 * DK] = by_chain(scaled.astype(BF16))


def inner(tokens, w_rq, k, v, ld, pack, other, distances):
    rows, d = tokens.shape
    frames = rows // P_SIZE
    table_shapes = [
        jax.ShapeDtypeStruct((2 * frames, (high - low) * 2 * frames), jnp.int32)
        for low, high in distances
    ]
    out = pl.pallas_call(
        functools.partial(inner_kernel, frames, distances),
        in_specs=[HBM, VMEM, HBM, HBM, SMEM, SMEM, HBM],
        out_specs=[VMEM] * 2 + [SMEM] * len(table_shapes),
        out_shape=[
            jax.ShapeDtypeStruct((rows, H * DV), F32),
            jax.ShapeDtypeStruct((rows, H * 2 * DK), BF16),
        ]
        + table_shapes,
        scratch_shapes=[
            pltpu.VMEM((rows, d), BF16),
            pltpu.VMEM((rows, H * DK), BF16),
            pltpu.VMEM((rows, H * DV), BF16),
            pltpu.VMEM((d, H * DK), BF16),
            pltpu.SemaphoreType.DMA((4,)),
        ],
        compiler_params=params(48),
        cost_estimate=cost(2 * rows * d * H * DK, 8 << 20),
        name="inner",
    )(tokens, ld, k, v, pack, other, w_rq)
    return out[0], out[1], out[2:]


def join(first, second):
    return spread(jnp.exp(second[1])) * first[0] + second[0], first[1] + second[1]


def chip_kernel(keep, got, stay, send, ordered, results):
    y, core = position()
    ordered[core] = keep[...]
    ordered[1 - core] = got[...]
    for q in range(2):
        write_message(
            results.at[q], *join(read_message(ordered[0, q]), read_message(ordered[1, q]))
        )
    stay[...] = results[y]
    send[...] = results[1 - y]


def plane_kernel(stay, got, out, ordered):
    y, _ = position()
    ordered[y] = stay[...]
    ordered[1 - y] = got[...]
    write_message(out, *join(read_message(ordered[0]), read_message(ordered[1])))


def prefix_kernel(count, *refs):
    (stay, got), earlier = refs[:2], refs[2 : 2 + count]
    mine, send, ordered, results = refs[2 + count :]
    y, _ = position()
    plane = lax.axis_index("tm") // LANES
    ordered[y] = stay[...]
    ordered[1 - y] = got[...]
    state = jnp.zeros((ROWS, DV), F32)
    for distance in range(count, 0, -1):
        step, _ = join((state, 0.0), read_message(earlier[distance - 1][...]))
        state = jnp.where(plane >= distance, step, 0.0)
    results[0] = state.astype(BF16)
    results[1] = join((state, 0.0), read_message(ordered[0]))[0].astype(BF16)
    mine[...] = results[y]
    send[...] = results[1 - y]


def split_kernel(keep, local_got, mine, got, kept, give, ordered, both, results):
    y, core = position()
    ordered[core] = keep[...]
    ordered[1 - core] = local_got[...]
    both[y] = mine[...]
    both[1 - y] = got[...]
    for q in range(2):
        state = both[q]
        results[0, q] = state
        results[1, q] = join((state.astype(F32), 0.0), read_message(ordered[0, q]))[0].astype(BF16)
    kept[...] = results[core]
    give[...] = results[1 - core]


def small(kernel, outs, scratch, *args):
    return pl.pallas_call(
        kernel,
        in_specs=[VMEM] * len(args),
        out_specs=[VMEM] * len(outs),
        out_shape=[jax.ShapeDtypeStruct(shape, BF16) for shape in outs],
        scratch_shapes=[pltpu.VMEM(shape, BF16) for shape in scratch],
        compiler_params=params(8),
    )(*args)


def hidden_kernel(frames, *refs):
    inner_ref, qq_ref = refs[:2]
    kept, got = refs[2:4]
    x_ref, gain_ref, wq, wk, wv = refs[4:9]
    hid_ref, q_ref = refs[9:11]
    kv_refs = refs[11 : 11 + frames]
    ordered, bq, bk, bv, sems = refs[11 + frames :]
    copies = [
        pltpu.make_async_copy(src, dst, sems.at[i])
        for i, (src, dst) in enumerate(((wq, bq), (wk, bk), (wv, bv)))
    ]
    for copy in copies:
        copy.start()
    _, core = position()
    for y in range(2):
        ordered[2 * y + core] = kept[y]
        ordered[2 * y + 1 - core] = got[y]
    for h in range(H):
        cols = slice(h * DV, (h + 1) * DV)
        state = ordered[h // HC, (h % HC) * 2 * DK : (h % HC + 1) * 2 * DK, :]
        o = inner_ref[:, cols] + nn(qq_ref[:, h * 2 * DK : (h + 1) * 2 * DK], state)
        scale = lax.rsqrt(jnp.mean(o * o, axis=1, keepdims=True) + 1e-05)
        y = o * scale * gain_ref[:, cols]
        hid_ref[:, cols] = (x_ref[:, cols].astype(F32) + y).astype(BF16)
    hid = hid_ref[...]
    copies[0].wait()
    q_ref[...] = nn(hid, bq[...]).astype(BF16)
    for i, buf in ((1, bk), (2, bv)):
        copies[i].wait()
        part = nn(hid, buf[...]).astype(BF16)
        for f in range(frames):
            kv_refs[f][:, (i - 1) * MC : i * MC] = part[f * P_SIZE : (f + 1) * P_SIZE]


def hidden_of(inner_out, qq, states, tokens, gain, w_mq, w_mk, w_mv):
    rows, d = tokens.shape
    frames = rows // P_SIZE
    return pl.pallas_call(
        functools.partial(hidden_kernel, frames),
        in_specs=[VMEM] * 6 + [HBM] * 3,
        out_specs=[VMEM] * (2 + frames),
        out_shape=[
            jax.ShapeDtypeStruct((rows, d), BF16),
            jax.ShapeDtypeStruct((rows, MC), BF16),
        ]
        + [jax.ShapeDtypeStruct((P_SIZE, 2 * MC), BF16)] * frames,
        scratch_shapes=[pltpu.VMEM((LANES, ROWS, DV), BF16)]
        + [pltpu.VMEM((d, MC), BF16)] * 3
        + [pltpu.SemaphoreType.DMA((3,))],
        compiler_params=params(),
        name="hidden",
    )(inner_out, qq, *states, tokens, gain.reshape(1, d), w_mq, w_mk, w_mv)


def list_assist(frames, at, steps, planes, index, flags):
    me = lax.axis_index("tm")
    clear(flags)
    for f in range(frames):

        def act(distance, its, place, f=f):
            @pl.when((distance == at) & (me // LANES + steps < planes))
            def _():
                flags[f, (its ^ lax.rem(me, LANES)) * frames + place] = jnp.int32(1)

        each_live(frames, f, index, act)


def attend_kernel(frames, blocks, groups, first, last, assist, *refs):
    if assist is None:
        live, refs = refs[0], refs[1:]
    else:
        index, live, refs = refs[0], refs[-1], refs[1:-1]
        list_assist(frames, *assist, index, live)
    asked, refs = refs[:groups], refs[groups:]
    if not first:
        acc_in, stat_in = refs[:2]
        refs = refs[2:]
    kv, refs = refs[:blocks], refs[blocks:]
    if last:
        outs, refs = refs[: 2 * groups], refs[2 * groups :]
    else:
        acc_out, stat_out = refs[:2]
        refs = refs[2:]
    scores, stat = refs
    rows = frames * P_SIZE
    scale = MD**-0.5
    base2 = scale * 1.4426950408889634
    pairs = [range(i, min(i + 2, blocks)) for i in range(0, blocks, 2)]
    spans = [slice(f * P_SIZE, (f + 1) * P_SIZE) for f in range(frames)]
    for g in range(groups):
        held = slice(g * rows, (g + 1) * rows)
        stat[...] = jnp.zeros_like(stat) if first else stat_in[held, :]
        for e in range(MH):
            cols, vcols = slice(e * MD, (e + 1) * MD), slice(MC + e * MD, MC + (e + 1) * MD)
            q = asked[g][:, cols]
            tops = [None] * frames
            for pair in pairs:
                s = nt(q, jnp.concatenate([kv[b][:, cols] for b in pair], axis=0))
                for j, b in enumerate(pair):
                    for f in range(frames):
                        part = s[spans[f], j * P_SIZE : (j + 1) * P_SIZE]
                        part = jnp.where(live[g * frames + f, b] == 1, part, NEG)
                        scores[spans[f], b * P_SIZE : (b + 1) * P_SIZE] = part
                        tops[f] = part if tops[f] is None else jnp.maximum(tops[f], part)
            top = jnp.concatenate([jnp.max(t, axis=1, keepdims=True) for t in tops], axis=0)
            top = jnp.maximum(top, 0.1 * NEG)
            if not first:
                before = stat[:, e : e + 1]
                top = jnp.maximum(top, before)
                fade = jnp.exp2((before - top) * base2)
            total, acc = None, None
            for pair in pairs:
                ps = []
                for b in pair:
                    p = jnp.exp2((scores[:, b * P_SIZE : (b + 1) * P_SIZE] - top) * base2)
                    total = p if total is None else total + p
                    ps.append(p.astype(BF16))
                part = nn(
                    jnp.concatenate(ps, axis=1),
                    jnp.concatenate([kv[b][:, vcols] for b in pair], axis=0),
                )
                acc = part if acc is None else acc + part
            total = jnp.sum(total, axis=1, keepdims=True)
            if not first:
                total = total + fade * stat[:, MH + e : MH + e + 1]
                acc = acc + fade * acc_in[held, cols]
            stat[:, e : e + 1] = top
            stat[:, MH + e : MH + e + 1] = total
            if last:
                outs[2 * g][:, cols] = (acc / jnp.maximum(total, 1e-30)).astype(outs[2 * g].dtype)
            else:
                acc_out[held, cols] = acc
        if last:
            flat = jnp.transpose(stat[...])
            low = jnp.log(jnp.maximum(flat[MH : 2 * MH], 1e-30))
            outs[2 * g + 1][...] = jnp.concatenate([flat[:MH] * scale + low, low], axis=0)
        else:
            stat_out[held, :] = stat[...]


def attend(lists, asked, kvs, state, last, assist=None):
    rows = asked[0].shape[0]
    frames = rows // P_SIZE
    blocks = len(kvs)
    groups = len(asked)
    first = state is None
    state = [] if first else list(state)
    out_shape = []
    if last:
        for g in range(groups):
            stays = g == 0 and assist is None
            out_shape += [
                jax.ShapeDtypeStruct((rows, MC), F32 if stays else BF16),
                jax.ShapeDtypeStruct((2 * MH, rows), F32),
            ]
    else:
        out_shape = [
            jax.ShapeDtypeStruct((groups * rows, MC), F32),
            jax.ShapeDtypeStruct((groups * rows, 128), F32),
        ]
    scratch = [pltpu.VMEM((rows, blocks * P_SIZE), F32), pltpu.VMEM((rows, 128), F32)]
    if assist is not None:
        scratch.append(pltpu.SMEM((frames, blocks), jnp.int32))
    return pl.pallas_call(
        functools.partial(attend_kernel, frames, blocks, groups, first, last, assist),
        in_specs=[SMEM] + [VMEM] * (groups + len(state) + blocks),
        out_specs=[VMEM] * len(out_shape),
        out_shape=out_shape,
        scratch_shapes=scratch,
        compiler_params=params(),
        cost_estimate=cost(4 * groups * blocks * rows * P_SIZE * MC, blocks * P_SIZE * MC * 4),
        name="assist" if assist is not None else "attend_last" if last else "attend",
    )(lists, *asked, *state, *kvs)


def output_kernel(parts, steps, *refs):
    values, stats = refs[0 : 2 * parts : 2], refs[1 : 2 * parts : 2]
    hid_ref, w_ref, out_ref, mixed = refs[2 * parts :]
    rows = hid_ref.shape[0]
    logs = [ref[...] for ref in stats]
    if parts > 2:
        logs[2] = jnp.where(lax.axis_index("tm") // LANES > steps, logs[2], NEG)
    top = functools.reduce(jnp.maximum, logs)
    shares = [jnp.exp(x - top) for x in logs]
    inv = 1.0 / functools.reduce(jnp.add, shares)
    pad = jnp.zeros((128 - parts * 2 * MH, rows), F32)
    weights = jnp.transpose(jnp.concatenate([x * inv for x in shares] + [pad], axis=0))
    for e in range(MH):
        cols = slice(e * MD, (e + 1) * MD)
        value = 0.0
        for i, ref in enumerate(values):
            at = i * 2 * MH + e
            value = value + ref[:, cols].astype(F32) * weights[:, at : at + 1]
        mixed[:, cols] = value.astype(BF16)
    out_ref[...] = (hid_ref[...].astype(F32) + nn(mixed[...], w_ref[...])).astype(BF16)


def output(parts, hid, w_out, steps):
    rows, d = hid.shape
    flat = [x for part in parts for x in part]
    return pl.pallas_call(
        functools.partial(output_kernel, len(parts), steps),
        in_specs=[VMEM] * (len(flat) + 2),
        out_specs=VMEM,
        out_shape=jax.ShapeDtypeStruct((rows, d), BF16),
        scratch_shapes=[pltpu.VMEM((rows, MC), BF16)],
        compiler_params=params(),
        name="output",
    )(*flat, hid, w_out)


def on_device(
    tokens, log_decay, mem_index, mem_count, w_rq, w_rk, w_rv, norm_gain, w_mq, w_mk, w_mv, w_out
):
    size = lax.axis_size("tm")
    planes = size // LANES

    def flip(x, bits):
        return lax.ppermute(x, "tm", [(i, i ^ bits) for i in range(size)])

    def up(x, distance):
        step = distance * LANES
        return lax.ppermute(x, "tm", [(i, (i + step) % size) for i in range(size)])

    message, chunk = (ROWS + TAIL, DV), (ROWS, DV)
    steps, reach = reaches(planes)
    spans = spans_of(steps)
    k, v, keep, give, pack = local(tokens, w_rk, w_rv, log_decay, mem_index, mem_count)
    core_got = flip(give, 1)
    other = flip(pack, 2)
    stay, send = small(
        chip_kernel, [message] * 2, [(2, 2) + message, (2,) + message], keep, core_got
    )
    column_got = flip(send, 2)
    (total,) = small(plane_kernel, [message], [(2,) + message], stay, column_got)
    earlier = [up(total, d) for d in range(1, planes)]
    inner_out, qq, tables = inner(tokens, w_rq, k, v, log_decay, pack, other, spans)
    mine, send = small(
        functools.partial(prefix_kernel, len(earlier)),
        [chunk] * 2,
        [(2,) + message, (2,) + chunk],
        stay,
        column_got,
        *earlier,
    )
    column_back = flip(send, 2)
    kept, give = small(
        split_kernel,
        [(2,) + chunk] * 2,
        [(2, 2) + message, (2,) + chunk, (2, 2) + chunk],
        keep,
        core_got,
        mine,
        column_back,
    )
    states = (kept, flip(give, 1))
    hid, q, *kv = hidden_of(inner_out, qq, states, tokens, norm_gain, w_mq, w_mk, w_mv)

    def between(x, pairs):
        return lax.ppermute(
            x, "tm", [(a * LANES + i, b * LANES + i) for a, b in pairs for i in range(LANES)]
        )

    def onward(x, distance):
        pairs = [(p, p + 1) for p in range(distance - 1, planes - 1)]
        return between(x, pairs + [(p, p) for p in range(distance - 1)] + [(planes - 1, distance - 1)])

    partner_q = flip(q, 2)
    held, across = [], []
    for distance in range(steps + 1):
        if distance:
            kv = [onward(x, distance) for x in kv]
        near = [flip(x, 1) for x in kv]
        held.append(kv + near)
        if 1 <= distance <= reach:
            column = [flip(x, 2) for x in kv]
            both = [flip(x, 1) for x in column]
            across.append(kv + near + column + both)
    parts = []
    if reach:
        helped = [(p, p + steps) for p in range(1, planes - steps)]
        down = [(b, a) for a, b in helped]
        far_q = between(q, down)
        far_pack = between(pack, down)
        far = None
        for at, blocks in enumerate(across, 1):
            far = attend(far_pack, [far_q], blocks, far, at == reach, (at, steps, planes))
        parts = [[between(x, helped) for x in far]]
    state = None
    for (low, high), table in zip(spans, tables):
        blocks = [x for group in held[low:high] for x in group]
        state = attend(table, [q, partner_q], blocks, state, high == steps + 1)
    o, lse, po, plse = state
    back = [flip(po, 2), flip(plse, 2)]
    return output([[o, lse], back] + parts, hid, w_out, steps)


def spans_of(steps):
    return [(low, min(low + 2, steps)) for low in range(0, steps, 2)] + [(steps, steps + 1)]


def reaches(planes):
    steps = planes // 2
    return steps, planes - 1 - steps


def solution(mesh):
    placed = (
        P(("groups", "tm"), None),
        P(None, ("groups", "tm")),
        P(("groups", "tm"), None),
        P(("groups", "tm")),
        P(),
        P(),
        P(),
        P(),
        P(),
        P(),
        P(),
        P(),
    )

    return jax.shard_map(
        on_device, mesh=mesh, in_specs=placed, out_specs=P(("groups", "tm"), None), check_vma=False
    )
```

```python
import functools

import jax
import jax.numpy as jnp
from jax import lax
from jax.experimental import pallas as pl
from jax.experimental.pallas import tpu as pltpu
from jax.sharding import PartitionSpec as P


H = 8
DK = 64
DV = 128
MH = 4
MD = 128
MC = 512
P_SIZE = 128
BLK = 64
LANES = 4
HC = H // LANES
ROWS = HC * 2 * DK
TAIL = 16
PAIRS = HC * 2
NEG = -1e30
F32 = jnp.float32
BF16 = jnp.bfloat16


VMEM = pl.BlockSpec(memory_space=pltpu.VMEM)
SMEM = pl.BlockSpec(memory_space=pltpu.SMEM)
HBM = pl.BlockSpec(memory_space=pltpu.HBM)


def params(mib=48):
    return pltpu.CompilerParams(vmem_limit_bytes=mib << 20)


def cost(flops, nbytes):
    return pl.CostEstimate(flops=flops, bytes_accessed=nbytes, transcendentals=0)


def chain_of(iota):
    return (iota // BLK) % 2


def nn(a, b, **kw):
    return lax.dot_general(a, b, (((1,), (0,)), ((), ())), preferred_element_type=F32, **kw)


def nt(a, b, **kw):
    return lax.dot_general(a, b, (((1,), (1,)), ((), ())), preferred_element_type=F32, **kw)


def by_chain(x):
    rows = x.shape[0]
    chain = chain_of(lax.broadcasted_iota(jnp.int32, (rows, DK), 0))
    zero = jnp.zeros_like(x)
    return jnp.concatenate([jnp.where(chain == 0, x, zero), jnp.where(chain == 1, x, zero)], axis=1)


def split3(x):
    hi = x.astype(BF16)
    rest = x - hi.astype(F32)
    mid = rest.astype(BF16)
    return hi, mid, (rest - mid.astype(F32)).astype(BF16)


def read_message(x):
    state = x[:ROWS].astype(F32)
    tail = x[ROWS:].astype(F32)
    total = tail[0:PAIRS] + tail[PAIRS : 2 * PAIRS] + tail[2 * PAIRS : 3 * PAIRS]
    return state, total


def spread(total):
    return jnp.concatenate(
        [jnp.broadcast_to(total[p : p + 1], (DK, total.shape[1])) for p in range(PAIRS)], axis=0
    )


def write_message(ref, state, total):
    ref[:ROWS, :] = state.astype(BF16)
    hi, mid, lo = split3(total)
    pad = jnp.zeros((TAIL - 3 * PAIRS, total.shape[1]), F32)
    ref[ROWS:, :] = jnp.concatenate(
        [hi.astype(F32), mid.astype(F32), lo.astype(F32), pad], axis=0
    ).astype(BF16)


def decay_terms(ld):
    return jnp.concatenate([t.astype(F32) for t in split3(ld)], axis=0).astype(BF16)


def column_sums(mask, ld):
    x = nt(mask.astype(BF16), decay_terms(ld))
    return x[:, :H] + x[:, H : 2 * H] + x[:, 2 * H : 3 * H]


def row_sums(mask, ld):
    x = nt(decay_terms(ld), mask.astype(BF16))
    return x[:H] + x[H : 2 * H] + x[2 * H : 3 * H]


def position():
    lane = lax.rem(lax.axis_index("tm"), LANES)
    return lane // 2, lane & 1


def local_kernel(x_in, ld_in, wk_in, wv_in, idx_in, cnt_in, k_ref, v_ref, keep, give, pack, *rest):
    chunks, x_ref, ld_ref, bk, bv, idx, cnt, sems = rest
    rows = x_ref.shape[0]
    copies = [
        pltpu.make_async_copy(src, dst, sems.at[i])
        for i, (src, dst) in enumerate(
            (
                (ld_in, ld_ref),
                (x_in, x_ref),
                (wk_in, bk),
                (wv_in, bv),
                (idx_in, idx),
                (cnt_in, cnt),
            )
        )
    ]
    for copy in copies:
        copy.start()
    t = lax.broadcasted_iota(jnp.int32, (rows, rows), 0)
    s = lax.broadcasted_iota(jnp.int32, (rows, rows), 1)
    after = ((s > t) & (chain_of(s) == chain_of(t))).astype(F32)
    copies[0].wait()
    ld = ld_ref[...]
    tail = jnp.exp(row_sums(after, ld))
    chain = chain_of(lax.broadcasted_iota(jnp.int32, ld.shape, 1))
    sums = [jnp.sum(jnp.where(chain == b, ld, 0.0), axis=1, keepdims=True) for b in (0, 1)]
    tails = [jnp.where(chain == b, tail, 0.0) for b in (0, 1)]
    copies[1].wait()
    copies[2].wait()
    x = x_ref[...]
    k = nn(x, bk[...]).astype(BF16)
    k_ref[...] = k
    turned = [
        jnp.transpose(k[:, q * HC * DK : (q + 1) * HC * DK].astype(F32)) for q in range(LANES)
    ]
    for copy in copies[3:]:
        copy.wait()
    v = nn(x, bv[...]).astype(BF16)
    v_ref[...] = v
    for q in range(LANES):
        states, totals = [], []
        for i in range(HC):
            h = q * HC + i
            kt = turned[q][i * DK : (i + 1) * DK]
            both = jnp.concatenate([(kt * tails[b][h : h + 1]).astype(BF16) for b in (0, 1)], axis=0)
            states.append(nn(both, v[:, h * DV : (h + 1) * DV]))
            totals += [jnp.broadcast_to(sums[b][h : h + 1], (1, DV)) for b in (0, 1)]
        write_message(
            chunks.at[q], jnp.concatenate(states, axis=0), jnp.concatenate(totals, axis=0)
        )
    _, core = position()
    for y in range(2):
        keep[y] = chunks[2 * y + core]
        give[y] = chunks[2 * y + 1 - core]
    frames, slots = idx.shape
    for f in range(frames):
        for i in range(slots):
            pack[f, i] = idx[f, i]
        pack[f, slots] = cnt[f]


def local(tokens, w_rk, w_rv, ld, index, live):
    rows, d = tokens.shape
    message = jax.ShapeDtypeStruct((2, ROWS + TAIL, DV), BF16)
    frames, slots = index.shape
    return pl.pallas_call(
        local_kernel,
        in_specs=[HBM] * 6,
        out_specs=[VMEM] * 4 + [SMEM],
        out_shape=[
            jax.ShapeDtypeStruct((rows, H * DK), BF16),
            jax.ShapeDtypeStruct((rows, H * DV), BF16),
            message,
            message,
            jax.ShapeDtypeStruct((frames, slots + 1), jnp.int32),
        ],
        scratch_shapes=[
            pltpu.VMEM((LANES, ROWS + TAIL, DV), BF16),
            pltpu.VMEM((rows, d), BF16),
            pltpu.VMEM((H, rows), F32),
            pltpu.VMEM((d, H * DK), BF16),
            pltpu.VMEM((d, H * DV), BF16),
            pltpu.SMEM((frames, slots), jnp.int32),
            pltpu.SMEM((frames,), jnp.int32),
            pltpu.SemaphoreType.DMA((6,)),
        ],
        compiler_params=params(62),
        name="local",
    )(tokens, ld, w_rk, w_rv, index, live)


def clear(flags):
    rows, blocks = flags.shape

    def one(i, _):
        flags[i // blocks, lax.rem(i, blocks)] = jnp.int32(0)
        return 0

    lax.fori_loop(0, rows * blocks, one, 0)


def each_live(frames, f, index, act):
    me = lax.axis_index("tm")
    slots = index.shape[1] - 1

    def visit(i, carry):
        frame = index[f, i]
        owner = frame // frames
        act(me // LANES - owner // LANES, lax.rem(owner, LANES), lax.rem(frame, frames))
        return carry

    lax.fori_loop(0, jnp.minimum(index[f, slots], slots), visit, 0)


def list_live(frames, distances, tables, groups):
    lane = lax.rem(lax.axis_index("tm"), LANES)
    for flags in tables:
        clear(flags)
    for g, index in enumerate(groups):
        for f in range(frames):
            row = g * frames + f
            if g == 0:
                tables[0][row, f] = jnp.int32(1)

            def act(distance, its, place, row=row):
                here = (its // 2) == (lane // 2)
                for flags, (low, high) in zip(tables, distances):

                    @pl.when(here & (distance >= low) & (distance < high))
                    def _(flags=flags, low=low):
                        block = ((distance - low) * 2 + ((its ^ lane) & 1)) * frames + place
                        flags[row, block] = jnp.int32(1)

            each_live(frames, f, index, act)


def inner_kernel(frames, distances, *refs):
    x_in, ld_ref, k_in, v_in, pack, other, wq_in = refs[:7]
    inner_ref, qq_ref = refs[7:9]
    tables, (x_ref, k_ref, v_ref, bq, sems) = refs[9:-5], refs[-5:]
    copies = [
        pltpu.make_async_copy(src, dst, sems.at[i])
        for i, (src, dst) in enumerate(
            ((x_in, x_ref), (wq_in, bq), (k_in, k_ref), (v_in, v_ref))
        )
    ]
    for copy in copies:
        copy.start()
    list_live(frames, distances, tables, (pack, other))
    rows = x_in.shape[0]
    ld = ld_ref[...]
    t = lax.broadcasted_iota(jnp.int32, (rows, rows), 0)
    s = lax.broadcasted_iota(jnp.int32, (rows, rows), 1)
    upto = (s <= t) & (chain_of(s) == chain_of(t))
    ones = upto.astype(F32)
    column = column_sums(ones, ld)
    row = row_sums(ones, ld)
    grown = jnp.exp(column) * DK**-0.5
    for copy in copies:
        copy.wait()
    q = nn(x_ref[...], bq[...]).astype(BF16)
    for h in range(H):
        qh = q[:, h * DK : (h + 1) * DK]
        gap = column[:, h : h + 1] - row[h : h + 1, :]
        weight = jnp.exp(jnp.where(upto, gap, NEG)) * DK**-0.5
        scores = nt(qh, k_ref[:, h * DK : (h + 1) * DK]) * weight
        inner_ref[:, h * DV : (h + 1) * DV] = nn(
            scores.astype(BF16), v_ref[:, h * DV : (h + 1) * DV]
        )
        scaled = qh.astype(F32) * grown[:, h : h + 1]
        qq_ref[:, h * 2 * DK : (h + 1) * 2 * DK] = by_chain(scaled.astype(BF16))


def inner(tokens, w_rq, k, v, ld, pack, other, distances):
    rows, d = tokens.shape
    frames = rows // P_SIZE
    table_shapes = [
        jax.ShapeDtypeStruct((2 * frames, (high - low) * 2 * frames), jnp.int32)
        for low, high in distances
    ]
    out = pl.pallas_call(
        functools.partial(inner_kernel, frames, distances),
        in_specs=[HBM, VMEM, HBM, HBM, SMEM, SMEM, HBM],
        out_specs=[VMEM] * 2 + [SMEM] * len(table_shapes),
        out_shape=[
            jax.ShapeDtypeStruct((rows, H * DV), F32),
            jax.ShapeDtypeStruct((rows, H * 2 * DK), BF16),
        ]
        + table_shapes,
        scratch_shapes=[
            pltpu.VMEM((rows, d), BF16),
            pltpu.VMEM((rows, H * DK), BF16),
            pltpu.VMEM((rows, H * DV), BF16),
            pltpu.VMEM((d, H * DK), BF16),
            pltpu.SemaphoreType.DMA((4,)),
        ],
        compiler_params=params(48),
        cost_estimate=cost(2 * rows * d * H * DK, 8 << 20),
        name="inner",
    )(tokens, ld, k, v, pack, other, w_rq)
    return out[0], out[1], out[2:]


def join(first, second):
    return spread(jnp.exp(second[1])) * first[0] + second[0], first[1] + second[1]


def chip_kernel(keep, got, stay, send, ordered, results):
    y, core = position()
    ordered[core] = keep[...]
    ordered[1 - core] = got[...]
    for q in range(2):
        write_message(
            results.at[q], *join(read_message(ordered[0, q]), read_message(ordered[1, q]))
        )
    stay[...] = results[y]
    send[...] = results[1 - y]


def plane_kernel(stay, got, out, ordered):
    y, _ = position()
    ordered[y] = stay[...]
    ordered[1 - y] = got[...]
    write_message(out, *join(read_message(ordered[0]), read_message(ordered[1])))


def prefix_kernel(count, *refs):
    (stay, got), earlier = refs[:2], refs[2 : 2 + count]
    mine, send, ordered, results = refs[2 + count :]
    y, _ = position()
    plane = lax.axis_index("tm") // LANES
    ordered[y] = stay[...]
    ordered[1 - y] = got[...]
    state = jnp.zeros((ROWS, DV), F32)
    for distance in range(count, 0, -1):
        step, _ = join((state, 0.0), read_message(earlier[distance - 1][...]))
        state = jnp.where(plane >= distance, step, 0.0)
    results[0] = state.astype(BF16)
    results[1] = join((state, 0.0), read_message(ordered[0]))[0].astype(BF16)
    mine[...] = results[y]
    send[...] = results[1 - y]


def split_kernel(keep, local_got, mine, got, kept, give, ordered, both, results):
    y, core = position()
    ordered[core] = keep[...]
    ordered[1 - core] = local_got[...]
    both[y] = mine[...]
    both[1 - y] = got[...]
    for q in range(2):
        state = both[q]
        results[0, q] = state
        results[1, q] = join((state.astype(F32), 0.0), read_message(ordered[0, q]))[0].astype(BF16)
    kept[...] = results[core]
    give[...] = results[1 - core]


def small(kernel, outs, scratch, *args):
    return pl.pallas_call(
        kernel,
        in_specs=[VMEM] * len(args),
        out_specs=[VMEM] * len(outs),
        out_shape=[jax.ShapeDtypeStruct(shape, BF16) for shape in outs],
        scratch_shapes=[pltpu.VMEM(shape, BF16) for shape in scratch],
        compiler_params=params(8),
    )(*args)


def hidden_kernel(frames, *refs):
    inner_ref, qq_ref = refs[:2]
    kept, got = refs[2:4]
    x_ref, gain_ref, wq, wk, wv = refs[4:9]
    hid_ref, q_ref = refs[9:11]
    kv_refs = refs[11 : 11 + frames]
    ordered, bq, bk, bv, sems = refs[11 + frames :]
    copies = [
        pltpu.make_async_copy(src, dst, sems.at[i])
        for i, (src, dst) in enumerate(((wq, bq), (wk, bk), (wv, bv)))
    ]
    for copy in copies:
        copy.start()
    _, core = position()
    for y in range(2):
        ordered[2 * y + core] = kept[y]
        ordered[2 * y + 1 - core] = got[y]
    for h in range(H):
        cols = slice(h * DV, (h + 1) * DV)
        state = ordered[h // HC, (h % HC) * 2 * DK : (h % HC + 1) * 2 * DK, :]
        o = inner_ref[:, cols] + nn(qq_ref[:, h * 2 * DK : (h + 1) * 2 * DK], state)
        scale = lax.rsqrt(jnp.mean(o * o, axis=1, keepdims=True) + 1e-05)
        y = o * scale * gain_ref[:, cols]
        hid_ref[:, cols] = (x_ref[:, cols].astype(F32) + y).astype(BF16)
    hid = hid_ref[...]
    copies[0].wait()
    q_ref[...] = nn(hid, bq[...]).astype(BF16)
    for i, buf in ((1, bk), (2, bv)):
        copies[i].wait()
        part = nn(hid, buf[...]).astype(BF16)
        for f in range(frames):
            kv_refs[f][:, (i - 1) * MC : i * MC] = part[f * P_SIZE : (f + 1) * P_SIZE]


def hidden_of(inner_out, qq, states, tokens, gain, w_mq, w_mk, w_mv):
    rows, d = tokens.shape
    frames = rows // P_SIZE
    return pl.pallas_call(
        functools.partial(hidden_kernel, frames),
        in_specs=[VMEM] * 6 + [HBM] * 3,
        out_specs=[VMEM] * (2 + frames),
        out_shape=[
            jax.ShapeDtypeStruct((rows, d), BF16),
            jax.ShapeDtypeStruct((rows, MC), BF16),
        ]
        + [jax.ShapeDtypeStruct((P_SIZE, 2 * MC), BF16)] * frames,
        scratch_shapes=[pltpu.VMEM((LANES, ROWS, DV), BF16)]
        + [pltpu.VMEM((d, MC), BF16)] * 3
        + [pltpu.SemaphoreType.DMA((3,))],
        compiler_params=params(),
        name="hidden",
    )(inner_out, qq, *states, tokens, gain.reshape(1, d), w_mq, w_mk, w_mv)


def list_assist(frames, at, steps, planes, index, flags):
    me = lax.axis_index("tm")
    clear(flags)
    for f in range(frames):

        def act(distance, its, place, f=f):
            @pl.when((distance == at) & (me // LANES + steps < planes))
            def _():
                flags[f, (its ^ lax.rem(me, LANES)) * frames + place] = jnp.int32(1)

        each_live(frames, f, index, act)


def attend_kernel(frames, blocks, row, first, last, assist, *refs):
    if assist is None:
        live, refs = refs[0], refs[1:]
    else:
        index, live, refs = refs[0], refs[-1], refs[1:-1]
    q_ref, refs = refs[0], refs[1:]
    if not first:
        acc_in, top_in, sum_in = refs[:3]
        refs = refs[3:]
    kv, refs = refs[:blocks], refs[blocks:]
    outs, (scores, stat) = refs[:-2], refs[-2:]
    rows = frames * P_SIZE
    scale = MD**-0.5
    base2 = scale * 1.4426950408889634
    pairs = [range(i, min(i + 2, blocks)) for i in range(0, blocks, 2)]
    spans = [slice(f * P_SIZE, (f + 1) * P_SIZE) for f in range(frames)]

    def run():
        if assist is not None:
            list_assist(frames, *assist, index, live)
        lane = lax.broadcasted_iota(jnp.int32, (rows, 128), 1)
        if last:
            stat[...] = jnp.zeros_like(stat)
        for e in range(MH):
            cols, vcols = slice(e * MD, (e + 1) * MD), slice(MC + e * MD, MC + (e + 1) * MD)
            held = slice(e * rows, (e + 1) * rows)
            q = q_ref[:, cols]
            tops = [None] * frames
            for pair in pairs:
                s = nt(q, jnp.concatenate([kv[b][:, cols] for b in pair], axis=0))
                for j, b in enumerate(pair):
                    for f in range(frames):
                        part = s[spans[f], j * P_SIZE : (j + 1) * P_SIZE]
                        part = jnp.where(live[row + f, b] == 1, part, NEG)
                        scores[spans[f], b * P_SIZE : (b + 1) * P_SIZE] = part
                        tops[f] = part if tops[f] is None else jnp.maximum(tops[f], part)
            top = jnp.concatenate([jnp.max(t, axis=1, keepdims=True) for t in tops], axis=0)
            top = jnp.broadcast_to(jnp.maximum(top, 0.1 * NEG), (rows, 128))
            if not first:
                before = top_in[held, :]
                top = jnp.maximum(top, before)
                fade = jnp.exp2((before - top) * base2)
            total, acc = None, None
            for pair in pairs:
                ps = []
                for b in pair:
                    p = jnp.exp2((scores[:, b * P_SIZE : (b + 1) * P_SIZE] - top) * base2)
                    total = p if total is None else total + p
                    ps.append(p.astype(BF16))
                part = nn(
                    jnp.concatenate(ps, axis=1),
                    jnp.concatenate([kv[b][:, vcols] for b in pair], axis=0),
                )
                acc = part if acc is None else acc + part
            if not first:
                total = total + fade * sum_in[held, :]
                acc = acc + fade * acc_in[:, cols]
            if last:
                whole = jnp.broadcast_to(jnp.sum(total, axis=1, keepdims=True), (rows, 128))
                whole = jnp.maximum(whole, 1e-30)
                outs[0][:, cols] = (acc / whole).astype(outs[0].dtype)
                stat[...] = jnp.where(
                    lane == e, top, jnp.where(lane == MH + e, whole, stat[...])
                )
            else:
                outs[0][:, cols] = acc
                outs[1][held, :] = top
                outs[2][held, :] = total
        if last:
            flat = jnp.transpose(stat[...])
            low = jnp.log(flat[MH : 2 * MH])
            outs[1][...] = jnp.concatenate([flat[:MH] * scale + low, low], axis=0)

    if assist is None:
        run()
    else:
        _, steps, planes = assist
        plane = lax.axis_index("tm") // LANES
        pl.when((plane >= 1) & (plane + steps < planes))(run)


def attend(lists, row, asked, kvs, state, last, dtype, assist=None):
    rows = asked.shape[0]
    frames = rows // P_SIZE
    blocks = len(kvs)
    first = state is None
    state = [] if first else list(state)
    if last:
        out_shape = [
            jax.ShapeDtypeStruct((rows, MC), dtype),
            jax.ShapeDtypeStruct((2 * MH, rows), F32),
        ]
    else:
        out_shape = [jax.ShapeDtypeStruct((rows, MC), F32)]
        out_shape += [jax.ShapeDtypeStruct((MH * rows, 128), F32)] * 2
    scratch = [pltpu.VMEM((rows, blocks * P_SIZE), F32), pltpu.VMEM((rows, 128), F32)]
    if assist is not None:
        scratch.append(pltpu.SMEM((frames, blocks), jnp.int32))
    return pl.pallas_call(
        functools.partial(attend_kernel, frames, blocks, row, first, last, assist),
        in_specs=[SMEM] + [VMEM] * (1 + len(state) + blocks),
        out_specs=[VMEM] * len(out_shape),
        out_shape=out_shape,
        scratch_shapes=scratch,
        compiler_params=params(),
        cost_estimate=cost(4 * blocks * rows * P_SIZE * MC, blocks * P_SIZE * MC * 4),
        name="assist" if assist is not None else "attend_last" if last else "attend",
    )(lists, asked, *state, *kvs)


def output_kernel(parts, steps, *refs):
    values, stats = refs[0 : 2 * parts : 2], refs[1 : 2 * parts : 2]
    hid_ref, w_ref, out_ref, mixed = refs[2 * parts :]
    rows = hid_ref.shape[0]
    logs = [ref[...] for ref in stats]
    if parts > 2:
        logs[2] = jnp.where(lax.axis_index("tm") // LANES > steps, logs[2], NEG)
    top = functools.reduce(jnp.maximum, logs)
    shares = [jnp.exp(x - top) for x in logs]
    inv = 1.0 / functools.reduce(jnp.add, shares)
    pad = jnp.zeros((128 - parts * 2 * MH, rows), F32)
    weights = jnp.transpose(jnp.concatenate([x * inv for x in shares] + [pad], axis=0))
    for e in range(MH):
        cols = slice(e * MD, (e + 1) * MD)
        value = 0.0
        for i, ref in enumerate(values):
            at = i * 2 * MH + e
            value = value + ref[:, cols].astype(F32) * weights[:, at : at + 1]
        mixed[:, cols] = value.astype(BF16)
    out_ref[...] = (hid_ref[...].astype(F32) + nn(mixed[...], w_ref[...])).astype(BF16)


def output(parts, hid, w_out, steps):
    rows, d = hid.shape
    flat = [x for part in parts for x in part]
    return pl.pallas_call(
        functools.partial(output_kernel, len(parts), steps),
        in_specs=[VMEM] * (len(flat) + 2),
        out_specs=VMEM,
        out_shape=jax.ShapeDtypeStruct((rows, d), BF16),
        scratch_shapes=[pltpu.VMEM((rows, MC), BF16)],
        compiler_params=params(),
        name="output",
    )(*flat, hid, w_out)


def on_device(
    tokens, log_decay, mem_index, mem_count, w_rq, w_rk, w_rv, norm_gain, w_mq, w_mk, w_mv, w_out
):
    size = lax.axis_size("tm")
    planes = size // LANES
    frames = tokens.shape[0] // P_SIZE

    def flip(x, bits):
        return lax.ppermute(x, "tm", [(i, i ^ bits) for i in range(size)])

    def up(x, distance):
        step = distance * LANES
        return lax.ppermute(x, "tm", [(i, (i + step) % size) for i in range(size)])

    message, chunk = (ROWS + TAIL, DV), (ROWS, DV)
    steps, reach = reaches(planes)
    spans = spans_of(steps)
    k, v, keep, give, pack = local(tokens, w_rk, w_rv, log_decay, mem_index, mem_count)
    core_got = flip(give, 1)
    other = flip(pack, 2)
    stay, send = small(
        chip_kernel, [message] * 2, [(2, 2) + message, (2,) + message], keep, core_got
    )
    column_got = flip(send, 2)
    (total,) = small(plane_kernel, [message], [(2,) + message], stay, column_got)
    earlier = [up(total, d) for d in range(1, planes)]
    inner_out, qq, tables = inner(tokens, w_rq, k, v, log_decay, pack, other, spans)
    mine, send = small(
        functools.partial(prefix_kernel, len(earlier)),
        [chunk] * 2,
        [(2,) + message, (2,) + chunk],
        stay,
        column_got,
        *earlier,
    )
    column_back = flip(send, 2)
    kept, give = small(
        split_kernel,
        [(2,) + chunk] * 2,
        [(2, 2) + message, (2,) + chunk, (2, 2) + chunk],
        keep,
        core_got,
        mine,
        column_back,
    )
    states = (kept, flip(give, 1))
    hid, q, *kv = hidden_of(inner_out, qq, states, tokens, norm_gain, w_mq, w_mk, w_mv)

    def between(x, pairs):
        return lax.ppermute(
            x, "tm", [(a * LANES + i, b * LANES + i) for a, b in pairs for i in range(LANES)]
        )

    def onward(x, distance):
        pairs = [(p, p + 1) for p in range(distance - 1, planes - 1)]
        return between(x, pairs + [(p, p) for p in range(distance - 1)] + [(planes - 1, distance - 1)])

    frames = len(kv)
    partner_q = flip(q, 2)
    held, across = [], []
    for distance in range(steps + 1):
        if distance:
            kv = [onward(x, distance) for x in kv]
        near = [flip(x, 1) for x in kv]
        held.append(kv + near)
        if 1 <= distance <= reach:
            column = [flip(x, 2) for x in kv]
            both = [flip(x, 1) for x in column]
            across.append(kv + near + column + both)
    parts = []
    if reach:
        helped = [(p, p + steps) for p in range(1, planes - steps)]
        down = [(b, a) for a, b in helped]
        far_q = between(q, down)
        far_pack = between(pack, down)
        far = None
        for at, blocks in enumerate(across, 1):
            far = attend(far_pack, 0, far_q, blocks, far, at == reach, BF16, (at, steps, planes))
        parts = [[between(x, helped) for x in far]]

    def attended(row, asked, dtype):
        state = None
        for (low, high), flags in zip(spans, tables):
            blocks = [x for group in held[low:high] for x in group]
            state = attend(flags, row, asked, blocks, state, high == steps + 1, dtype)
        return state

    theirs = attended(frames, partner_q, BF16)
    back = [flip(x, 2) for x in theirs]
    mine = attended(0, q, F32)
    return output([mine, back] + parts, hid, w_out, steps)


def spans_of(steps):
    return [(low, min(low + 2, steps)) for low in range(0, steps, 2)] + [(steps, steps + 1)]


def reaches(planes):
    steps = planes // 2
    return steps, planes - 1 - steps


def solution(mesh):
    placed = (
        P(("groups", "tm"), None),
        P(None, ("groups", "tm")),
        P(("groups", "tm"), None),
        P(("groups", "tm")),
        P(),
        P(),
        P(),
        P(),
        P(),
        P(),
        P(),
        P(),
    )

    return jax.shard_map(
        on_device, mesh=mesh, in_specs=placed, out_specs=P(("groups", "tm"), None), check_vma=False
    )
```

```python
import functools

import jax
import jax.numpy as jnp
from jax import lax
from jax.experimental import pallas as pl
from jax.experimental.pallas import tpu as pltpu
from jax.sharding import PartitionSpec as P


H = 8
DK = 64
DV = 128
MH = 4
MD = 128
MC = 512
P_SIZE = 128
BLK = 64
LANES = 4
HC = H // LANES
ROWS = HC * 2 * DK
TAIL = 16
PAIRS = HC * 2
NEG = -1e30
F32 = jnp.float32
BF16 = jnp.bfloat16


VMEM = pl.BlockSpec(memory_space=pltpu.VMEM)
SMEM = pl.BlockSpec(memory_space=pltpu.SMEM)
HBM = pl.BlockSpec(memory_space=pltpu.HBM)


def params(mib=48):
    return pltpu.CompilerParams(vmem_limit_bytes=mib << 20)


def cost(flops, nbytes):
    return pl.CostEstimate(flops=flops, bytes_accessed=nbytes, transcendentals=0)


def chain_of(iota):
    return (iota // BLK) % 2


def nn(a, b, **kw):
    return lax.dot_general(a, b, (((1,), (0,)), ((), ())), preferred_element_type=F32, **kw)


def nt(a, b, **kw):
    return lax.dot_general(a, b, (((1,), (1,)), ((), ())), preferred_element_type=F32, **kw)


def by_chain(x):
    rows = x.shape[0]
    chain = chain_of(lax.broadcasted_iota(jnp.int32, (rows, DK), 0))
    zero = jnp.zeros_like(x)
    return jnp.concatenate([jnp.where(chain == 0, x, zero), jnp.where(chain == 1, x, zero)], axis=1)


def split3(x):
    hi = x.astype(BF16)
    rest = x - hi.astype(F32)
    mid = rest.astype(BF16)
    return hi, mid, (rest - mid.astype(F32)).astype(BF16)


def read_message(x):
    state = x[:ROWS].astype(F32)
    tail = x[ROWS:].astype(F32)
    total = tail[0:PAIRS] + tail[PAIRS : 2 * PAIRS] + tail[2 * PAIRS : 3 * PAIRS]
    return state, total


def spread(total):
    return jnp.concatenate(
        [jnp.broadcast_to(total[p : p + 1], (DK, total.shape[1])) for p in range(PAIRS)], axis=0
    )


def write_message(ref, state, total):
    ref[:ROWS, :] = state.astype(BF16)
    hi, mid, lo = split3(total)
    pad = jnp.zeros((TAIL - 3 * PAIRS, total.shape[1]), F32)
    ref[ROWS:, :] = jnp.concatenate(
        [hi.astype(F32), mid.astype(F32), lo.astype(F32), pad], axis=0
    ).astype(BF16)


def decay_terms(ld):
    return jnp.concatenate([t.astype(F32) for t in split3(ld)], axis=0).astype(BF16)


def column_sums(mask, ld):
    x = nt(mask.astype(BF16), decay_terms(ld))
    return x[:, :H] + x[:, H : 2 * H] + x[:, 2 * H : 3 * H]


def row_sums(mask, ld):
    x = nt(decay_terms(ld), mask.astype(BF16))
    return x[:H] + x[H : 2 * H] + x[2 * H : 3 * H]


def position():
    lane = lax.rem(lax.axis_index("tm"), LANES)
    return lane // 2, lane & 1


def local_kernel(x_in, ld_in, wk_in, wv_in, idx_in, cnt_in, k_ref, v_ref, keep, give, pack, *rest):
    chunks, x_ref, ld_ref, bk, bv, idx, cnt, sems = rest
    rows = x_ref.shape[0]
    copies = [
        pltpu.make_async_copy(src, dst, sems.at[i])
        for i, (src, dst) in enumerate(
            (
                (ld_in, ld_ref),
                (x_in, x_ref),
                (wk_in, bk),
                (wv_in, bv),
                (idx_in, idx),
                (cnt_in, cnt),
            )
        )
    ]
    for copy in copies:
        copy.start()
    t = lax.broadcasted_iota(jnp.int32, (rows, rows), 0)
    s = lax.broadcasted_iota(jnp.int32, (rows, rows), 1)
    after = ((s > t) & (chain_of(s) == chain_of(t))).astype(F32)
    copies[0].wait()
    ld = ld_ref[...]
    tail = jnp.exp(row_sums(after, ld))
    chain = chain_of(lax.broadcasted_iota(jnp.int32, ld.shape, 1))
    sums = [jnp.sum(jnp.where(chain == b, ld, 0.0), axis=1, keepdims=True) for b in (0, 1)]
    tails = [jnp.where(chain == b, tail, 0.0) for b in (0, 1)]
    copies[1].wait()
    copies[2].wait()
    x = x_ref[...]
    k = nn(x, bk[...]).astype(BF16)
    k_ref[...] = k
    turned = [
        jnp.transpose(k[:, q * HC * DK : (q + 1) * HC * DK].astype(F32)) for q in range(LANES)
    ]
    for copy in copies[3:]:
        copy.wait()
    v = nn(x, bv[...]).astype(BF16)
    v_ref[...] = v
    for q in range(LANES):
        states, totals = [], []
        for i in range(HC):
            h = q * HC + i
            kt = turned[q][i * DK : (i + 1) * DK]
            both = jnp.concatenate([(kt * tails[b][h : h + 1]).astype(BF16) for b in (0, 1)], axis=0)
            states.append(nn(both, v[:, h * DV : (h + 1) * DV]))
            totals += [jnp.broadcast_to(sums[b][h : h + 1], (1, DV)) for b in (0, 1)]
        write_message(
            chunks.at[q], jnp.concatenate(states, axis=0), jnp.concatenate(totals, axis=0)
        )
    _, core = position()
    for y in range(2):
        keep[y] = chunks[2 * y + core]
        give[y] = chunks[2 * y + 1 - core]
    frames, slots = idx.shape
    for f in range(frames):
        for i in range(slots):
            pack[f, i] = idx[f, i]
        pack[f, slots] = cnt[f]


def local(tokens, w_rk, w_rv, ld, index, live):
    rows, d = tokens.shape
    message = jax.ShapeDtypeStruct((2, ROWS + TAIL, DV), BF16)
    frames, slots = index.shape
    return pl.pallas_call(
        local_kernel,
        in_specs=[HBM] * 6,
        out_specs=[VMEM] * 4 + [SMEM],
        out_shape=[
            jax.ShapeDtypeStruct((rows, H * DK), BF16),
            jax.ShapeDtypeStruct((rows, H * DV), BF16),
            message,
            message,
            jax.ShapeDtypeStruct((frames, slots + 1), jnp.int32),
        ],
        scratch_shapes=[
            pltpu.VMEM((LANES, ROWS + TAIL, DV), BF16),
            pltpu.VMEM((rows, d), BF16),
            pltpu.VMEM((H, rows), F32),
            pltpu.VMEM((d, H * DK), BF16),
            pltpu.VMEM((d, H * DV), BF16),
            pltpu.SMEM((frames, slots), jnp.int32),
            pltpu.SMEM((frames,), jnp.int32),
            pltpu.SemaphoreType.DMA((6,)),
        ],
        compiler_params=params(62),
        name="local",
    )(tokens, ld, w_rk, w_rv, index, live)


def clear(flags):
    rows, blocks = flags.shape

    def one(i, _):
        flags[i // blocks, lax.rem(i, blocks)] = jnp.int32(0)
        return 0

    lax.fori_loop(0, rows * blocks, one, 0)


def each_live(frames, f, index, act):
    me = lax.axis_index("tm")
    slots = index.shape[1] - 1

    def visit(i, carry):
        frame = index[f, i]
        owner = frame // frames
        act(me // LANES - owner // LANES, lax.rem(owner, LANES), lax.rem(frame, frames))
        return carry

    lax.fori_loop(0, jnp.minimum(index[f, slots], slots), visit, 0)


def list_live(frames, distances, tables, groups):
    lane = lax.rem(lax.axis_index("tm"), LANES)
    for flags in tables:
        clear(flags)
    for g, index in enumerate(groups):
        for f in range(frames):
            row = g * frames + f
            if g == 0:
                tables[0][row, f] = jnp.int32(1)

            def act(distance, its, place, row=row):
                here = (its // 2) == (lane // 2)
                for flags, (low, high) in zip(tables, distances):

                    @pl.when(here & (distance >= low) & (distance < high))
                    def _(flags=flags, low=low):
                        block = ((distance - low) * 2 + ((its ^ lane) & 1)) * frames + place
                        flags[row, block] = jnp.int32(1)

            each_live(frames, f, index, act)


def inner_kernel(frames, distances, *refs):
    x_in, ld_ref, k_in, v_in, pack, other, wq_in = refs[:7]
    inner_ref, qq_ref = refs[7:9]
    tables, (x_ref, k_ref, v_ref, bq, sems) = refs[9:-5], refs[-5:]
    copies = [
        pltpu.make_async_copy(src, dst, sems.at[i])
        for i, (src, dst) in enumerate(
            ((x_in, x_ref), (wq_in, bq), (k_in, k_ref), (v_in, v_ref))
        )
    ]
    for copy in copies:
        copy.start()
    list_live(frames, distances, tables, (pack, other))
    rows = x_in.shape[0]
    ld = ld_ref[...]
    t = lax.broadcasted_iota(jnp.int32, (rows, rows), 0)
    s = lax.broadcasted_iota(jnp.int32, (rows, rows), 1)
    upto = (s <= t) & (chain_of(s) == chain_of(t))
    ones = upto.astype(F32)
    column = column_sums(ones, ld)
    row = row_sums(ones, ld)
    grown = jnp.exp(column) * DK**-0.5
    for copy in copies:
        copy.wait()
    q = nn(x_ref[...], bq[...]).astype(BF16)
    for h in range(H):
        qh = q[:, h * DK : (h + 1) * DK]
        gap = column[:, h : h + 1] - row[h : h + 1, :]
        weight = jnp.exp(jnp.where(upto, gap, NEG)) * DK**-0.5
        scores = nt(qh, k_ref[:, h * DK : (h + 1) * DK]) * weight
        inner_ref[:, h * DV : (h + 1) * DV] = nn(
            scores.astype(BF16), v_ref[:, h * DV : (h + 1) * DV]
        )
        scaled = qh.astype(F32) * grown[:, h : h + 1]
        qq_ref[:, h * 2 * DK : (h + 1) * 2 * DK] = by_chain(scaled.astype(BF16))


def inner(tokens, w_rq, k, v, ld, pack, other, distances):
    rows, d = tokens.shape
    frames = rows // P_SIZE
    table_shapes = [
        jax.ShapeDtypeStruct((2 * frames, (high - low) * 2 * frames), jnp.int32)
        for low, high in distances
    ]
    out = pl.pallas_call(
        functools.partial(inner_kernel, frames, distances),
        in_specs=[HBM, VMEM, HBM, HBM, SMEM, SMEM, HBM],
        out_specs=[VMEM] * 2 + [SMEM] * len(table_shapes),
        out_shape=[
            jax.ShapeDtypeStruct((rows, H * DV), F32),
            jax.ShapeDtypeStruct((rows, H * 2 * DK), BF16),
        ]
        + table_shapes,
        scratch_shapes=[
            pltpu.VMEM((rows, d), BF16),
            pltpu.VMEM((rows, H * DK), BF16),
            pltpu.VMEM((rows, H * DV), BF16),
            pltpu.VMEM((d, H * DK), BF16),
            pltpu.SemaphoreType.DMA((4,)),
        ],
        compiler_params=params(48),
        cost_estimate=cost(2 * rows * d * H * DK, 8 << 20),
        name="inner",
    )(tokens, ld, k, v, pack, other, w_rq)
    return out[0], out[1], out[2:]


def join(first, second):
    return spread(jnp.exp(second[1])) * first[0] + second[0], first[1] + second[1]


def chip_kernel(keep, got, stay, send, ordered, results):
    y, core = position()
    ordered[core] = keep[...]
    ordered[1 - core] = got[...]
    for q in range(2):
        write_message(
            results.at[q], *join(read_message(ordered[0, q]), read_message(ordered[1, q]))
        )
    stay[...] = results[y]
    send[...] = results[1 - y]


def plane_kernel(stay, got, out, ordered):
    y, _ = position()
    ordered[y] = stay[...]
    ordered[1 - y] = got[...]
    write_message(out, *join(read_message(ordered[0]), read_message(ordered[1])))


def prefix_kernel(count, *refs):
    (stay, got), earlier = refs[:2], refs[2 : 2 + count]
    mine, send, ordered, results = refs[2 + count :]
    y, _ = position()
    plane = lax.axis_index("tm") // LANES
    ordered[y] = stay[...]
    ordered[1 - y] = got[...]
    state = jnp.zeros((ROWS, DV), F32)
    for distance in range(count, 0, -1):
        step, _ = join((state, 0.0), read_message(earlier[distance - 1][...]))
        state = jnp.where(plane >= distance, step, 0.0)
    results[0] = state.astype(BF16)
    results[1] = join((state, 0.0), read_message(ordered[0]))[0].astype(BF16)
    mine[...] = results[y]
    send[...] = results[1 - y]


def split_kernel(keep, local_got, mine, got, kept, give, ordered, both, results):
    y, core = position()
    ordered[core] = keep[...]
    ordered[1 - core] = local_got[...]
    both[y] = mine[...]
    both[1 - y] = got[...]
    for q in range(2):
        state = both[q]
        results[0, q] = state
        results[1, q] = join((state.astype(F32), 0.0), read_message(ordered[0, q]))[0].astype(BF16)
    kept[...] = results[core]
    give[...] = results[1 - core]


def small(kernel, outs, scratch, *args):
    return pl.pallas_call(
        kernel,
        in_specs=[VMEM] * len(args),
        out_specs=[VMEM] * len(outs),
        out_shape=[jax.ShapeDtypeStruct(shape, BF16) for shape in outs],
        scratch_shapes=[pltpu.VMEM(shape, BF16) for shape in scratch],
        compiler_params=params(8),
    )(*args)


def hidden_kernel(frames, *refs):
    inner_ref, qq_ref = refs[:2]
    kept, got = refs[2:4]
    x_ref, gain_ref, wq, wk, wv = refs[4:9]
    hid_ref, q_ref = refs[9:11]
    kv_refs = refs[11 : 11 + frames]
    ordered, bq, bk, bv, sems = refs[11 + frames :]
    copies = [
        pltpu.make_async_copy(src, dst, sems.at[i])
        for i, (src, dst) in enumerate(((wq, bq), (wk, bk), (wv, bv)))
    ]
    for copy in copies:
        copy.start()
    _, core = position()
    for y in range(2):
        ordered[2 * y + core] = kept[y]
        ordered[2 * y + 1 - core] = got[y]
    for h in range(H):
        cols = slice(h * DV, (h + 1) * DV)
        state = ordered[h // HC, (h % HC) * 2 * DK : (h % HC + 1) * 2 * DK, :]
        o = inner_ref[:, cols] + nn(qq_ref[:, h * 2 * DK : (h + 1) * 2 * DK], state)
        scale = lax.rsqrt(jnp.mean(o * o, axis=1, keepdims=True) + 1e-05)
        y = o * scale * gain_ref[:, cols]
        hid_ref[:, cols] = (x_ref[:, cols].astype(F32) + y).astype(BF16)
    hid = hid_ref[...]
    copies[0].wait()
    q_ref[...] = nn(hid, bq[...]).astype(BF16)
    for i, buf in ((1, bk), (2, bv)):
        copies[i].wait()
        part = nn(hid, buf[...]).astype(BF16)
        for f in range(frames):
            kv_refs[f][:, (i - 1) * MC : i * MC] = part[f * P_SIZE : (f + 1) * P_SIZE]


def hidden_of(inner_out, qq, states, tokens, gain, w_mq, w_mk, w_mv):
    rows, d = tokens.shape
    frames = rows // P_SIZE
    return pl.pallas_call(
        functools.partial(hidden_kernel, frames),
        in_specs=[VMEM] * 6 + [HBM] * 3,
        out_specs=[VMEM] * (2 + frames),
        out_shape=[
            jax.ShapeDtypeStruct((rows, d), BF16),
            jax.ShapeDtypeStruct((rows, MC), BF16),
        ]
        + [jax.ShapeDtypeStruct((P_SIZE, 2 * MC), BF16)] * frames,
        scratch_shapes=[pltpu.VMEM((LANES, ROWS, DV), BF16)]
        + [pltpu.VMEM((d, MC), BF16)] * 3
        + [pltpu.SemaphoreType.DMA((3,))],
        compiler_params=params(),
        name="hidden",
    )(inner_out, qq, *states, tokens, gain.reshape(1, d), w_mq, w_mk, w_mv)


def list_assist(frames, at, half, steps, planes, index, flags):
    me = lax.axis_index("tm")
    clear(flags)
    for f in range(frames):

        def act(distance, its, place, f=f):
            apart = its ^ lax.rem(me, LANES)

            @pl.when((distance == at) & (apart // 2 == half) & (me // LANES + steps < planes))
            def _():
                flags[f, (apart & 1) * frames + place] = jnp.int32(1)

        each_live(frames, f, index, act)


def attend_kernel(frames, blocks, row, first, last, assist, *refs):
    if assist is None:
        live, refs = refs[0], refs[1:]
    else:
        index, live, refs = refs[0], refs[-1], refs[1:-1]
    q_ref, refs = refs[0], refs[1:]
    if not first:
        acc_in, top_in, sum_in = refs[:3]
        refs = refs[3:]
    kv, refs = refs[:blocks], refs[blocks:]
    outs, (scores, stat) = refs[:-2], refs[-2:]
    rows = frames * P_SIZE
    scale = MD**-0.5
    base2 = scale * 1.4426950408889634
    pairs = [range(i, min(i + 2, blocks)) for i in range(0, blocks, 2)]
    spans = [slice(f * P_SIZE, (f + 1) * P_SIZE) for f in range(frames)]

    def run():
        if assist is not None:
            list_assist(frames, *assist, index, live)
        lane = lax.broadcasted_iota(jnp.int32, (rows, 128), 1)
        if last:
            stat[...] = jnp.zeros_like(stat)
        for e in range(MH):
            cols, vcols = slice(e * MD, (e + 1) * MD), slice(MC + e * MD, MC + (e + 1) * MD)
            held = slice(e * rows, (e + 1) * rows)
            q = q_ref[:, cols]
            tops = [None] * frames
            for pair in pairs:
                s = nt(q, jnp.concatenate([kv[b][:, cols] for b in pair], axis=0))
                for j, b in enumerate(pair):
                    for f in range(frames):
                        part = s[spans[f], j * P_SIZE : (j + 1) * P_SIZE]
                        part = jnp.where(live[row + f, b] == 1, part, NEG)
                        scores[spans[f], b * P_SIZE : (b + 1) * P_SIZE] = part
                        tops[f] = part if tops[f] is None else jnp.maximum(tops[f], part)
            top = jnp.concatenate([jnp.max(t, axis=1, keepdims=True) for t in tops], axis=0)
            top = jnp.broadcast_to(jnp.maximum(top, 0.1 * NEG), (rows, 128))
            if not first:
                before = top_in[held, :]
                top = jnp.maximum(top, before)
                fade = jnp.exp2((before - top) * base2)
            total, acc = None, None
            for pair in pairs:
                ps = []
                for b in pair:
                    p = jnp.exp2((scores[:, b * P_SIZE : (b + 1) * P_SIZE] - top) * base2)
                    total = p if total is None else total + p
                    ps.append(p.astype(BF16))
                part = nn(
                    jnp.concatenate(ps, axis=1),
                    jnp.concatenate([kv[b][:, vcols] for b in pair], axis=0),
                )
                acc = part if acc is None else acc + part
            if not first:
                total = total + fade * sum_in[held, :]
                acc = acc + fade * acc_in[:, cols]
            if last:
                whole = jnp.broadcast_to(jnp.sum(total, axis=1, keepdims=True), (rows, 128))
                whole = jnp.maximum(whole, 1e-30)
                outs[0][:, cols] = (acc / whole).astype(outs[0].dtype)
                stat[...] = jnp.where(
                    lane == e, top, jnp.where(lane == MH + e, whole, stat[...])
                )
            else:
                outs[0][:, cols] = acc
                outs[1][held, :] = top
                outs[2][held, :] = total
        if last:
            flat = jnp.transpose(stat[...])
            low = jnp.log(flat[MH : 2 * MH])
            outs[1][...] = jnp.concatenate([flat[:MH] * scale + low, low], axis=0)

    if assist is None:
        run()
    else:
        steps, planes = assist[2:]
        plane = lax.axis_index("tm") // LANES
        pl.when((plane >= 1) & (plane + steps < planes))(run)


def attend(lists, row, asked, kvs, state, last, dtype, assist=None):
    rows = asked.shape[0]
    frames = rows // P_SIZE
    blocks = len(kvs)
    first = state is None
    state = [] if first else list(state)
    if last:
        out_shape = [
            jax.ShapeDtypeStruct((rows, MC), dtype),
            jax.ShapeDtypeStruct((2 * MH, rows), F32),
        ]
    else:
        out_shape = [jax.ShapeDtypeStruct((rows, MC), F32)]
        out_shape += [jax.ShapeDtypeStruct((MH * rows, 128), F32)] * 2
    scratch = [pltpu.VMEM((rows, blocks * P_SIZE), F32), pltpu.VMEM((rows, 128), F32)]
    if assist is not None:
        scratch.append(pltpu.SMEM((frames, blocks), jnp.int32))
    return pl.pallas_call(
        functools.partial(attend_kernel, frames, blocks, row, first, last, assist),
        in_specs=[SMEM] + [VMEM] * (1 + len(state) + blocks),
        out_specs=[VMEM] * len(out_shape),
        out_shape=out_shape,
        scratch_shapes=scratch,
        compiler_params=params(),
        cost_estimate=cost(4 * blocks * rows * P_SIZE * MC, blocks * P_SIZE * MC * 4),
        name="assist" if assist is not None else "attend_last" if last else "attend",
    )(lists, asked, *state, *kvs)


def output_kernel(parts, steps, *refs):
    values, stats = refs[0 : 2 * parts : 2], refs[1 : 2 * parts : 2]
    hid_ref, w_ref, out_ref, mixed = refs[2 * parts :]
    rows = hid_ref.shape[0]
    logs = [ref[...] for ref in stats]
    if parts > 2:
        logs[2] = jnp.where(lax.axis_index("tm") // LANES > steps, logs[2], NEG)
    top = functools.reduce(jnp.maximum, logs)
    shares = [jnp.exp(x - top) for x in logs]
    inv = 1.0 / functools.reduce(jnp.add, shares)
    pad = jnp.zeros((128 - parts * 2 * MH, rows), F32)
    weights = jnp.transpose(jnp.concatenate([x * inv for x in shares] + [pad], axis=0))
    for e in range(MH):
        cols = slice(e * MD, (e + 1) * MD)
        value = 0.0
        for i, ref in enumerate(values):
            at = i * 2 * MH + e
            value = value + ref[:, cols].astype(F32) * weights[:, at : at + 1]
        mixed[:, cols] = value.astype(BF16)
    out_ref[...] = (hid_ref[...].astype(F32) + nn(mixed[...], w_ref[...])).astype(BF16)


def output(parts, hid, w_out, steps):
    rows, d = hid.shape
    flat = [x for part in parts for x in part]
    return pl.pallas_call(
        functools.partial(output_kernel, len(parts), steps),
        in_specs=[VMEM] * (len(flat) + 2),
        out_specs=VMEM,
        out_shape=jax.ShapeDtypeStruct((rows, d), BF16),
        scratch_shapes=[pltpu.VMEM((rows, MC), BF16)],
        compiler_params=params(),
        name="output",
    )(*flat, hid, w_out)


def on_device(
    tokens, log_decay, mem_index, mem_count, w_rq, w_rk, w_rv, norm_gain, w_mq, w_mk, w_mv, w_out
):
    size = lax.axis_size("tm")
    planes = size // LANES
    frames = tokens.shape[0] // P_SIZE

    def flip(x, bits):
        return lax.ppermute(x, "tm", [(i, i ^ bits) for i in range(size)])

    def up(x, distance):
        step = distance * LANES
        return lax.ppermute(x, "tm", [(i, (i + step) % size) for i in range(size)])

    message, chunk = (ROWS + TAIL, DV), (ROWS, DV)
    steps, reach = reaches(planes)
    spans = spans_of(steps)
    k, v, keep, give, pack = local(tokens, w_rk, w_rv, log_decay, mem_index, mem_count)
    core_got = flip(give, 1)
    other = flip(pack, 2)
    stay, send = small(
        chip_kernel, [message] * 2, [(2, 2) + message, (2,) + message], keep, core_got
    )
    column_got = flip(send, 2)
    (total,) = small(plane_kernel, [message], [(2,) + message], stay, column_got)
    earlier = [up(total, d) for d in range(1, planes)]
    inner_out, qq, tables = inner(tokens, w_rq, k, v, log_decay, pack, other, spans)
    mine, send = small(
        functools.partial(prefix_kernel, len(earlier)),
        [chunk] * 2,
        [(2,) + message, (2,) + chunk],
        stay,
        column_got,
        *earlier,
    )
    column_back = flip(send, 2)
    kept, give = small(
        split_kernel,
        [(2,) + chunk] * 2,
        [(2, 2) + message, (2,) + chunk, (2, 2) + chunk],
        keep,
        core_got,
        mine,
        column_back,
    )
    states = (kept, flip(give, 1))
    hid, q, *kv = hidden_of(inner_out, qq, states, tokens, norm_gain, w_mq, w_mk, w_mv)

    def between(x, pairs):
        return lax.ppermute(
            x, "tm", [(a * LANES + i, b * LANES + i) for a, b in pairs for i in range(LANES)]
        )

    def onward(x, distance):
        pairs = [(p, p + 1) for p in range(distance - 1, planes - 1)]
        return between(x, pairs + [(planes - 1, 0)] * (distance == 1))

    frames = len(kv)
    partner_q = flip(q, 2)
    held, across = [], []
    for distance in range(steps + 1):
        if distance:
            kv = [onward(x, distance) for x in kv]
        near = [flip(x, 1) for x in kv]
        held.append(kv + near)
        if 1 <= distance <= reach:
            column = [flip(x, 2) for x in kv]
            both = [flip(x, 1) for x in column]
            across += [(distance, 0, kv + near), (distance, 1, column + both)]
    parts = []
    if reach:
        helped = [(p, p + steps) for p in range(1, planes - steps)]
        down = [(b, a) for a, b in helped]
        far_q = between(q, down)
        far_pack = between(pack, down)
        far = None
        for at, half, blocks in across:
            last = at == reach and half == 1
            far = attend(
                far_pack, 0, far_q, blocks, far, last, BF16, (at, half, steps, planes)
            )
        parts = [[between(x, helped) for x in far]]

    def attended(row, asked, dtype):
        state = None
        for (low, high), flags in zip(spans, tables):
            blocks = [x for group in held[low:high] for x in group]
            state = attend(flags, row, asked, blocks, state, high == steps + 1, dtype)
        return state

    theirs = attended(frames, partner_q, BF16)
    back = [flip(x, 2) for x in theirs]
    mine = attended(0, q, F32)
    return output([mine, back] + parts, hid, w_out, steps)


def spans_of(steps):
    return [(low, min(low + 2, steps)) for low in range(0, steps, 2)] + [(steps, steps + 1)]


def reaches(planes):
    steps = planes // 2
    return steps, planes - 1 - steps


def solution(mesh):
    placed = (
        P(("groups", "tm"), None),
        P(None, ("groups", "tm")),
        P(("groups", "tm"), None),
        P(("groups", "tm")),
        P(),
        P(),
        P(),
        P(),
        P(),
        P(),
        P(),
        P(),
    )

    return jax.shard_map(
        on_device, mesh=mesh, in_specs=placed, out_specs=P(("groups", "tm"), None), check_vma=False
    )
```

```python
import functools

import jax
import jax.numpy as jnp
from jax import lax
from jax.experimental import pallas as pl
from jax.experimental.pallas import tpu as pltpu
from jax.sharding import PartitionSpec as P


H = 8
DK = 64
DV = 128
MH = 4
MD = 128
MC = 512
P_SIZE = 128
BLK = 64
LANES = 4
HC = H // LANES
ROWS = HC * 2 * DK
TAIL = 16
PAIRS = HC * 2
NEG = -1e30
F32 = jnp.float32
BF16 = jnp.bfloat16


VMEM = pl.BlockSpec(memory_space=pltpu.VMEM)
SMEM = pl.BlockSpec(memory_space=pltpu.SMEM)
HBM = pl.BlockSpec(memory_space=pltpu.HBM)


def params(mib=48):
    return pltpu.CompilerParams(vmem_limit_bytes=mib << 20)


def cost(flops, nbytes):
    return pl.CostEstimate(flops=flops, bytes_accessed=nbytes, transcendentals=0)


def chain_of(iota):
    return (iota // BLK) % 2


def nn(a, b, **kw):
    return lax.dot_general(a, b, (((1,), (0,)), ((), ())), preferred_element_type=F32, **kw)


def nt(a, b, **kw):
    return lax.dot_general(a, b, (((1,), (1,)), ((), ())), preferred_element_type=F32, **kw)


def by_chain(x):
    rows = x.shape[0]
    chain = chain_of(lax.broadcasted_iota(jnp.int32, (rows, DK), 0))
    zero = jnp.zeros_like(x)
    return jnp.concatenate([jnp.where(chain == 0, x, zero), jnp.where(chain == 1, x, zero)], axis=1)


def split3(x):
    hi = x.astype(BF16)
    rest = x - hi.astype(F32)
    mid = rest.astype(BF16)
    return hi, mid, (rest - mid.astype(F32)).astype(BF16)


def read_message(x):
    state = x[:ROWS].astype(F32)
    tail = x[ROWS:].astype(F32)
    total = tail[0:PAIRS] + tail[PAIRS : 2 * PAIRS] + tail[2 * PAIRS : 3 * PAIRS]
    return state, total


def spread(total):
    return jnp.concatenate(
        [jnp.broadcast_to(total[p : p + 1], (DK, total.shape[1])) for p in range(PAIRS)], axis=0
    )


def write_message(ref, state, total):
    ref[:ROWS, :] = state.astype(BF16)
    hi, mid, lo = split3(total)
    pad = jnp.zeros((TAIL - 3 * PAIRS, total.shape[1]), F32)
    ref[ROWS:, :] = jnp.concatenate(
        [hi.astype(F32), mid.astype(F32), lo.astype(F32), pad], axis=0
    ).astype(BF16)


def decay_terms(ld):
    return jnp.concatenate([t.astype(F32) for t in split3(ld)], axis=0).astype(BF16)


def column_sums(mask, ld):
    x = nt(mask.astype(BF16), decay_terms(ld))
    return x[:, :H] + x[:, H : 2 * H] + x[:, 2 * H : 3 * H]


def row_sums(mask, ld):
    x = nt(decay_terms(ld), mask.astype(BF16))
    return x[:H] + x[H : 2 * H] + x[2 * H : 3 * H]


def position():
    lane = lax.rem(lax.axis_index("tm"), LANES)
    return lane // 2, lane & 1


def local_kernel(x_in, ld_in, wk_in, wv_in, idx_in, cnt_in, k_ref, v_ref, keep, give, pack, *rest):
    chunks, x_ref, ld_ref, bk, bv, idx, cnt, sems = rest
    rows = x_ref.shape[0]
    copies = [
        pltpu.make_async_copy(src, dst, sems.at[i])
        for i, (src, dst) in enumerate(
            (
                (ld_in, ld_ref),
                (x_in, x_ref),
                (wk_in, bk),
                (wv_in, bv),
                (idx_in, idx),
                (cnt_in, cnt),
            )
        )
    ]
    for copy in copies:
        copy.start()
    t = lax.broadcasted_iota(jnp.int32, (rows, rows), 0)
    s = lax.broadcasted_iota(jnp.int32, (rows, rows), 1)
    after = ((s > t) & (chain_of(s) == chain_of(t))).astype(F32)
    copies[0].wait()
    ld = ld_ref[...]
    tail = jnp.exp(row_sums(after, ld))
    chain = chain_of(lax.broadcasted_iota(jnp.int32, ld.shape, 1))
    sums = [jnp.sum(jnp.where(chain == b, ld, 0.0), axis=1, keepdims=True) for b in (0, 1)]
    tails = [jnp.where(chain == b, tail, 0.0) for b in (0, 1)]
    copies[1].wait()
    copies[2].wait()
    x = x_ref[...]
    k = nn(x, bk[...]).astype(BF16)
    k_ref[...] = k
    turned = [
        jnp.transpose(k[:, q * HC * DK : (q + 1) * HC * DK].astype(F32)) for q in range(LANES)
    ]
    for copy in copies[3:]:
        copy.wait()
    v = nn(x, bv[...]).astype(BF16)
    v_ref[...] = v
    for q in range(LANES):
        states, totals = [], []
        for i in range(HC):
            h = q * HC + i
            kt = turned[q][i * DK : (i + 1) * DK]
            both = jnp.concatenate([(kt * tails[b][h : h + 1]).astype(BF16) for b in (0, 1)], axis=0)
            states.append(nn(both, v[:, h * DV : (h + 1) * DV]))
            totals += [jnp.broadcast_to(sums[b][h : h + 1], (1, DV)) for b in (0, 1)]
        write_message(
            chunks.at[q], jnp.concatenate(states, axis=0), jnp.concatenate(totals, axis=0)
        )
    _, core = position()
    for y in range(2):
        keep[y] = chunks[2 * y + core]
        give[y] = chunks[2 * y + 1 - core]
    frames, slots = idx.shape
    for f in range(frames):
        for i in range(slots):
            pack[f, i] = idx[f, i]
        pack[f, slots] = cnt[f]


def local(tokens, w_rk, w_rv, ld, index, live):
    rows, d = tokens.shape
    message = jax.ShapeDtypeStruct((2, ROWS + TAIL, DV), BF16)
    frames, slots = index.shape
    return pl.pallas_call(
        local_kernel,
        in_specs=[HBM] * 6,
        out_specs=[VMEM] * 4 + [SMEM],
        out_shape=[
            jax.ShapeDtypeStruct((rows, H * DK), BF16),
            jax.ShapeDtypeStruct((rows, H * DV), BF16),
            message,
            message,
            jax.ShapeDtypeStruct((frames, slots + 1), jnp.int32),
        ],
        scratch_shapes=[
            pltpu.VMEM((LANES, ROWS + TAIL, DV), BF16),
            pltpu.VMEM((rows, d), BF16),
            pltpu.VMEM((H, rows), F32),
            pltpu.VMEM((d, H * DK), BF16),
            pltpu.VMEM((d, H * DV), BF16),
            pltpu.SMEM((frames, slots), jnp.int32),
            pltpu.SMEM((frames,), jnp.int32),
            pltpu.SemaphoreType.DMA((6,)),
        ],
        compiler_params=params(62),
        name="local",
    )(tokens, ld, w_rk, w_rv, index, live)


def clear(flags):
    for row in range(flags.shape[0]):
        for block in range(flags.shape[1]):
            flags[row, block] = jnp.int32(0)


def each_live(frames, f, index, act):
    me = lax.axis_index("tm")
    slots = index.shape[1] - 1

    def visit(i, carry):
        frame = index[f, i]
        owner = frame // frames
        act(me // LANES - owner // LANES, lax.rem(owner, LANES), lax.rem(frame, frames))
        return carry

    lax.fori_loop(0, jnp.minimum(index[f, slots], slots), visit, 0)


def list_live(frames, distances, tables, groups):
    lane = lax.rem(lax.axis_index("tm"), LANES)
    for flags in tables:
        clear(flags)
    for g, index in enumerate(groups):
        for f in range(frames):
            row = g * frames + f
            if g == 0:
                tables[0][row, f] = jnp.int32(1)

            def act(distance, its, place, row=row):
                here = (its // 2) == (lane // 2)
                for flags, (low, high) in zip(tables, distances):

                    @pl.when(here & (distance >= low) & (distance < high))
                    def _(flags=flags, low=low):
                        block = ((distance - low) * 2 + ((its ^ lane) & 1)) * frames + place
                        flags[row, block] = jnp.int32(1)

            each_live(frames, f, index, act)


def inner_kernel(frames, distances, *refs):
    x_in, ld_ref, k_in, v_in, pack, other, wq_in = refs[:7]
    inner_ref, qq_ref = refs[7:9]
    tables, (x_ref, k_ref, v_ref, bq, sems) = refs[9:-5], refs[-5:]
    copies = [
        pltpu.make_async_copy(src, dst, sems.at[i])
        for i, (src, dst) in enumerate(
            ((x_in, x_ref), (wq_in, bq), (k_in, k_ref), (v_in, v_ref))
        )
    ]
    for copy in copies:
        copy.start()
    list_live(frames, distances, tables, (pack, other))
    rows = x_in.shape[0]
    ld = ld_ref[...]
    t = lax.broadcasted_iota(jnp.int32, (rows, rows), 0)
    s = lax.broadcasted_iota(jnp.int32, (rows, rows), 1)
    upto = (s <= t) & (chain_of(s) == chain_of(t))
    ones = upto.astype(F32)
    column = column_sums(ones, ld)
    row = row_sums(ones, ld)
    grown = jnp.exp(column) * DK**-0.5
    for copy in copies:
        copy.wait()
    q = nn(x_ref[...], bq[...]).astype(BF16)
    for h in range(H):
        qh = q[:, h * DK : (h + 1) * DK]
        gap = column[:, h : h + 1] - row[h : h + 1, :]
        weight = jnp.exp(jnp.where(upto, gap, NEG)) * DK**-0.5
        scores = nt(qh, k_ref[:, h * DK : (h + 1) * DK]) * weight
        inner_ref[:, h * DV : (h + 1) * DV] = nn(
            scores.astype(BF16), v_ref[:, h * DV : (h + 1) * DV]
        )
        scaled = qh.astype(F32) * grown[:, h : h + 1]
        qq_ref[:, h * 2 * DK : (h + 1) * 2 * DK] = by_chain(scaled.astype(BF16))


def inner(tokens, w_rq, k, v, ld, pack, other, distances):
    rows, d = tokens.shape
    frames = rows // P_SIZE
    table_shapes = [
        jax.ShapeDtypeStruct((2 * frames, (high - low) * 2 * frames), jnp.int32)
        for low, high in distances
    ]
    out = pl.pallas_call(
        functools.partial(inner_kernel, frames, distances),
        in_specs=[HBM, VMEM, HBM, HBM, SMEM, SMEM, HBM],
        out_specs=[VMEM] * 2 + [SMEM] * len(table_shapes),
        out_shape=[
            jax.ShapeDtypeStruct((rows, H * DV), F32),
            jax.ShapeDtypeStruct((rows, H * 2 * DK), BF16),
        ]
        + table_shapes,
        scratch_shapes=[
            pltpu.VMEM((rows, d), BF16),
            pltpu.VMEM((rows, H * DK), BF16),
            pltpu.VMEM((rows, H * DV), BF16),
            pltpu.VMEM((d, H * DK), BF16),
            pltpu.SemaphoreType.DMA((4,)),
        ],
        compiler_params=params(48),
        cost_estimate=cost(2 * rows * d * H * DK, 8 << 20),
        name="inner",
    )(tokens, ld, k, v, pack, other, w_rq)
    return out[0], out[1], out[2:]


def join(first, second):
    return spread(jnp.exp(second[1])) * first[0] + second[0], first[1] + second[1]


def chip_kernel(keep, got, stay, send, ordered, results):
    y, core = position()
    ordered[core] = keep[...]
    ordered[1 - core] = got[...]
    for q in range(2):
        write_message(
            results.at[q], *join(read_message(ordered[0, q]), read_message(ordered[1, q]))
        )
    stay[...] = results[y]
    send[...] = results[1 - y]


def plane_kernel(stay, got, out, ordered):
    y, _ = position()
    ordered[y] = stay[...]
    ordered[1 - y] = got[...]
    write_message(out, *join(read_message(ordered[0]), read_message(ordered[1])))


def prefix_kernel(count, *refs):
    (stay, got), earlier = refs[:2], refs[2 : 2 + count]
    mine, send, ordered, results = refs[2 + count :]
    y, _ = position()
    plane = lax.axis_index("tm") // LANES
    ordered[y] = stay[...]
    ordered[1 - y] = got[...]
    state = jnp.zeros((ROWS, DV), F32)
    for distance in range(count, 0, -1):
        step, _ = join((state, 0.0), read_message(earlier[distance - 1][...]))
        state = jnp.where(plane >= distance, step, 0.0)
    results[0] = state.astype(BF16)
    results[1] = join((state, 0.0), read_message(ordered[0]))[0].astype(BF16)
    mine[...] = results[y]
    send[...] = results[1 - y]


def split_kernel(keep, local_got, mine, got, kept, give, ordered, both, results):
    y, core = position()
    ordered[core] = keep[...]
    ordered[1 - core] = local_got[...]
    both[y] = mine[...]
    both[1 - y] = got[...]
    for q in range(2):
        state = both[q]
        results[0, q] = state
        results[1, q] = join((state.astype(F32), 0.0), read_message(ordered[0, q]))[0].astype(BF16)
    kept[...] = results[core]
    give[...] = results[1 - core]


def small(kernel, outs, scratch, *args):
    return pl.pallas_call(
        kernel,
        in_specs=[VMEM] * len(args),
        out_specs=[VMEM] * len(outs),
        out_shape=[jax.ShapeDtypeStruct(shape, BF16) for shape in outs],
        scratch_shapes=[pltpu.VMEM(shape, BF16) for shape in scratch],
        compiler_params=params(8),
    )(*args)


def hidden_kernel(frames, *refs):
    inner_ref, qq_ref = refs[:2]
    kept, got = refs[2:4]
    x_ref, gain_ref, wq, wk, wv = refs[4:9]
    hid_ref, q_ref = refs[9:11]
    kv_refs = refs[11 : 11 + frames]
    ordered, bq, bk, bv, sems = refs[11 + frames :]
    copies = [
        pltpu.make_async_copy(src, dst, sems.at[i])
        for i, (src, dst) in enumerate(((wq, bq), (wk, bk), (wv, bv)))
    ]
    for copy in copies:
        copy.start()
    _, core = position()
    for y in range(2):
        ordered[2 * y + core] = kept[y]
        ordered[2 * y + 1 - core] = got[y]
    for h in range(H):
        cols = slice(h * DV, (h + 1) * DV)
        state = ordered[h // HC, (h % HC) * 2 * DK : (h % HC + 1) * 2 * DK, :]
        o = inner_ref[:, cols] + nn(qq_ref[:, h * 2 * DK : (h + 1) * 2 * DK], state)
        scale = lax.rsqrt(jnp.mean(o * o, axis=1, keepdims=True) + 1e-05)
        y = o * scale * gain_ref[:, cols]
        hid_ref[:, cols] = (x_ref[:, cols].astype(F32) + y).astype(BF16)
    hid = hid_ref[...]
    copies[0].wait()
    q_ref[...] = nn(hid, bq[...]).astype(BF16)
    for i, buf in ((1, bk), (2, bv)):
        copies[i].wait()
        part = nn(hid, buf[...]).astype(BF16)
        for f in range(frames):
            kv_refs[f][:, (i - 1) * MC : i * MC] = part[f * P_SIZE : (f + 1) * P_SIZE]


def hidden_of(inner_out, qq, states, tokens, gain, w_mq, w_mk, w_mv):
    rows, d = tokens.shape
    frames = rows // P_SIZE
    return pl.pallas_call(
        functools.partial(hidden_kernel, frames),
        in_specs=[VMEM] * 6 + [HBM] * 3,
        out_specs=[VMEM] * (2 + frames),
        out_shape=[
            jax.ShapeDtypeStruct((rows, d), BF16),
            jax.ShapeDtypeStruct((rows, MC), BF16),
        ]
        + [jax.ShapeDtypeStruct((P_SIZE, 2 * MC), BF16)] * frames,
        scratch_shapes=[pltpu.VMEM((LANES, ROWS, DV), BF16)]
        + [pltpu.VMEM((d, MC), BF16)] * 3
        + [pltpu.SemaphoreType.DMA((3,))],
        compiler_params=params(),
        name="hidden",
    )(inner_out, qq, *states, tokens, gain.reshape(1, d), w_mq, w_mk, w_mv)


def list_assist(frames, at, half, steps, planes, index, flags):
    me = lax.axis_index("tm")
    clear(flags)
    for f in range(frames):

        def act(distance, its, place, f=f):
            apart = its ^ lax.rem(me, LANES)

            @pl.when((distance == at) & (apart // 2 == half) & (me // LANES + steps < planes))
            def _():
                flags[f, (apart & 1) * frames + place] = jnp.int32(1)

        each_live(frames, f, index, act)


def attend_kernel(frames, blocks, row, first, last, assist, *refs):
    if assist is None:
        live, refs = refs[0], refs[1:]
    else:
        index, live, refs = refs[0], refs[-1], refs[1:-1]
    q_ref, refs = refs[0], refs[1:]
    if not first:
        acc_in, top_in, sum_in = refs[:3]
        refs = refs[3:]
    kv, refs = refs[:blocks], refs[blocks:]
    outs, (scores, stat) = refs[:-2], refs[-2:]
    rows = frames * P_SIZE
    scale = MD**-0.5
    base2 = scale * 1.4426950408889634
    pairs = [range(i, min(i + 2, blocks)) for i in range(0, blocks, 2)]
    spans = [slice(f * P_SIZE, (f + 1) * P_SIZE) for f in range(frames)]

    def run():
        if assist is not None:
            list_assist(frames, *assist, index, live)
        lane = lax.broadcasted_iota(jnp.int32, (rows, 128), 1)
        kept = []
        for e in range(MH):
            cols, vcols = slice(e * MD, (e + 1) * MD), slice(MC + e * MD, MC + (e + 1) * MD)
            held = slice(e * rows, (e + 1) * rows)
            q = q_ref[:, cols]
            tops = [None] * frames
            for pair in pairs:
                s = nt(q, jnp.concatenate([kv[b][:, cols] for b in pair], axis=0))
                for j, b in enumerate(pair):
                    for f in range(frames):
                        part = s[spans[f], j * P_SIZE : (j + 1) * P_SIZE]
                        part = jnp.where(live[row + f, b] == 1, part, NEG)
                        scores[e, spans[f], b * P_SIZE : (b + 1) * P_SIZE] = part
                        tops[f] = part if tops[f] is None else jnp.maximum(tops[f], part)
            top = jnp.concatenate([jnp.max(t, axis=1, keepdims=True) for t in tops], axis=0)
            top = jnp.broadcast_to(jnp.maximum(top, 0.1 * NEG), (rows, 128))
            if not first:
                before = top_in[held, :]
                top = jnp.maximum(top, before)
                fade = jnp.exp2((before - top) * base2)
            total, acc = None, None
            for pair in pairs:
                ps = []
                for b in pair:
                    p = jnp.exp2((scores[e, :, b * P_SIZE : (b + 1) * P_SIZE] - top) * base2)
                    total = p if total is None else total + p
                    ps.append(p.astype(BF16))
                part = nn(
                    jnp.concatenate(ps, axis=1),
                    jnp.concatenate([kv[b][:, vcols] for b in pair], axis=0),
                )
                acc = part if acc is None else acc + part
            if not first:
                total = total + fade * sum_in[held, :]
                acc = acc + fade * acc_in[:, cols]
            if last:
                whole = jnp.broadcast_to(jnp.sum(total, axis=1, keepdims=True), (rows, 128))
                whole = jnp.maximum(whole, 1e-30)
                outs[0][:, cols] = (acc / whole).astype(outs[0].dtype)
                kept.append((top, whole))
            else:
                outs[0][:, cols] = acc
                outs[1][held, :] = top
                outs[2][held, :] = total
        if last:
            merged = jnp.zeros((rows, 128), F32)
            for e, (top, whole) in enumerate(kept):
                merged = jnp.where(lane == e, top, jnp.where(lane == MH + e, whole, merged))
            stat[...] = merged
            flat = jnp.transpose(stat[...])
            low = jnp.log(flat[MH : 2 * MH])
            outs[1][...] = jnp.concatenate([flat[:MH] * scale + low, low], axis=0)

    if assist is None:
        run()
    else:
        steps, planes = assist[2:]
        plane = lax.axis_index("tm") // LANES
        pl.when((plane >= 1) & (plane + steps < planes))(run)


def attend(lists, row, asked, kvs, state, last, dtype, assist=None):
    rows = asked.shape[0]
    frames = rows // P_SIZE
    blocks = len(kvs)
    first = state is None
    state = [] if first else list(state)
    if last:
        out_shape = [
            jax.ShapeDtypeStruct((rows, MC), dtype),
            jax.ShapeDtypeStruct((2 * MH, rows), F32),
        ]
    else:
        out_shape = [jax.ShapeDtypeStruct((rows, MC), F32)]
        out_shape += [jax.ShapeDtypeStruct((MH * rows, 128), F32)] * 2
    scratch = [pltpu.VMEM((MH, rows, blocks * P_SIZE), F32), pltpu.VMEM((rows, 128), F32)]
    if assist is not None:
        scratch.append(pltpu.SMEM((frames, blocks), jnp.int32))
    return pl.pallas_call(
        functools.partial(attend_kernel, frames, blocks, row, first, last, assist),
        in_specs=[SMEM] + [VMEM] * (1 + len(state) + blocks),
        out_specs=[VMEM] * len(out_shape),
        out_shape=out_shape,
        scratch_shapes=scratch,
        compiler_params=params(),
        cost_estimate=cost(4 * blocks * rows * P_SIZE * MC, blocks * P_SIZE * MC * 4),
        name="assist" if assist is not None else "attend_last" if last else "attend",
    )(lists, asked, *state, *kvs)


def output_kernel(parts, steps, *refs):
    values, stats = refs[0 : 2 * parts : 2], refs[1 : 2 * parts : 2]
    hid_ref, w_ref, out_ref, mixed = refs[2 * parts :]
    rows = hid_ref.shape[0]
    logs = [ref[...] for ref in stats]
    if parts > 2:
        logs[2] = jnp.where(lax.axis_index("tm") // LANES > steps, logs[2], NEG)
    top = functools.reduce(jnp.maximum, logs)
    shares = [jnp.exp(x - top) for x in logs]
    inv = 1.0 / functools.reduce(jnp.add, shares)
    pad = jnp.zeros((128 - parts * 2 * MH, rows), F32)
    weights = jnp.transpose(jnp.concatenate([x * inv for x in shares] + [pad], axis=0))
    for e in range(MH):
        cols = slice(e * MD, (e + 1) * MD)
        value = 0.0
        for i, ref in enumerate(values):
            at = i * 2 * MH + e
            value = value + ref[:, cols].astype(F32) * weights[:, at : at + 1]
        mixed[:, cols] = value.astype(BF16)
    out_ref[...] = (hid_ref[...].astype(F32) + nn(mixed[...], w_ref[...])).astype(BF16)


def output(parts, hid, w_out, steps):
    rows, d = hid.shape
    flat = [x for part in parts for x in part]
    return pl.pallas_call(
        functools.partial(output_kernel, len(parts), steps),
        in_specs=[VMEM] * (len(flat) + 2),
        out_specs=VMEM,
        out_shape=jax.ShapeDtypeStruct((rows, d), BF16),
        scratch_shapes=[pltpu.VMEM((rows, MC), BF16)],
        compiler_params=params(),
        name="output",
    )(*flat, hid, w_out)


def on_device(
    tokens, log_decay, mem_index, mem_count, w_rq, w_rk, w_rv, norm_gain, w_mq, w_mk, w_mv, w_out
):
    size = lax.axis_size("tm")
    planes = size // LANES
    frames = tokens.shape[0] // P_SIZE

    def flip(x, bits):
        return lax.ppermute(x, "tm", [(i, i ^ bits) for i in range(size)])

    def up(x, distance):
        step = distance * LANES
        return lax.ppermute(x, "tm", [(i, (i + step) % size) for i in range(size)])

    message, chunk = (ROWS + TAIL, DV), (ROWS, DV)
    steps, reach = reaches(planes)
    spans = spans_of(steps)
    k, v, keep, give, pack = local(tokens, w_rk, w_rv, log_decay, mem_index, mem_count)
    core_got = flip(give, 1)
    other = flip(pack, 2)
    stay, send = small(
        chip_kernel, [message] * 2, [(2, 2) + message, (2,) + message], keep, core_got
    )
    column_got = flip(send, 2)
    (total,) = small(plane_kernel, [message], [(2,) + message], stay, column_got)
    earlier = [up(total, d) for d in range(1, planes)]
    inner_out, qq, tables = inner(tokens, w_rq, k, v, log_decay, pack, other, spans)
    mine, send = small(
        functools.partial(prefix_kernel, len(earlier)),
        [chunk] * 2,
        [(2,) + message, (2,) + chunk],
        stay,
        column_got,
        *earlier,
    )
    column_back = flip(send, 2)
    kept, give = small(
        split_kernel,
        [(2,) + chunk] * 2,
        [(2, 2) + message, (2,) + chunk, (2, 2) + chunk],
        keep,
        core_got,
        mine,
        column_back,
    )
    states = (kept, flip(give, 1))
    hid, q, *kv = hidden_of(inner_out, qq, states, tokens, norm_gain, w_mq, w_mk, w_mv)

    def between(x, pairs):
        return lax.ppermute(
            x, "tm", [(a * LANES + i, b * LANES + i) for a, b in pairs for i in range(LANES)]
        )

    def onward(x, distance):
        pairs = [(p, p + 1) for p in range(distance - 1, planes - 1)]
        return between(x, pairs + [(planes - 1, 0)] * (distance == 1))

    frames = len(kv)
    partner_q = flip(q, 2)
    held, across = [], []
    for distance in range(steps + 1):
        if distance:
            kv = [onward(x, distance) for x in kv]
        near = [flip(x, 1) for x in kv]
        held.append(kv + near)
        if 1 <= distance <= reach:
            column = [flip(x, 2) for x in kv]
            both = [flip(x, 1) for x in column]
            across += [(distance, 0, kv + near), (distance, 1, column + both)]
    parts = []
    if reach:
        helped = [(p, p + steps) for p in range(1, planes - steps)]
        down = [(b, a) for a, b in helped]
        far_q = between(q, down)
        far_pack = between(pack, down)
        far = None
        for at, half, blocks in across:
            last = at == reach and half == 1
            far = attend(
                far_pack, 0, far_q, blocks, far, last, BF16, (at, half, steps, planes)
            )
        parts = [[between(x, helped) for x in far]]

    def attended(row, asked, dtype):
        state = None
        for (low, high), flags in zip(spans, tables):
            blocks = [x for group in held[low:high] for x in group]
            state = attend(flags, row, asked, blocks, state, high == steps + 1, dtype)
        return state

    theirs = attended(frames, partner_q, BF16)
    back = [flip(x, 2) for x in theirs]
    mine = attended(0, q, F32)
    return output([mine, back] + parts, hid, w_out, steps)


def spans_of(steps):
    return [(low, min(low + 2, steps)) for low in range(0, steps, 2)] + [(steps, steps + 1)]


def reaches(planes):
    steps = planes // 2
    return steps, planes - 1 - steps


def solution(mesh):
    placed = (
        P(("groups", "tm"), None),
        P(None, ("groups", "tm")),
        P(("groups", "tm"), None),
        P(("groups", "tm")),
        P(),
        P(),
        P(),
        P(),
        P(),
        P(),
        P(),
        P(),
    )

    return jax.shard_map(
        on_device, mesh=mesh, in_specs=placed, out_specs=P(("groups", "tm"), None), check_vma=False
    )
```

```python
import functools

import jax
import jax.numpy as jnp
from jax import lax
from jax.experimental import pallas as pl
from jax.experimental.pallas import tpu as pltpu
from jax.sharding import PartitionSpec as P


H = 8
DK = 64
DV = 128
MH = 4
MD = 128
MC = 512
P_SIZE = 128
BLK = 64
LANES = 4
HC = H // LANES
ROWS = HC * 2 * DK
TAIL = 16
PAIRS = HC * 2
NEG = -1e30
F32 = jnp.float32
BF16 = jnp.bfloat16


VMEM = pl.BlockSpec(memory_space=pltpu.VMEM)
SMEM = pl.BlockSpec(memory_space=pltpu.SMEM)
HBM = pl.BlockSpec(memory_space=pltpu.HBM)


def params(mib=48):
    return pltpu.CompilerParams(vmem_limit_bytes=mib << 20)


def cost(flops, nbytes):
    return pl.CostEstimate(flops=flops, bytes_accessed=nbytes, transcendentals=0)


def chain_of(iota):
    return (iota // BLK) % 2


def nn(a, b, **kw):
    return lax.dot_general(a, b, (((1,), (0,)), ((), ())), preferred_element_type=F32, **kw)


def nt(a, b, **kw):
    return lax.dot_general(a, b, (((1,), (1,)), ((), ())), preferred_element_type=F32, **kw)


def by_chain(x):
    rows = x.shape[0]
    chain = chain_of(lax.broadcasted_iota(jnp.int32, (rows, DK), 0))
    zero = jnp.zeros_like(x)
    return jnp.concatenate([jnp.where(chain == 0, x, zero), jnp.where(chain == 1, x, zero)], axis=1)


def split3(x):
    hi = x.astype(BF16)
    rest = x - hi.astype(F32)
    mid = rest.astype(BF16)
    return hi, mid, (rest - mid.astype(F32)).astype(BF16)


def read_message(x):
    state = x[:ROWS].astype(F32)
    tail = x[ROWS:].astype(F32)
    total = tail[0:PAIRS] + tail[PAIRS : 2 * PAIRS] + tail[2 * PAIRS : 3 * PAIRS]
    return state, total


def spread(total):
    return jnp.concatenate(
        [jnp.broadcast_to(total[p : p + 1], (DK, total.shape[1])) for p in range(PAIRS)], axis=0
    )


def write_message(ref, state, total):
    ref[:ROWS, :] = state.astype(BF16)
    hi, mid, lo = split3(total)
    pad = jnp.zeros((TAIL - 3 * PAIRS, total.shape[1]), F32)
    ref[ROWS:, :] = jnp.concatenate(
        [hi.astype(F32), mid.astype(F32), lo.astype(F32), pad], axis=0
    ).astype(BF16)


def decay_terms(ld):
    return jnp.concatenate([t.astype(F32) for t in split3(ld)], axis=0).astype(BF16)


def column_sums(mask, ld):
    x = nt(mask.astype(BF16), decay_terms(ld))
    return x[:, :H] + x[:, H : 2 * H] + x[:, 2 * H : 3 * H]


def row_sums(mask, ld):
    x = nt(decay_terms(ld), mask.astype(BF16))
    return x[:H] + x[H : 2 * H] + x[2 * H : 3 * H]


def position():
    lane = lax.rem(lax.axis_index("tm"), LANES)
    return lane // 2, lane & 1


def local_kernel(x_in, ld_in, wk_in, wv_in, idx_in, cnt_in, k_ref, v_ref, keep, give, pack, *rest):
    chunks, x_ref, ld_ref, bk, bv, idx, cnt, sems = rest
    rows = x_ref.shape[0]
    copies = [
        pltpu.make_async_copy(src, dst, sems.at[i])
        for i, (src, dst) in enumerate(
            (
                (ld_in, ld_ref),
                (x_in, x_ref),
                (wk_in, bk),
                (wv_in, bv),
                (idx_in, idx),
                (cnt_in, cnt),
            )
        )
    ]
    for copy in copies:
        copy.start()
    t = lax.broadcasted_iota(jnp.int32, (rows, rows), 0)
    s = lax.broadcasted_iota(jnp.int32, (rows, rows), 1)
    after = ((s > t) & (chain_of(s) == chain_of(t))).astype(F32)
    copies[0].wait()
    ld = ld_ref[...]
    tail = jnp.exp(row_sums(after, ld))
    chain = chain_of(lax.broadcasted_iota(jnp.int32, ld.shape, 1))
    sums = [jnp.sum(jnp.where(chain == b, ld, 0.0), axis=1, keepdims=True) for b in (0, 1)]
    tails = [jnp.where(chain == b, tail, 0.0) for b in (0, 1)]
    copies[1].wait()
    copies[2].wait()
    x = x_ref[...]
    k = nn(x, bk[...]).astype(BF16)
    k_ref[...] = k
    turned = [
        jnp.transpose(k[:, q * HC * DK : (q + 1) * HC * DK].astype(F32)) for q in range(LANES)
    ]
    for copy in copies[3:]:
        copy.wait()
    v = nn(x, bv[...]).astype(BF16)
    v_ref[...] = v
    for q in range(LANES):
        states, totals = [], []
        for i in range(HC):
            h = q * HC + i
            kt = turned[q][i * DK : (i + 1) * DK]
            both = jnp.concatenate([(kt * tails[b][h : h + 1]).astype(BF16) for b in (0, 1)], axis=0)
            states.append(nn(both, v[:, h * DV : (h + 1) * DV]))
            totals += [jnp.broadcast_to(sums[b][h : h + 1], (1, DV)) for b in (0, 1)]
        write_message(
            chunks.at[q], jnp.concatenate(states, axis=0), jnp.concatenate(totals, axis=0)
        )
    _, core = position()
    for y in range(2):
        keep[y] = chunks[2 * y + core]
        give[y] = chunks[2 * y + 1 - core]
    frames, slots = idx.shape
    for f in range(frames):
        for i in range(slots):
            pack[f, i] = idx[f, i]
        pack[f, slots] = cnt[f]


def local(tokens, w_rk, w_rv, ld, index, live):
    rows, d = tokens.shape
    message = jax.ShapeDtypeStruct((2, ROWS + TAIL, DV), BF16)
    frames, slots = index.shape
    return pl.pallas_call(
        local_kernel,
        in_specs=[HBM] * 6,
        out_specs=[VMEM] * 4 + [SMEM],
        out_shape=[
            jax.ShapeDtypeStruct((rows, H * DK), BF16),
            jax.ShapeDtypeStruct((rows, H * DV), BF16),
            message,
            message,
            jax.ShapeDtypeStruct((frames, slots + 1), jnp.int32),
        ],
        scratch_shapes=[
            pltpu.VMEM((LANES, ROWS + TAIL, DV), BF16),
            pltpu.VMEM((rows, d), BF16),
            pltpu.VMEM((H, rows), F32),
            pltpu.VMEM((d, H * DK), BF16),
            pltpu.VMEM((d, H * DV), BF16),
            pltpu.SMEM((frames, slots), jnp.int32),
            pltpu.SMEM((frames,), jnp.int32),
            pltpu.SemaphoreType.DMA((6,)),
        ],
        compiler_params=params(50),
        name="local",
    )(tokens, ld, w_rk, w_rv, index, live)


def clear(flags):
    for row in range(flags.shape[0]):
        for block in range(flags.shape[1]):
            flags[row, block] = jnp.int32(0)


def each_live(frames, f, index, act):
    me = lax.axis_index("tm")
    slots = index.shape[1] - 1

    def visit(i, carry):
        frame = index[f, i]
        owner = frame // frames
        act(me // LANES - owner // LANES, lax.rem(owner, LANES), lax.rem(frame, frames))
        return carry

    lax.fori_loop(0, jnp.minimum(index[f, slots], slots), visit, 0)


def list_live(frames, distances, tables, groups):
    lane = lax.rem(lax.axis_index("tm"), LANES)
    for flags in tables:
        clear(flags)
    for g, index in enumerate(groups):
        for f in range(frames):
            row = g * frames + f
            if g == 0:
                tables[0][row, f] = jnp.int32(1)

            def act(distance, its, place, row=row):
                here = (its // 2) == (lane // 2)
                for flags, (low, high) in zip(tables, distances):

                    @pl.when(here & (distance >= low) & (distance < high))
                    def _(flags=flags, low=low):
                        block = ((distance - low) * 2 + ((its ^ lane) & 1)) * frames + place
                        flags[row, block] = jnp.int32(1)

            each_live(frames, f, index, act)


def inner_kernel(frames, distances, *refs):
    x_in, ld_ref, k_in, v_in, pack, other, wq_in = refs[:7]
    inner_ref, qq_ref = refs[7:9]
    tables, (x_ref, k_ref, v_ref, bq, sems) = refs[9:-5], refs[-5:]
    copies = [
        pltpu.make_async_copy(src, dst, sems.at[i])
        for i, (src, dst) in enumerate(
            ((x_in, x_ref), (wq_in, bq), (k_in, k_ref), (v_in, v_ref))
        )
    ]
    for copy in copies:
        copy.start()
    list_live(frames, distances, tables, (pack, other))
    rows = x_in.shape[0]
    ld = ld_ref[...]
    t = lax.broadcasted_iota(jnp.int32, (rows, rows), 0)
    s = lax.broadcasted_iota(jnp.int32, (rows, rows), 1)
    upto = (s <= t) & (chain_of(s) == chain_of(t))
    ones = upto.astype(F32)
    column = column_sums(ones, ld)
    row = row_sums(ones, ld)
    grown = jnp.exp(column) * DK**-0.5
    for copy in copies:
        copy.wait()
    q = nn(x_ref[...], bq[...]).astype(BF16)
    for h in range(H):
        qh = q[:, h * DK : (h + 1) * DK]
        gap = column[:, h : h + 1] - row[h : h + 1, :]
        weight = jnp.exp(jnp.where(upto, gap, NEG)) * DK**-0.5
        scores = nt(qh, k_ref[:, h * DK : (h + 1) * DK]) * weight
        inner_ref[:, h * DV : (h + 1) * DV] = nn(
            scores.astype(BF16), v_ref[:, h * DV : (h + 1) * DV]
        )
        scaled = qh.astype(F32) * grown[:, h : h + 1]
        qq_ref[:, h * 2 * DK : (h + 1) * 2 * DK] = by_chain(scaled.astype(BF16))


def inner(tokens, w_rq, k, v, ld, pack, other, distances):
    rows, d = tokens.shape
    frames = rows // P_SIZE
    table_shapes = [
        jax.ShapeDtypeStruct((2 * frames, (high - low) * 2 * frames), jnp.int32)
        for low, high in distances
    ]
    out = pl.pallas_call(
        functools.partial(inner_kernel, frames, distances),
        in_specs=[HBM, VMEM, HBM, HBM, SMEM, SMEM, HBM],
        out_specs=[VMEM] * 2 + [SMEM] * len(table_shapes),
        out_shape=[
            jax.ShapeDtypeStruct((rows, H * DV), F32),
            jax.ShapeDtypeStruct((rows, H * 2 * DK), BF16),
        ]
        + table_shapes,
        scratch_shapes=[
            pltpu.VMEM((rows, d), BF16),
            pltpu.VMEM((rows, H * DK), BF16),
            pltpu.VMEM((rows, H * DV), BF16),
            pltpu.VMEM((d, H * DK), BF16),
            pltpu.SemaphoreType.DMA((4,)),
        ],
        compiler_params=params(48),
        cost_estimate=cost(2 * rows * d * H * DK, 8 << 20),
        name="inner",
    )(tokens, ld, k, v, pack, other, w_rq)
    return out[0], out[1], out[2:]


def join(first, second):
    return spread(jnp.exp(second[1])) * first[0] + second[0], first[1] + second[1]


def chip_kernel(keep, got, stay, send, ordered, results):
    y, core = position()
    ordered[core] = keep[...]
    ordered[1 - core] = got[...]
    for q in range(2):
        write_message(
            results.at[q], *join(read_message(ordered[0, q]), read_message(ordered[1, q]))
        )
    stay[...] = results[y]
    send[...] = results[1 - y]


def plane_kernel(stay, got, out, ordered):
    y, _ = position()
    ordered[y] = stay[...]
    ordered[1 - y] = got[...]
    write_message(out, *join(read_message(ordered[0]), read_message(ordered[1])))


def prefix_kernel(count, *refs):
    (stay, got), earlier = refs[:2], refs[2 : 2 + count]
    mine, send, ordered, results = refs[2 + count :]
    y, _ = position()
    plane = lax.axis_index("tm") // LANES
    ordered[y] = stay[...]
    ordered[1 - y] = got[...]
    state = jnp.zeros((ROWS, DV), F32)
    for distance in range(count, 0, -1):
        step, _ = join((state, 0.0), read_message(earlier[distance - 1][...]))
        state = jnp.where(plane >= distance, step, 0.0)
    results[0] = state.astype(BF16)
    results[1] = join((state, 0.0), read_message(ordered[0]))[0].astype(BF16)
    mine[...] = results[y]
    send[...] = results[1 - y]


def split_kernel(keep, local_got, mine, got, kept, give, ordered, both, results):
    y, core = position()
    ordered[core] = keep[...]
    ordered[1 - core] = local_got[...]
    both[y] = mine[...]
    both[1 - y] = got[...]
    for q in range(2):
        state = both[q]
        results[0, q] = state
        results[1, q] = join((state.astype(F32), 0.0), read_message(ordered[0, q]))[0].astype(BF16)
    kept[...] = results[core]
    give[...] = results[1 - core]


def small(kernel, outs, scratch, *args):
    return pl.pallas_call(
        kernel,
        in_specs=[VMEM] * len(args),
        out_specs=[VMEM] * len(outs),
        out_shape=[jax.ShapeDtypeStruct(shape, BF16) for shape in outs],
        scratch_shapes=[pltpu.VMEM(shape, BF16) for shape in scratch],
        compiler_params=params(8),
    )(*args)


def hidden_kernel(frame, inner_ref, qq_ref, kept, got, x_ref, gain_ref, wk, wv, hid_ref, kv_ref, ordered):
    span = slice(frame * P_SIZE, (frame + 1) * P_SIZE)
    _, core = position()
    for y in range(2):
        ordered[2 * y + core] = kept[y]
        ordered[2 * y + 1 - core] = got[y]
    for h in range(H):
        cols = slice(h * DV, (h + 1) * DV)
        state = ordered[h // HC, (h % HC) * 2 * DK : (h % HC + 1) * 2 * DK, :]
        o = inner_ref[span, cols] + nn(qq_ref[span, h * 2 * DK : (h + 1) * 2 * DK], state)
        scale = lax.rsqrt(jnp.mean(o * o, axis=1, keepdims=True) + 1e-05)
        y = o * scale * gain_ref[:, cols]
        hid_ref[:, cols] = (x_ref[span, cols].astype(F32) + y).astype(BF16)
    hid = hid_ref[...]
    for i, w in enumerate((wk, wv)):
        kv_ref[:, i * MC : (i + 1) * MC] = nn(hid, w[...]).astype(BF16)


def hidden_of(frame, inner_out, qq, states, tokens, gain, w_mk, w_mv):
    d = tokens.shape[1]
    return pl.pallas_call(
        functools.partial(hidden_kernel, frame),
        in_specs=[VMEM] * 8,
        out_specs=[VMEM] * 2,
        out_shape=[
            jax.ShapeDtypeStruct((P_SIZE, d), BF16),
            jax.ShapeDtypeStruct((P_SIZE, 2 * MC), BF16),
        ],
        scratch_shapes=[pltpu.VMEM((LANES, ROWS, DV), BF16)],
        compiler_params=params(),
        name="hidden",
    )(inner_out, qq, *states, tokens, gain.reshape(1, d), w_mk, w_mv)


def query_kernel(*refs):
    hids, (w_ref, q_ref) = refs[:-2], refs[-2:]
    hid = jnp.concatenate([ref[...] for ref in hids], axis=0)
    q_ref[...] = nn(hid, w_ref[...]).astype(BF16)


def queries_of(hids, w_mq):
    return pl.pallas_call(
        query_kernel,
        in_specs=[VMEM] * (len(hids) + 1),
        out_specs=VMEM,
        out_shape=jax.ShapeDtypeStruct((len(hids) * P_SIZE, MC), BF16),
        compiler_params=params(),
        name="queries",
    )(*hids, w_mq)


def list_assist(frames, at, half, steps, planes, index, flags):
    me = lax.axis_index("tm")
    clear(flags)
    for f in range(frames):

        def act(distance, its, place, f=f):
            apart = its ^ lax.rem(me, LANES)

            @pl.when((distance == at) & (apart // 2 == half) & (me // LANES + steps < planes))
            def _():
                flags[f, (apart & 1) * frames + place] = jnp.int32(1)

        each_live(frames, f, index, act)


def attend_kernel(frames, blocks, row, first, last, low, assist, *refs):
    if assist is None:
        live, refs = refs[0], refs[1:]
    else:
        index, live, refs = refs[0], refs[-1], refs[1:-1]
    q_ref, refs = refs[0], refs[1:]
    if not first:
        acc_in, top_in, sum_in = refs[:3]
        refs = refs[3:]
    kv, refs = refs[:blocks], refs[blocks:]
    outs, (scores, stat) = refs[:-2], refs[-2:]
    rows = frames * P_SIZE
    scale = MD**-0.5
    base2 = scale * 1.4426950408889634
    pairs = [range(i, min(i + 2, blocks)) for i in range(0, blocks, 2)]
    spans = [slice(f * P_SIZE, (f + 1) * P_SIZE) for f in range(frames)]

    def finish(e, top, total, acc, kept):
        whole = jnp.broadcast_to(jnp.sum(total, axis=1, keepdims=True), (rows, 128))
        whole = jnp.maximum(whole, 1e-30)
        outs[0][:, e * MD : (e + 1) * MD] = (acc / whole).astype(outs[0].dtype)
        kept.append((top, whole))

    def close(kept):
        lane = lax.broadcasted_iota(jnp.int32, (rows, 128), 1)
        merged = jnp.zeros((rows, 128), F32)
        for e, (top, whole) in enumerate(kept):
            merged = jnp.where(lane == e, top, jnp.where(lane == MH + e, whole, merged))
        stat[...] = merged
        flat = jnp.transpose(stat[...])
        logs = jnp.log(flat[MH : 2 * MH])
        outs[1][...] = jnp.concatenate([flat[:MH] * scale + logs, logs], axis=0)

    def skip():
        kept = []
        for e in range(MH):
            held = slice(e * rows, (e + 1) * rows)
            acc = acc_in[:, e * MD : (e + 1) * MD]
            if last:
                finish(e, top_in[held, :], sum_in[held, :], acc, kept)
            else:
                outs[0][:, e * MD : (e + 1) * MD] = acc
                outs[1][held, :] = top_in[held, :]
                outs[2][held, :] = sum_in[held, :]
        if last:
            close(kept)

    def run():
        if assist is not None:
            list_assist(frames, *assist, index, live)
        kept = []
        for e in range(MH):
            cols, vcols = slice(e * MD, (e + 1) * MD), slice(MC + e * MD, MC + (e + 1) * MD)
            held = slice(e * rows, (e + 1) * rows)
            q = q_ref[:, cols]
            tops = [None] * frames
            for pair in pairs:
                s = nt(q, jnp.concatenate([kv[b][:, cols] for b in pair], axis=0))
                for j, b in enumerate(pair):
                    for f in range(frames):
                        part = s[spans[f], j * P_SIZE : (j + 1) * P_SIZE]
                        part = jnp.where(live[row + f, b] == 1, part, NEG)
                        scores[e, spans[f], b * P_SIZE : (b + 1) * P_SIZE] = part
                        tops[f] = part if tops[f] is None else jnp.maximum(tops[f], part)
            top = jnp.concatenate([jnp.max(t, axis=1, keepdims=True) for t in tops], axis=0)
            top = jnp.broadcast_to(jnp.maximum(top, 0.1 * NEG), (rows, 128))
            if not first:
                before = top_in[held, :]
                top = jnp.maximum(top, before)
                fade = jnp.exp2((before - top) * base2)
            total, acc = None, None
            for pair in pairs:
                ps = []
                for b in pair:
                    p = jnp.exp2((scores[e, :, b * P_SIZE : (b + 1) * P_SIZE] - top) * base2)
                    total = p if total is None else total + p
                    ps.append(p.astype(BF16))
                part = nn(
                    jnp.concatenate(ps, axis=1),
                    jnp.concatenate([kv[b][:, vcols] for b in pair], axis=0),
                )
                acc = part if acc is None else acc + part
            if not first:
                total = total + fade * sum_in[held, :]
                acc = acc + fade * acc_in[:, cols]
            if last:
                finish(e, top, total, acc, kept)
            else:
                outs[0][:, cols] = acc
                outs[1][held, :] = top
                outs[2][held, :] = total
        if last:
            close(kept)

    if assist is None and not first:
        reaches_down = lax.axis_index("tm") // LANES >= low
        pl.when(reaches_down)(run)
        pl.when(jnp.logical_not(reaches_down))(skip)
    elif assist is None:
        run()
    else:
        steps, planes = assist[2:]
        plane = lax.axis_index("tm") // LANES
        pl.when((plane >= 1) & (plane + steps < planes))(run)


def attend(lists, row, asked, kvs, state, last, dtype, low=0, assist=None):
    rows = asked.shape[0]
    frames = rows // P_SIZE
    blocks = len(kvs)
    first = state is None
    state = [] if first else list(state)
    if last:
        out_shape = [
            jax.ShapeDtypeStruct((rows, MC), dtype),
            jax.ShapeDtypeStruct((2 * MH, rows), F32),
        ]
    else:
        out_shape = [jax.ShapeDtypeStruct((rows, MC), F32)]
        out_shape += [jax.ShapeDtypeStruct((MH * rows, 128), F32)] * 2
    scratch = [pltpu.VMEM((MH, rows, blocks * P_SIZE), F32), pltpu.VMEM((rows, 128), F32)]
    if assist is not None:
        scratch.append(pltpu.SMEM((frames, blocks), jnp.int32))
    return pl.pallas_call(
        functools.partial(attend_kernel, frames, blocks, row, first, last, low, assist),
        in_specs=[SMEM] + [VMEM] * (1 + len(state) + blocks),
        out_specs=[VMEM] * len(out_shape),
        out_shape=out_shape,
        scratch_shapes=scratch,
        compiler_params=params(),
        cost_estimate=cost(4 * blocks * rows * P_SIZE * MC, blocks * P_SIZE * MC * 4),
        name="assist" if assist is not None else "attend_last" if last else "attend",
    )(lists, asked, *state, *kvs)


def output_kernel(parts, steps, *refs):
    values, stats = refs[0 : 2 * parts : 2], refs[1 : 2 * parts : 2]
    hids, (w_ref, out_ref, mixed) = refs[2 * parts : -3], refs[-3:]
    rows = out_ref.shape[0]
    logs = [ref[...] for ref in stats]
    if parts > 2:
        logs[2] = jnp.where(lax.axis_index("tm") // LANES > steps, logs[2], NEG)
    top = functools.reduce(jnp.maximum, logs)
    shares = [jnp.exp(x - top) for x in logs]
    inv = 1.0 / functools.reduce(jnp.add, shares)
    pad = jnp.zeros((128 - parts * 2 * MH, rows), F32)
    weights = jnp.transpose(jnp.concatenate([x * inv for x in shares] + [pad], axis=0))
    for e in range(MH):
        cols = slice(e * MD, (e + 1) * MD)
        value = 0.0
        for i, ref in enumerate(values):
            at = i * 2 * MH + e
            value = value + ref[:, cols].astype(F32) * weights[:, at : at + 1]
        mixed[:, cols] = value.astype(BF16)
    hid = jnp.concatenate([ref[...] for ref in hids], axis=0)
    out_ref[...] = (hid.astype(F32) + nn(mixed[...], w_ref[...])).astype(BF16)


def output(parts, hids, w_out, steps):
    rows, d = len(hids) * P_SIZE, hids[0].shape[1]
    flat = [x for part in parts for x in part]
    return pl.pallas_call(
        functools.partial(output_kernel, len(parts), steps),
        in_specs=[VMEM] * (len(flat) + len(hids) + 1),
        out_specs=VMEM,
        out_shape=jax.ShapeDtypeStruct((rows, d), BF16),
        scratch_shapes=[pltpu.VMEM((rows, MC), BF16)],
        compiler_params=params(),
        name="output",
    )(*flat, *hids, w_out)


def on_device(
    tokens, log_decay, mem_index, mem_count, w_rq, w_rk, w_rv, norm_gain, w_mq, w_mk, w_mv, w_out
):
    size = lax.axis_size("tm")
    planes = size // LANES
    frames = tokens.shape[0] // P_SIZE

    def flip(x, bits):
        return lax.ppermute(x, "tm", [(i, i ^ bits) for i in range(size)])

    def up(x, distance):
        step = distance * LANES
        return lax.ppermute(x, "tm", [(i, (i + step) % size) for i in range(size)])

    message, chunk = (ROWS + TAIL, DV), (ROWS, DV)
    steps, reach = reaches(planes)
    spans = spans_of(steps)
    k, v, keep, give, pack = local(tokens, w_rk, w_rv, log_decay, mem_index, mem_count)
    core_got = flip(give, 1)
    other = flip(pack, 2)
    stay, send = small(
        chip_kernel, [message] * 2, [(2, 2) + message, (2,) + message], keep, core_got
    )
    column_got = flip(send, 2)
    (total,) = small(plane_kernel, [message], [(2,) + message], stay, column_got)
    earlier = [up(total, d) for d in range(1, planes)]
    inner_out, qq, tables = inner(tokens, w_rq, k, v, log_decay, pack, other, spans)
    mine, send = small(
        functools.partial(prefix_kernel, len(earlier)),
        [chunk] * 2,
        [(2,) + message, (2,) + chunk],
        stay,
        column_got,
        *earlier,
    )
    column_back = flip(send, 2)
    kept, give = small(
        split_kernel,
        [(2,) + chunk] * 2,
        [(2, 2) + message, (2,) + chunk, (2, 2) + chunk],
        keep,
        core_got,
        mine,
        column_back,
    )
    states = (kept, flip(give, 1))
    hids, kv = [], []
    for f in range(tokens.shape[0] // P_SIZE):
        x, keys = hidden_of(f, inner_out, qq, states, tokens, norm_gain, w_mk, w_mv)
        hids.append(x)
        kv.append(keys)
    q = queries_of(hids, w_mq)

    def between(x, pairs):
        return lax.ppermute(
            x, "tm", [(a * LANES + i, b * LANES + i) for a, b in pairs for i in range(LANES)]
        )

    def onward(x, distance):
        pairs = [(p, p + 1) for p in range(distance - 1, planes - 1)]
        return between(x, pairs + [(planes - 1, 0)] * (distance == 1))

    frames = len(kv)
    partner_q = flip(q, 2)
    held, across = [], []
    for distance in range(steps + 1):
        if distance:
            kv = [onward(x, distance) for x in kv]
        near = [flip(x, 1) for x in kv]
        held.append(kv + near)
        if 1 <= distance <= reach:
            column = [flip(x, 2) for x in kv]
            both = [flip(x, 1) for x in column]
            across += [(distance, 0, kv + near), (distance, 1, column + both)]
    parts = []
    if reach:
        helped = [(p, p + steps) for p in range(1, planes - steps)]
        down = [(b, a) for a, b in helped]
        far_q = between(q, down)
        far_pack = between(pack, down)
        far = None
        for at, half, blocks in across:
            last = at == reach and half == 1
            far = attend(far_pack, 0, far_q, blocks, far, last, BF16, 0, (at, half, steps, planes))
        parts = [[between(x, helped) for x in far]]

    def attended(row, asked, dtype):
        state = None
        for (low, high), flags in zip(spans, tables):
            blocks = [x for group in held[low:high] for x in group]
            state = attend(flags, row, asked, blocks, state, high == steps + 1, dtype, low)
        return state

    theirs = attended(frames, partner_q, BF16)
    back = [flip(x, 2) for x in theirs]
    mine = attended(0, q, F32)
    return output([mine, back] + parts, hids, w_out, steps)


def spans_of(steps):
    return [(low, min(low + 2, steps)) for low in range(0, steps, 2)] + [(steps, steps + 1)]


def reaches(planes):
    steps = planes // 2
    return steps, planes - 1 - steps


def solution(mesh):
    placed = (
        P(("groups", "tm"), None),
        P(None, ("groups", "tm")),
        P(("groups", "tm"), None),
        P(("groups", "tm")),
        P(),
        P(),
        P(),
        P(),
        P(),
        P(),
        P(),
        P(),
    )

    return jax.shard_map(
        on_device, mesh=mesh, in_specs=placed, out_specs=P(("groups", "tm"), None), check_vma=False
    )
```
